32 devices in a mesh: tile: 4 (over y, x), phi: 8 (over z, core).
Axes of the slice: x: 2, y: 2, z: 4, core: 2. Of those that a mesh axis runs over, the one named last changes fastest.
Arguments:
- conserved: float32 [256, 5, 4096], P(('tile', 'phi')), may hold values from -6 to 6
- face_field: float32 [256, 3, 4096], P(('tile', 'phi')), may hold values from -1.5 to 1.5
- block_ids: int32 [256], P(('tile', 'phi')), may hold values from 0 to 63, as said below
- int_shift: int32 [64], P('tile'), may hold values from 0 to 511
- frac_shift: float32 [64], P('tile'), may hold values from 0 to 1, as said below
Outputs:
- conserved_out: float32 [256, 5, 4096], P(('tile', 'phi'))
- field_out: float32 [256, 3, 4096], P(('tile', 'phi'))
The draws below stay inside these ranges and needn't reach their ends.
Inputs may be any that keep to these rules, and one draw needn't show every extreme that they name: `block_ids`: within each slab (aligned runs of 64 entries, one slab per index of tile) every number from 0 to 63 appears once. Number v belongs to the owner v // 8. The slots of one device hold at most 2 blocks of any one owner, and in every slab some device holds exactly 2 blocks of some owner. `frac_shift`: multiples of 1/256, below 1.
All inputs are finite; a program needn't handle non-finite values.
Results may differ from the reference program's by a relative error of at most 0.0003.
Values sent between devices are 32-bit elements; how exact they have to be, the bound alone decides.
No kernel may reach another device: no remote copies, remote signals or barrier semaphores. Data moves between devices by JAX's collectives and lax.ppermute only.
A program may use at most 64 MiB of HBM per device.

```python
import jax
import jax.numpy as jnp
import numpy as np
from jax import lax

BS = 16
TB = 2
PB = 4
BDEV = 8
CAP = 2
NTH = 32
NPH = 512
RAD = 64
SLOTS = 256
N_TILE = 4
N_PHI = 8


def draw_block_ids(key, part):
    large_groups = BDEV // (2 * CAP)
    small_groups = BDEV // CAP
    group_sizes = [CAP] * large_groups + [CAP // 2] * small_groups
    group_count = len(group_sizes)
    group_table = jnp.asarray(np.repeat(np.arange(group_count), group_sizes).astype(np.int32))

    def one_permutation(perm_key):
        return jax.random.permutation(perm_key, BDEV)

    def one_tile(tile_key):
        offset_key, slot_key, block_key = jax.random.split(tile_key, 3)
        offsets = jax.random.permutation(offset_key, N_PHI)[:group_count]
        positions = jax.vmap(one_permutation)(jax.random.split(slot_key, N_PHI))
        orders = jax.vmap(one_permutation)(jax.random.split(block_key, N_PHI))
        groups = group_table[positions]
        sources = jnp.arange(N_PHI)[:, None]
        targets = (sources + offsets[groups]) % N_PHI
        return targets * BDEV + orders[targets, positions]
    tile_keys = jax.random.split(jax.random.fold_in(key, 11), N_TILE)
    return jax.vmap(one_tile)(tile_keys).reshape(-1).astype(jnp.int32)


def draw_frac_shift(key, part):
    numerators = jax.random.randint(jax.random.fold_in(key, 23), (RAD,), 0, 256)
    return numerators.astype(jnp.float32) / 256.0


def place_ends(entries, key, smallest, high):
    place = [jax.random.randint(jax.random.fold_in(key, axis), (), 0, length) for axis, length in enumerate(entries.shape)]
    widest = entries.shape.index(max(entries.shape))
    next_to = place[:widest] + [(place[widest] + 1) % entries.shape[widest]] + place[widest + 1:]
    return entries.at[tuple(place)].set(smallest).at[tuple(next_to)].set(high)


def level_of(key, extent, shards, smallest, high):
    def one(axis_at, blocks):
        draws = jax.random.uniform(jax.random.fold_in(jax.random.fold_in(key, 6), axis_at), (blocks,), jnp.float32, smallest / len(shards), high / len(shards))
        return jnp.repeat(jnp.exp(draws), extent[axis_at] // blocks).reshape((-1,) + (1,) * (len(extent) - axis_at - 1))

    factor_of = one(*shards[0])
    for cut in shards[1:]:
        factor_of = factor_of * one(*cut)
    return factor_of


def gaussian(stream_key, extent, scale, most, cuts=(), held_as=jnp.bfloat16):
    gain = level_of(stream_key, extent, cuts, -0.22, 0.18) if cuts else 1.0
    entries = jax.random.normal(stream_key, extent, jnp.float32) * scale * gain
    return jnp.minimum(jnp.maximum(entries, -most), most).astype(held_as)


def setup_inputs(seed: int = 0) -> dict:
    seeds = jax.random.split(jax.random.key(seed), 6)
    conserved = gaussian(seeds[0], (SLOTS, 5, BS * BS * BS), 1.0, 6.0, ((0, 32),), jnp.float32)
    face_field = gaussian(seeds[1], (SLOTS, 3, BS * BS * BS), 0.25, 1.5, ((0, 32),), jnp.float32)
    block_ids = draw_block_ids(jax.random.fold_in(seeds[5], 71), 0)
    int_shift = place_ends(jax.random.randint(seeds[3], (RAD,), 0, NPH), jax.random.fold_in(seeds[3], 1), 0, NPH - 1).astype(jnp.int32)
    frac_shift = draw_frac_shift(jax.random.fold_in(seeds[5], 71), 0)
    return {"conserved": conserved, "face_field": face_field, "block_ids": block_ids, "int_shift": int_shift, "frac_shift": frac_shift}


NODES = (-3, -2, -1, 0, 1, 2, 3)


def flux_weights(fraction):
    position = -fraction
    lagrange = []
    for a in NODES:
        product = jnp.ones_like(fraction)
        for b in NODES:
            if b != a:
                product = product * (position - float(b)) / float(a - b)
        lagrange.append(product)
    weights = []
    for m in range(-3, 3):
        weight_sum = jnp.zeros_like(fraction)
        if m >= 0:
            for a in range(m + 1, 4):
                weight_sum = weight_sum - lagrange[a + 3]
        else:
            for a in range(-3, m + 1):
                weight_sum = weight_sum + lagrange[a + 3]
        weights.append(weight_sum)
    return weights


def remap_rows(fields, whole_shift, part_shift):
    length = fields.shape[2]
    cells_phi = jnp.arange(length, dtype=jnp.int32)
    source = (cells_phi[None, :] - whole_shift[:, None]) % length
    source_all = jnp.broadcast_to(source[None], fields.shape)
    shifted = jnp.take_along_axis(fields, source_all, axis=2)
    weights = flux_weights(part_shift)
    face_flux = jnp.zeros_like(shifted)
    for term_index in range(6):
        face_flux = face_flux + weights[term_index][None, :, None] * jnp.roll(shifted, 3 - term_index, axis=2)
    updated = shifted - (jnp.roll(face_flux, -1, axis=2) - face_flux)
    magnetic = fields[5:7]
    prefix = jnp.cumsum(magnetic, axis=2) - magnetic
    row_total = jnp.sum(magnetic, axis=2, keepdims=True)
    behind = jnp.take_along_axis(prefix, source_all[5:7], axis=2)
    wrapped = (cells_phi[None, :] < whole_shift[:, None]).astype(jnp.float32)
    whole_flux = prefix - behind + wrapped[None] * row_total
    return updated, whole_flux + face_flux[5:7]


def reference(conserved, face_field, block_ids, int_shift, frac_shift):
    stacked = jnp.concatenate([conserved, face_field], axis=1).reshape(N_TILE, N_PHI * BDEV, 8, BS * BS * BS)
    numbers = block_ids.reshape(N_TILE, N_PHI * BDEV)
    shifts = int_shift.reshape(N_TILE, BS)
    fractions = frac_shift.reshape(N_TILE, BS)

    def one_tile(inputs):
        blocks, slot_ids, tile_shift, tile_frac = inputs
        canonical = jnp.zeros_like(blocks).at[slot_ids].set(blocks)
        row_grid = canonical.reshape(N_PHI, TB, PB, 8, BS, BS, BS).transpose(3, 4, 1, 5, 0, 2, 6).reshape(8, BS * NTH, NPH)
        updated, fluxes = remap_rows(row_grid[:7], jnp.repeat(tile_shift, NTH), jnp.repeat(tile_frac, NTH))
        return updated, fluxes, row_grid[7]

    updated, fluxes, azimuthal = lax.map(one_tile, (stacked, numbers, shifts, fractions))
    radial_flux = fluxes[:, 0].reshape(RAD, NTH, NPH)
    polar_flux = fluxes[:, 1].reshape(RAD, NTH, NPH)
    radial_next = jnp.concatenate([radial_flux[1:], jnp.zeros_like(radial_flux[:1])], axis=0)
    polar_next = jnp.concatenate([polar_flux[:, 1:], jnp.zeros_like(polar_flux[:, :1])], axis=1)
    new_azimuthal = azimuthal.reshape(RAD, NTH, NPH) + (radial_next - radial_flux) + (polar_next - polar_flux)
    full_grid = jnp.concatenate([updated.reshape(N_TILE, 7, BS, NTH, NPH), new_azimuthal.reshape(N_TILE, 1, BS, NTH, NPH)], axis=1)
    blocks_out = full_grid.reshape(N_TILE, 8, BS, TB, BS, N_PHI, PB, BS).transpose(0, 5, 3, 6, 1, 2, 4, 7).reshape(N_TILE * N_PHI * BDEV, 8, BS * BS * BS)
    return blocks_out[:, :5], blocks_out[:, 5:]
```

```python
import functools

import jax
import jax.numpy as jnp
from jax import lax
from jax.experimental import pallas as pl
from jax.experimental.pallas import tpu as pltpu
from jax.sharding import PartitionSpec as P

BS = 16
TB = 2
PB = 4
LANES = 128
SUB = 8
NODES = (-3, -2, -1, 0, 1, 2, 3)
F32 = jnp.float32
BF16 = jnp.bfloat16


def halves(x):
    hi = x.astype(BF16)
    return hi, (x - hi.astype(F32)).astype(BF16)


def thirds(x):
    hi = x.astype(BF16)
    rest = x - hi.astype(F32)
    mid = rest.astype(BF16)
    return hi, mid, (rest - mid.astype(F32)).astype(BF16)


def dot(a, b):
    return jnp.dot(a, b, preferred_element_type=F32)


def nearest_blocks(shift):
    whole = (shift + BS // 2) // BS
    return whole, shift - whole * BS


def pack_fields_kernel(cfg, me_ref, ids_ref, face_ref, *refs):
    outs, tile_ref, sem, id_sem = refs[: cfg.n], refs[cfg.n], refs[cfg.n + 1], refs[cfg.n + 2]
    me = me_ref[0]
    rows = lax.broadcasted_iota(jnp.int32, (SUB, LANES), 0)
    ids = jnp.zeros((SUB, LANES), jnp.int32)
    for slot in range(SUB):
        ids = jnp.where(rows == slot, ids_ref[slot], ids)
    tile_ref[...] = ids.astype(F32)[None]
    copies = []
    for k in range(cfg.n):
        dest = jnp.bitwise_xor(me, k)
        for c in range(3):
            copies.append(
                pltpu.make_async_copy(
                    face_ref.at[c, pl.ds(dest * cfg.tiles, cfg.tiles)],
                    outs[k].at[pl.ds(c * cfg.tiles, cfg.tiles)],
                    sem.at[k * 3 + c],
                )
            )
        copies.append(
            pltpu.make_async_copy(tile_ref, outs[k].at[pl.ds(3 * cfg.tiles, 1)], id_sem.at[k])
        )
    for copy in copies:
        copy.start()
    for copy in copies:
        copy.wait()


def pack_conserved_kernel(cfg, me_ref, conserved_ref, *refs):
    outs, sem = refs[: cfg.n], refs[cfg.n]
    me = me_ref[0]
    copies = []
    for k in range(cfg.n):
        dest = jnp.bitwise_xor(me, k)
        copies.append(
            pltpu.make_async_copy(
                conserved_ref.at[:, pl.ds(dest * cfg.tiles, cfg.tiles)], outs[k], sem.at[k]
            )
        )
    for copy in copies:
        copy.start()
    for copy in copies:
        copy.wait()


def unpack_kernel(cfg, me_ref, *refs):
    first, second = refs[: cfg.n], refs[cfg.n : 2 * cfg.n]
    conserved_ref, field_ref, sem = refs[2 * cfg.n :]
    me = me_ref[0]
    copies = []
    for k in range(cfg.n):
        at = pl.ds(jnp.bitwise_xor(me, k) * cfg.tiles, cfg.tiles)
        copies.append(
            pltpu.make_async_copy(second[k].at[pl.ds(0, 5)], conserved_ref.at[:, at], sem.at[k, 0])
        )
        copies.append(
            pltpu.make_async_copy(first[k], field_ref.at[pl.ds(0, 2), at], sem.at[k, 1])
        )
        copies.append(
            pltpu.make_async_copy(
                second[k].at[pl.ds(5, 1)], field_ref.at[pl.ds(2, 1), at], sem.at[k, 2]
            )
        )
    for copy in copies:
        copy.start()
    for copy in copies:
        copy.wait()


def operators_kernel(cfg, me_ref, shift_ref, frac_ref, mh_ref, ml_ref, gh_ref, gl_ref, tj_ref):
    size = cfg.lanes
    first = (me_ref[0] * cfg.rows) // BS
    row = lax.broadcasted_iota(jnp.int32, (size, size), 0)
    col = lax.broadcasted_iota(jnp.int32, (size, size), 1)
    same = (row // BS) == (col // BS)
    e_in, e_out = row % BS, col % BS
    zero = jnp.zeros((size, size), F32)
    tj_ref[0] = jnp.where(same & (e_in < e_out), 1.0, zero).astype(BF16)
    tj_ref[1] = jnp.where(same, 1.0, zero).astype(BF16)
    for al in range(cfg.radii):
        _, rest = nearest_blocks(shift_ref[first + al])
        position = -jnp.full((1, size), frac_ref[first + al], F32)
        lagrange = []
        for a in NODES:
            product = jnp.ones_like(position)
            for b in NODES:
                if b != a:
                    product = product * ((position - float(b)) * (1.0 / float(a - b)))
            lagrange.append(product)
        weights = []
        for m in range(-3, 3):
            total = jnp.zeros_like(position)
            if m >= 0:
                for a in range(m + 1, 4):
                    total = total - lagrange[a + 3]
            else:
                for a in range(-3, m + 1):
                    total = total + lagrange[a + 3]
            weights.append(total)
        for d in range(3):
            at = e_in + BS * (d - 1)
            tap = jnp.where(same, at - e_out + rest, 100)
            remap, flux = zero, zero
            for a in NODES:
                hit = tap == a
                remap = jnp.where(hit, lagrange[a + 3], remap)
                if a < 3:
                    flux = jnp.where(hit, weights[a + 3], flux)
            flux = flux - jnp.where(same & (at < e_out - rest), 1.0, zero)
            mh_ref[al, d], ml_ref[al, d] = halves(remap)
            gh_ref[al, d], gl_ref[al, d] = halves(flux)


def gather_matrix(cfg, me, ids, whole):
    shape = (cfg.slots, 3 * cfg.slots)
    target = lax.broadcasted_iota(jnp.int32, shape, 0)
    owner = jnp.bitwise_xor(target >> 3, me)
    q_out, b_out = owner * PB + (target & 3), (target >> 2) & 1
    v = jnp.broadcast_to(ids, shape)
    q_in, b_in = (v >> 3) * PB + (v & 3), (v >> 2) & 1
    same = b_in == b_out
    cells = cfg.n * PB
    rows = []
    for d in (-1, 0, 1):
        hit = same & (((q_out - whole + d - q_in + 2 * cells) & (cells - 1)) == 0)
        rows.append(jnp.where(hit, 1.0, 0.0))
    rows.append(jnp.where(same & (q_in == q_out), 1.0, 0.0))
    back = (q_out - 1 - q_in + cells) & (cells - 1)
    count = jnp.where(back <= whole, 1.0, 0.0) + jnp.where(back + cells <= whole, 1.0, 0.0)
    rows.append(jnp.where(same, count, 0.0))
    return rows


def three_dots(high, low, mh, ml):
    rows = high.shape[0]
    both = dot(jnp.concatenate([high, low], axis=0), mh)
    return both[:rows] + both[rows:] + dot(high, ml)


def fields_kernel(cfg, me_ref, shift_ref, *refs):
    n, slots, tiles, wide = cfg.n, cfg.slots, cfg.tiles, cfg.lanes
    pieces = refs[:n]
    mh_ref, ml_ref, gh_ref, gl_ref, tj_ref = refs[n : n + 5]
    outs = refs[n + 5 : 2 * n + 5]
    bp_ref, halo_ref, polar_ref, rows_ref = refs[2 * n + 5 :]
    me = me_ref[0]
    first = (me * cfg.rows) // BS
    per = wide // LANES
    ids = jnp.concatenate([p[3 * tiles] for p in pieces] * 3, axis=0)
    ids = jnp.transpose(ids)[0:1].astype(jnp.int32)

    def source(c, al):
        x = jnp.concatenate(
            [
                jnp.concatenate([p[c * tiles + al * per + t] for p in pieces], axis=0)
                for t in range(per)
            ],
            axis=1,
        )
        return jnp.concatenate(thirds(x), axis=0)

    lane = lax.broadcasted_iota(jnp.int32, (slots, wide), 1)
    lower = (lax.broadcasted_iota(jnp.int32, (slots, wide), 0) >> 2) & 1 == 0
    total = []
    for al in range(cfg.radii):
        whole, _ = nearest_blocks(shift_ref[first + al])
        rows = gather_matrix(cfg, me, ids, whole)
        taken = jnp.concatenate(rows, axis=0).astype(BF16)
        rows_ref[al] = taken[: 3 * slots]
        own = taken[3 * slots : 4 * slots]
        y = [dot(taken, source(c, al)) for c in range(2)]
        part = [
            halves(jnp.concatenate([y[c][j * slots : (j + 1) * slots] for c in range(2)], axis=0))
            for j in range(5)
        ]
        remap = jnp.zeros((2 * slots, wide), F32)
        flux = jnp.zeros((2 * slots, wide), F32)
        for d in range(3):
            remap = remap + three_dots(*part[d], mh_ref[al, d], ml_ref[al, d])
            flux = flux + three_dots(*part[d], gh_ref[al, d], gl_ref[al, d])
        for j in range(2):
            both = dot(jnp.concatenate(part[3 + j], axis=0), tj_ref[j])
            flux = flux + (both[: 2 * slots] + both[2 * slots :])
        for c in range(2):
            for k in range(n):
                for t in range(per):
                    outs[k][c, al * per + t] = remap[
                        c * slots + k * SUB : c * slots + (k + 1) * SUB,
                        t * LANES : (t + 1) * LANES,
                    ]
        radial, polar = flux[:slots], flux[slots:]
        if cfg.split == 1:
            up = jnp.where(lower, jnp.concatenate([polar[4:], polar[:4]], axis=0), 0.0)
            after = pltpu.roll(jnp.where(lane < BS, up, polar), wide - BS, 1)
        else:
            after = jnp.where(lane < wide - BS, pltpu.roll(polar, wide - BS, 1), 0.0)
        azimuthal = dot(own, source(2, al))
        total.append((azimuthal + (after - polar) - radial, radial))
        if al == 0:
            for k in range(n):
                at = pl.ds(pl.multiple_of(jnp.bitwise_xor(me, k) * SUB, SUB), SUB)
                for t in range(per):
                    cut = (slice(k * SUB, (k + 1) * SUB), slice(t * LANES, (t + 1) * LANES))
                    halo_ref[t, at, :] = radial[cut]
                    if cfg.split > 1:
                        polar_ref[t, at, :] = polar[cut]
            if cfg.split == 1:
                polar_ref[...] = jnp.zeros_like(polar_ref)
    for al in range(cfg.radii):
        bp = total[al][0]
        if al + 1 < cfg.radii:
            bp = bp + total[al + 1][1]
        for t in range(per):
            bp_ref[al * per + t] = bp[:, t * LANES : (t + 1) * LANES]


def conserved_kernel(cfg, me_ref, *refs):
    n, slots, wide = cfg.n, cfg.slots, cfg.lanes
    pieces = refs[:n]
    mh_ref, ml_ref, rows_ref, bp_ref, halo_ref, polar_ref = refs[n : n + 6]
    outs = refs[n + 6 :]
    me = me_ref[0]
    per = wide // LANES
    for al in range(cfg.radii):
        taken = rows_ref[al]
        ys = []
        for c in range(5):
            x = jnp.concatenate(
                [
                    jnp.concatenate([p[c, al * per + t] for p in pieces], axis=0)
                    for t in range(per)
                ],
                axis=1,
            )
            ys.append(dot(taken, jnp.concatenate(thirds(x), axis=0)))
        out = jnp.zeros((5 * slots, wide), F32)
        for d in range(3):
            part = halves(
                jnp.concatenate([y[d * slots : (d + 1) * slots] for y in ys], axis=0)
            )
            out = out + three_dots(*part, mh_ref[al, d], ml_ref[al, d])
        for c in range(5):
            for k in range(n):
                for t in range(per):
                    outs[k][c, al * per + t] = out[
                        c * slots + k * SUB : c * slots + (k + 1) * SUB,
                        t * LANES : (t + 1) * LANES,
                    ]
    for k in range(n):
        at = pl.ds(pl.multiple_of(jnp.bitwise_xor(me, k) * SUB, SUB), SUB)
        for t in range(cfg.tiles):
            bp = bp_ref[t, k * SUB : (k + 1) * SUB, :]
            if t >= cfg.tiles - per:
                bp = bp + halo_ref[t - (cfg.tiles - per), at, :]
                if cfg.split > 1 and t == cfg.tiles - 1:
                    after = polar_ref[0, at, :]
                    low = (lax.broadcasted_iota(jnp.int32, after.shape, 0) >> 2) == 0
                    up = jnp.where(low, jnp.concatenate([after[4:], after[:4]], axis=0), 0.0)
                    here = lax.rem(me, cfg.split)
                    after = jnp.where(here == cfg.split - 1, up, after)
                    lane = lax.broadcasted_iota(jnp.int32, after.shape, 1)
                    after = jnp.where(lane < BS, after, 0.0)
                    bp = bp + pltpu.roll(after, LANES - BS, 1)
            outs[k][5, t] = bp


class Sizes:
    def __init__(self, n):
        self.n = n
        self.rows = BS * BS // n
        self.tiles = self.rows * BS // LANES
        self.lanes = min(self.rows, BS) * BS
        self.radii = max(1, self.rows // BS)
        self.split = max(1, BS // self.rows)
        self.slots = n * SUB


def shape(*dims, dtype=F32):
    return jax.ShapeDtypeStruct(dims, dtype)


def shards(conserved, face_field, block_ids, int_shift, frac_shift):
    n = lax.axis_size("phi")
    cfg = Sizes(n)
    count = lax.axis_size("tile") * n
    tiles, slots = cfg.tiles, cfg.slots
    per = cfg.lanes // LANES
    smem = pl.BlockSpec(memory_space=pltpu.SMEM)
    vmem = pl.BlockSpec(memory_space=pltpu.VMEM)
    anywhere = pl.BlockSpec(memory_space=pl.ANY)
    params = pltpu.CompilerParams(vmem_limit_bytes=48 * 2**20)
    me = lax.axis_index("phi").astype(jnp.int32).reshape(1)

    def tiled(x):
        return x.reshape(SUB, x.shape[1], n * tiles, LANES).transpose(1, 2, 0, 3)

    def untiled(x):
        return x.transpose(2, 0, 1, 3).reshape(SUB, x.shape[0], n * tiles * LANES)

    def exchange(pieces):
        return [pieces[0]] + [
            lax.ppermute(pieces[k], "phi", [(s, s ^ k) for s in range(n)]) for k in range(1, n)
        ]

    sent = pl.pallas_call(
        functools.partial(pack_fields_kernel, cfg),
        out_shape=[shape(3 * tiles + 1, SUB, LANES)] * n,
        in_specs=[smem, smem, anywhere],
        out_specs=[anywhere] * n,
        scratch_shapes=[
            pltpu.VMEM((1, SUB, LANES), F32),
            pltpu.SemaphoreType.DMA((3 * n,)),
            pltpu.SemaphoreType.DMA((n,)),
        ],
        name="pack_fields",
    )(me, block_ids, tiled(face_field))
    fields = exchange(sent)
    sent = pl.pallas_call(
        functools.partial(pack_conserved_kernel, cfg),
        out_shape=[shape(5, tiles, SUB, LANES)] * n,
        in_specs=[smem, anywhere],
        out_specs=[anywhere] * n,
        scratch_shapes=[pltpu.SemaphoreType.DMA((n,))],
        name="pack_conserved",
    )(me, tiled(conserved))
    fluid = exchange(sent)

    square = shape(cfg.radii, 3, cfg.lanes, cfg.lanes, dtype=BF16)
    mh, ml, gh, gl, tj = pl.pallas_call(
        functools.partial(operators_kernel, cfg),
        out_shape=[square] * 4 + [shape(2, cfg.lanes, cfg.lanes, dtype=BF16)],
        in_specs=[smem] * 3,
        out_specs=[vmem] * 5,
        compiler_params=params,
        name="operators",
    )(me, int_shift, frac_shift)

    *first, bp, halo, polar, taken = pl.pallas_call(
        functools.partial(fields_kernel, cfg),
        out_shape=[shape(2, tiles, SUB, LANES)] * n
        + [
            shape(tiles, slots, LANES),
            shape(per, slots, LANES),
            shape(per, slots, LANES) if cfg.split > 1 else shape(1, SUB, LANES),
            shape(cfg.radii, 3 * slots, 3 * slots, dtype=BF16),
        ],
        in_specs=[smem] * 2 + [vmem] * (n + 5),
        out_specs=[vmem] * (n + 4),
        compiler_params=params,
        name="fields",
    )(me, int_shift, *fields, mh, ml, gh, gl, tj)
    halo = lax.ppermute(
        halo, ("tile", "phi"), [(s, s - cfg.split) for s in range(cfg.split, count)]
    )
    if cfg.split > 1:
        polar = lax.ppermute(
            polar,
            "phi",
            [(s, s - 1 if s % cfg.split else s + cfg.split - 1) for s in range(n)],
        )
    first = exchange(first)
    second = pl.pallas_call(
        functools.partial(conserved_kernel, cfg),
        out_shape=[shape(6, tiles, SUB, LANES)] * n,
        in_specs=[smem] + [vmem] * (n + 6),
        out_specs=[vmem] * n,
        compiler_params=params,
        name="conserved",
    )(me, *fluid, mh, ml, taken, bp, halo, polar)
    second = exchange(second)
    conserved_out, field_out = pl.pallas_call(
        functools.partial(unpack_kernel, cfg),
        out_shape=[shape(5, n * tiles, SUB, LANES), shape(3, n * tiles, SUB, LANES)],
        in_specs=[smem] + [anywhere] * (2 * n),
        out_specs=[anywhere] * 2,
        scratch_shapes=[pltpu.SemaphoreType.DMA((n, 3))],
        name="unpack",
    )(me, *first, *second)
    return untiled(conserved_out), untiled(field_out)


def solution(mesh):
    return jax.shard_map(
        shards,
        mesh=mesh,
        in_specs=(
            P(("tile", "phi"), None, None),
            P(("tile", "phi"), None, None),
            P(("tile", "phi")),
            P("tile"),
            P("tile"),
        ),
        out_specs=(P(("tile", "phi"), None, None), P(("tile", "phi"), None, None)),
        check_vma=False,
    )
```

```python
import functools

import jax
import jax.numpy as jnp
from jax import lax
from jax.experimental import pallas as pl
from jax.experimental.pallas import tpu as pltpu
from jax.sharding import PartitionSpec as P

BS = 16
TB = 2
PB = 4
LANES = 128
SUB = 8
NODES = (-3, -2, -1, 0, 1, 2, 3)
F32 = jnp.float32
BF16 = jnp.bfloat16


def halves(x):
    hi = x.astype(BF16)
    return hi, (x - hi.astype(F32)).astype(BF16)


def thirds(x):
    hi = x.astype(BF16)
    rest = x - hi.astype(F32)
    mid = rest.astype(BF16)
    return hi, mid, (rest - mid.astype(F32)).astype(BF16)


def dot(a, b):
    return jnp.dot(a, b, preferred_element_type=F32)


def nearest_blocks(shift):
    whole = (shift + BS // 2) // BS
    return whole, shift - whole * BS


def pack_fields_kernel(cfg, me_ref, ids_ref, face_ref, *refs):
    outs, sem = refs[: cfg.n], refs[cfg.n]
    me = me_ref[0]
    copies = []
    for k in range(cfg.n):
        dest = jnp.bitwise_xor(me, k)
        for c in range(3):
            copies.append(
                pltpu.make_async_copy(
                    face_ref.at[c, pl.ds(dest * cfg.tiles, cfg.tiles)],
                    outs[k].at[pl.ds(c * cfg.tiles, cfg.tiles)],
                    sem.at[k * 3 + c],
                )
            )
    for copy in copies:
        copy.start()
    rows = lax.broadcasted_iota(jnp.int32, (SUB, LANES), 0)
    ids = jnp.zeros((SUB, LANES), jnp.int32)
    for slot in range(SUB):
        ids = jnp.where(rows == slot, ids_ref[slot], ids)
    for k in range(cfg.n):
        outs[k][3 * cfg.tiles] = ids.astype(F32)
    for copy in copies:
        copy.wait()


def pack_conserved_kernel(cfg, me_ref, conserved_ref, *refs):
    outs, sem = refs[: cfg.n], refs[cfg.n]
    me = me_ref[0]
    copies = []
    for k in range(cfg.n):
        dest = jnp.bitwise_xor(me, k)
        copies.append(
            pltpu.make_async_copy(
                conserved_ref.at[:, pl.ds(dest * cfg.tiles, cfg.tiles)], outs[k], sem.at[k]
            )
        )
    for copy in copies:
        copy.start()
    for copy in copies:
        copy.wait()


def unpack_kernel(cfg, me_ref, *refs):
    first, second = refs[: cfg.n], refs[cfg.n : 2 * cfg.n]
    conserved_ref, field_ref, sem = refs[2 * cfg.n :]
    me = me_ref[0]
    copies = []
    for k in range(cfg.n):
        at = pl.ds(jnp.bitwise_xor(me, k) * cfg.tiles, cfg.tiles)
        copies.append(
            pltpu.make_async_copy(second[k].at[pl.ds(0, 5)], conserved_ref.at[:, at], sem.at[k, 0])
        )
        copies.append(
            pltpu.make_async_copy(first[k], field_ref.at[pl.ds(0, 2), at], sem.at[k, 1])
        )
        copies.append(
            pltpu.make_async_copy(
                second[k].at[pl.ds(5, 1)], field_ref.at[pl.ds(2, 1), at], sem.at[k, 2]
            )
        )
    for copy in copies:
        copy.start()
    for copy in copies:
        copy.wait()


def operators_kernel(cfg, me_ref, shift_ref, frac_ref, mh_ref, ml_ref, gh_ref, gl_ref, tj_ref):
    size = cfg.lanes
    first = (me_ref[0] * cfg.rows) // BS
    row = lax.broadcasted_iota(jnp.int32, (size, size), 0)
    col = lax.broadcasted_iota(jnp.int32, (size, size), 1)
    same = (row // BS) == (col // BS)
    e_in, e_out = row % BS, col % BS
    zero = jnp.zeros((size, size), F32)
    tj_ref[0] = jnp.where(same & (e_in < e_out), 1.0, zero).astype(BF16)
    tj_ref[1] = jnp.where(same, 1.0, zero).astype(BF16)
    for al in range(cfg.radii):
        _, rest = nearest_blocks(shift_ref[first + al])
        position = -jnp.full((1, size), frac_ref[first + al], F32)
        lagrange = []
        for a in NODES:
            product = jnp.ones_like(position)
            for b in NODES:
                if b != a:
                    product = product * ((position - float(b)) * (1.0 / float(a - b)))
            lagrange.append(product)
        weights = []
        for m in range(-3, 3):
            total = jnp.zeros_like(position)
            if m >= 0:
                for a in range(m + 1, 4):
                    total = total - lagrange[a + 3]
            else:
                for a in range(-3, m + 1):
                    total = total + lagrange[a + 3]
            weights.append(total)
        for d in range(3):
            at = e_in + BS * (d - 1)
            tap = jnp.where(same, at - e_out + rest, 100)
            remap, flux = zero, zero
            for a in NODES:
                hit = tap == a
                remap = jnp.where(hit, lagrange[a + 3], remap)
                if a < 3:
                    flux = jnp.where(hit, weights[a + 3], flux)
            flux = flux - jnp.where(same & (at < e_out - rest), 1.0, zero)
            mh_ref[al, d], ml_ref[al, d] = halves(remap)
            gh_ref[al, d], gl_ref[al, d] = halves(flux)


def gather_matrix(cfg, me, ids, whole):
    shape = (cfg.slots, 3 * cfg.slots)
    target = lax.broadcasted_iota(jnp.int32, shape, 0)
    owner = jnp.bitwise_xor(target >> 3, me)
    q_out, b_out = owner * PB + (target & 3), (target >> 2) & 1
    v = jnp.broadcast_to(ids, shape)
    q_in, b_in = (v >> 3) * PB + (v & 3), (v >> 2) & 1
    same = b_in == b_out
    cells = cfg.n * PB
    rows = []
    for d in (-1, 0, 1):
        hit = same & (((q_out - whole + d - q_in + 2 * cells) & (cells - 1)) == 0)
        rows.append(jnp.where(hit, 1.0, 0.0))
    rows.append(jnp.where(same & (q_in == q_out), 1.0, 0.0))
    back = (q_out - 1 - q_in + cells) & (cells - 1)
    count = jnp.where(back <= whole, 1.0, 0.0) + jnp.where(back + cells <= whole, 1.0, 0.0)
    rows.append(jnp.where(same, count, 0.0))
    return rows


def three_dots(high, low, mh, ml):
    rows = high.shape[0]
    both = dot(jnp.concatenate([high, low], axis=0), mh)
    return both[:rows] + both[rows:] + dot(high, ml)


def fields_kernel(cfg, me_ref, shift_ref, *refs):
    n, slots, tiles, wide = cfg.n, cfg.slots, cfg.tiles, cfg.lanes
    pieces = refs[:n]
    mh_ref, ml_ref, gh_ref, gl_ref, tj_ref = refs[n : n + 5]
    outs = refs[n + 5 : 2 * n + 5]
    bp_ref, halo_ref, polar_ref, rows_ref = refs[2 * n + 5 :]
    me = me_ref[0]
    first = (me * cfg.rows) // BS
    per = wide // LANES
    ids = jnp.concatenate([p[3 * tiles] for p in pieces] * 3, axis=0)
    ids = jnp.transpose(ids)[0:1].astype(jnp.int32)

    def source(c, al):
        x = jnp.concatenate(
            [
                jnp.concatenate([p[c * tiles + al * per + t] for p in pieces], axis=0)
                for t in range(per)
            ],
            axis=1,
        )
        return jnp.concatenate(thirds(x), axis=0)

    lane = lax.broadcasted_iota(jnp.int32, (slots, wide), 1)
    lower = (lax.broadcasted_iota(jnp.int32, (slots, wide), 0) >> 2) & 1 == 0
    total = []
    for al in range(cfg.radii):
        whole, _ = nearest_blocks(shift_ref[first + al])
        rows = gather_matrix(cfg, me, ids, whole)
        taken = jnp.concatenate(rows, axis=0).astype(BF16)
        rows_ref[al] = taken[: 3 * slots]
        own = taken[3 * slots : 4 * slots]
        y = [dot(taken, source(c, al)) for c in range(2)]
        part = [
            halves(jnp.concatenate([y[c][j * slots : (j + 1) * slots] for c in range(2)], axis=0))
            for j in range(5)
        ]
        remap = jnp.zeros((2 * slots, wide), F32)
        flux = jnp.zeros((2 * slots, wide), F32)
        for d in range(3):
            remap = remap + three_dots(*part[d], mh_ref[al, d], ml_ref[al, d])
            flux = flux + three_dots(*part[d], gh_ref[al, d], gl_ref[al, d])
        for j in range(2):
            both = dot(jnp.concatenate(part[3 + j], axis=0), tj_ref[j])
            flux = flux + (both[: 2 * slots] + both[2 * slots :])
        for c in range(2):
            for k in range(n):
                for t in range(per):
                    outs[k][c, al * per + t] = remap[
                        c * slots + k * SUB : c * slots + (k + 1) * SUB,
                        t * LANES : (t + 1) * LANES,
                    ]
        radial, polar = flux[:slots], flux[slots:]
        if cfg.split == 1:
            up = jnp.where(lower, jnp.concatenate([polar[4:], polar[:4]], axis=0), 0.0)
            after = pltpu.roll(jnp.where(lane < BS, up, polar), wide - BS, 1)
        else:
            after = jnp.where(lane < wide - BS, pltpu.roll(polar, wide - BS, 1), 0.0)
        azimuthal = dot(own, source(2, al))
        total.append((azimuthal + (after - polar) - radial, radial))
        if al == 0:
            for k in range(n):
                at = pl.ds(pl.multiple_of(jnp.bitwise_xor(me, k) * SUB, SUB), SUB)
                for t in range(per):
                    cut = (slice(k * SUB, (k + 1) * SUB), slice(t * LANES, (t + 1) * LANES))
                    halo_ref[t, at, :] = radial[cut]
                    if cfg.split > 1:
                        polar_ref[t, at, :] = polar[cut]
            if cfg.split == 1:
                polar_ref[...] = jnp.zeros_like(polar_ref)
    for al in range(cfg.radii):
        bp = total[al][0]
        if al + 1 < cfg.radii:
            bp = bp + total[al + 1][1]
        for t in range(per):
            bp_ref[al * per + t] = bp[:, t * LANES : (t + 1) * LANES]


def conserved_kernel(cfg, me_ref, *refs):
    n, slots, wide = cfg.n, cfg.slots, cfg.lanes
    pieces = refs[:n]
    mh_ref, ml_ref, rows_ref, bp_ref, halo_ref, polar_ref = refs[n : n + 6]
    outs = refs[n + 6 :]
    me = me_ref[0]
    per = wide // LANES
    for al in range(cfg.radii):
        taken = rows_ref[al]
        ys = []
        for c in range(5):
            x = jnp.concatenate(
                [
                    jnp.concatenate([p[c, al * per + t] for p in pieces], axis=0)
                    for t in range(per)
                ],
                axis=1,
            )
            ys.append(dot(taken, jnp.concatenate(thirds(x), axis=0)))
        out = jnp.zeros((5 * slots, wide), F32)
        for d in range(3):
            part = halves(
                jnp.concatenate([y[d * slots : (d + 1) * slots] for y in ys], axis=0)
            )
            out = out + three_dots(*part, mh_ref[al, d], ml_ref[al, d])
        for c in range(5):
            for k in range(n):
                for t in range(per):
                    outs[k][c, al * per + t] = out[
                        c * slots + k * SUB : c * slots + (k + 1) * SUB,
                        t * LANES : (t + 1) * LANES,
                    ]
    for k in range(n):
        at = pl.ds(pl.multiple_of(jnp.bitwise_xor(me, k) * SUB, SUB), SUB)
        for t in range(cfg.tiles):
            bp = bp_ref[t, k * SUB : (k + 1) * SUB, :]
            if t >= cfg.tiles - per:
                bp = bp + halo_ref[t - (cfg.tiles - per), at, :]
                if cfg.split > 1 and t == cfg.tiles - 1:
                    after = polar_ref[0, at, :]
                    low = (lax.broadcasted_iota(jnp.int32, after.shape, 0) >> 2) == 0
                    up = jnp.where(low, jnp.concatenate([after[4:], after[:4]], axis=0), 0.0)
                    here = lax.rem(me, cfg.split)
                    after = jnp.where(here == cfg.split - 1, up, after)
                    lane = lax.broadcasted_iota(jnp.int32, after.shape, 1)
                    after = jnp.where(lane < BS, after, 0.0)
                    bp = bp + pltpu.roll(after, LANES - BS, 1)
            outs[k][5, t] = bp


class Sizes:
    def __init__(self, n):
        self.n = n
        self.rows = BS * BS // n
        self.tiles = self.rows * BS // LANES
        self.lanes = min(self.rows, BS) * BS
        self.radii = max(1, self.rows // BS)
        self.split = max(1, BS // self.rows)
        self.slots = n * SUB


def shape(*dims, dtype=F32):
    return jax.ShapeDtypeStruct(dims, dtype)


def shards(conserved, face_field, block_ids, int_shift, frac_shift):
    n = lax.axis_size("phi")
    cfg = Sizes(n)
    count = lax.axis_size("tile") * n
    tiles, slots = cfg.tiles, cfg.slots
    per = cfg.lanes // LANES
    smem = pl.BlockSpec(memory_space=pltpu.SMEM)
    vmem = pl.BlockSpec(memory_space=pltpu.VMEM)
    anywhere = pl.BlockSpec(memory_space=pl.ANY)
    params = pltpu.CompilerParams(vmem_limit_bytes=48 * 2**20)
    me = lax.axis_index("phi").astype(jnp.int32).reshape(1)

    def tiled(x):
        return x.reshape(SUB, x.shape[1], n * tiles, LANES).transpose(1, 2, 0, 3)

    def untiled(x):
        return x.transpose(2, 0, 1, 3).reshape(SUB, x.shape[0], n * tiles * LANES)

    def exchange(pieces):
        return [pieces[0]] + [
            lax.ppermute(pieces[k], "phi", [(s, s ^ k) for s in range(n)]) for k in range(1, n)
        ]

    sent = pl.pallas_call(
        functools.partial(pack_fields_kernel, cfg),
        out_shape=[shape(3 * tiles + 1, SUB, LANES)] * n,
        in_specs=[smem, smem, anywhere],
        out_specs=[vmem] * n,
        scratch_shapes=[pltpu.SemaphoreType.DMA((3 * n,))],
        name="pack_fields",
    )(me, block_ids, tiled(face_field))
    fields = exchange(sent)
    sent = pl.pallas_call(
        functools.partial(pack_conserved_kernel, cfg),
        out_shape=[shape(5, tiles, SUB, LANES)] * n,
        in_specs=[smem, anywhere],
        out_specs=[vmem] * n,
        scratch_shapes=[pltpu.SemaphoreType.DMA((n,))],
        name="pack_conserved",
    )(me, tiled(conserved))
    fluid = exchange(sent)

    square = shape(cfg.radii, 3, cfg.lanes, cfg.lanes, dtype=BF16)
    mh, ml, gh, gl, tj = pl.pallas_call(
        functools.partial(operators_kernel, cfg),
        out_shape=[square] * 4 + [shape(2, cfg.lanes, cfg.lanes, dtype=BF16)],
        in_specs=[smem] * 3,
        out_specs=[vmem] * 5,
        compiler_params=params,
        name="operators",
    )(me, int_shift, frac_shift)

    *first, bp, halo, polar, taken = pl.pallas_call(
        functools.partial(fields_kernel, cfg),
        out_shape=[shape(2, tiles, SUB, LANES)] * n
        + [
            shape(tiles, slots, LANES),
            shape(per, slots, LANES),
            shape(per, slots, LANES) if cfg.split > 1 else shape(1, SUB, LANES),
            shape(cfg.radii, 3 * slots, 3 * slots, dtype=BF16),
        ],
        in_specs=[smem] * 2 + [vmem] * (n + 5),
        out_specs=[vmem] * (n + 4),
        compiler_params=params,
        name="fields",
    )(me, int_shift, *fields, mh, ml, gh, gl, tj)
    halo = lax.ppermute(
        halo, ("tile", "phi"), [(s, s - cfg.split) for s in range(cfg.split, count)]
    )
    if cfg.split > 1:
        polar = lax.ppermute(
            polar,
            "phi",
            [(s, s - 1 if s % cfg.split else s + cfg.split - 1) for s in range(n)],
        )
    first = exchange(first)
    second = pl.pallas_call(
        functools.partial(conserved_kernel, cfg),
        out_shape=[shape(6, tiles, SUB, LANES)] * n,
        in_specs=[smem] + [vmem] * (n + 6),
        out_specs=[vmem] * n,
        compiler_params=params,
        name="conserved",
    )(me, *fluid, mh, ml, taken, bp, halo, polar)
    second = exchange(second)
    conserved_out, field_out = pl.pallas_call(
        functools.partial(unpack_kernel, cfg),
        out_shape=[shape(5, n * tiles, SUB, LANES), shape(3, n * tiles, SUB, LANES)],
        in_specs=[smem] + [vmem] * (2 * n),
        out_specs=[anywhere] * 2,
        scratch_shapes=[pltpu.SemaphoreType.DMA((n, 3))],
        name="unpack",
    )(me, *first, *second)
    return untiled(conserved_out), untiled(field_out)


def solution(mesh):
    return jax.shard_map(
        shards,
        mesh=mesh,
        in_specs=(
            P(("tile", "phi"), None, None),
            P(("tile", "phi"), None, None),
            P(("tile", "phi")),
            P("tile"),
            P("tile"),
        ),
        out_specs=(P(("tile", "phi"), None, None), P(("tile", "phi"), None, None)),
        check_vma=False,
    )
```

```python
import functools

import jax
import jax.numpy as jnp
from jax import lax
from jax.experimental import pallas as pl
from jax.experimental.pallas import tpu as pltpu
from jax.sharding import PartitionSpec as P

BS = 16
TB = 2
PB = 4
LANES = 128
SUB = 8
NODES = (-3, -2, -1, 0, 1, 2, 3)
F32 = jnp.float32
BF16 = jnp.bfloat16


def halves(x):
    hi = x.astype(BF16)
    return hi, (x - hi.astype(F32)).astype(BF16)


def thirds(x):
    hi = x.astype(BF16)
    rest = x - hi.astype(F32)
    mid = rest.astype(BF16)
    return hi, mid, (rest - mid.astype(F32)).astype(BF16)


def dot(a, b):
    return jnp.dot(a, b, preferred_element_type=F32)


def nearest_blocks(shift):
    whole = (shift + BS // 2) // BS
    return whole, shift - whole * BS


def start_all(copies):
    for copy in copies:
        copy.start()
    return copies


def wait_all(copies):
    for copy in copies:
        copy.wait()


def copy_in(cfg, source_ref, count, dest, out_ref, at, sem):
    return [
        pltpu.make_async_copy(
            source_ref.at[c, pl.ds(dest * cfg.tiles, cfg.tiles)],
            out_ref.at[pl.ds(at + c * cfg.tiles, cfg.tiles)],
            sem.at[c],
        )
        for c in range(count)
    ]


def id_tile(ids_ref):
    rows = lax.broadcasted_iota(jnp.int32, (SUB, LANES), 0)
    ids = jnp.zeros((SUB, LANES), jnp.int32)
    for slot in range(SUB):
        ids = jnp.where(rows == slot, ids_ref[slot], ids)
    return ids.astype(F32)


def pack_kernel(cfg, me_ref, source_ref, *refs):
    outs, sem = refs[: cfg.n], refs[cfg.n]
    copies = []
    for out, k in zip(outs, cfg.order):
        dest = jnp.bitwise_xor(me_ref[0], k)
        copies += copy_in(cfg, source_ref, source_ref.shape[0], dest, out, 0, sem.at[k])
    wait_all(start_all(copies))


def pack_fields_kernel(cfg, me_ref, ids_ref, *refs):
    ids = id_tile(ids_ref)
    for out in refs[1 : cfg.n + 1]:
        out[3 * cfg.tiles] = ids
    pack_kernel(cfg, me_ref, *refs)


def unpack_kernel(cfg, me_ref, *refs):
    pieces = refs[: cfg.n]
    conserved_ref, field_ref, sem = refs[cfg.n :]
    copies = []
    for piece, k in zip(pieces, cfg.order):
        at = pl.ds(jnp.bitwise_xor(me_ref[0], k) * cfg.tiles, cfg.tiles)
        for j, (first, count, out) in enumerate(((0, 5, conserved_ref), (5, 3, field_ref))):
            copies.append(
                pltpu.make_async_copy(
                    piece.at[pl.ds(first, count)], out.at[:, at], sem.at[k, j]
                )
            )
    wait_all(start_all(copies))


def operators_kernel(cfg, me_ref, shift_ref, frac_ref, mh_ref, ml_ref, gh_ref, gl_ref, tj_ref):
    size = cfg.lanes
    first = (me_ref[0] * cfg.rows) // BS
    row = lax.broadcasted_iota(jnp.int32, (size, size), 0)
    col = lax.broadcasted_iota(jnp.int32, (size, size), 1)
    same = (row // BS) == (col // BS)
    e_in, e_out = row % BS, col % BS
    zero = jnp.zeros((size, size), F32)
    tj_ref[0] = jnp.where(same & (e_in < e_out), 1.0, zero).astype(BF16)
    tj_ref[1] = jnp.where(same, 1.0, zero).astype(BF16)
    for al in range(cfg.radii):
        _, rest = nearest_blocks(shift_ref[first + al])
        position = -jnp.full((1, size), frac_ref[first + al], F32)
        lagrange = []
        for a in NODES:
            product = jnp.ones_like(position)
            for b in NODES:
                if b != a:
                    product = product * ((position - float(b)) * (1.0 / float(a - b)))
            lagrange.append(product)
        weights = []
        for m in range(-3, 3):
            total = jnp.zeros_like(position)
            if m >= 0:
                for a in range(m + 1, 4):
                    total = total - lagrange[a + 3]
            else:
                for a in range(-3, m + 1):
                    total = total + lagrange[a + 3]
            weights.append(total)
        for d in range(3):
            at = e_in + BS * (d - 1)
            tap = jnp.where(same, at - e_out + rest, 100)
            remap, flux = zero, zero
            for a in NODES:
                hit = tap == a
                remap = jnp.where(hit, lagrange[a + 3], remap)
                if a < 3:
                    flux = jnp.where(hit, weights[a + 3], flux)
            flux = flux - jnp.where(same & (at < e_out - rest), 1.0, zero)
            mh_ref[al, d], ml_ref[al, d] = halves(remap)
            gh_ref[al, d], gl_ref[al, d] = halves(flux)


def gather_matrix(cfg, me, ids, whole):
    shape = (cfg.slots, 3 * cfg.slots)
    target = lax.broadcasted_iota(jnp.int32, shape, 0)
    owner = jnp.bitwise_xor(target >> 3, me)
    q_out, b_out = owner * PB + (target & 3), (target >> 2) & 1
    v = jnp.broadcast_to(ids, shape)
    q_in, b_in = (v >> 3) * PB + (v & 3), (v >> 2) & 1
    same = b_in == b_out
    cells = cfg.n * PB
    rows = []
    for d in (-1, 0, 1):
        hit = same & (((q_out - whole + d - q_in + 2 * cells) & (cells - 1)) == 0)
        rows.append(jnp.where(hit, 1.0, 0.0))
    rows.append(jnp.where(same & (q_in == q_out), 1.0, 0.0))
    back = (q_out - 1 - q_in + cells) & (cells - 1)
    count = jnp.where(back <= whole, 1.0, 0.0) + jnp.where(back + cells <= whole, 1.0, 0.0)
    rows.append(jnp.where(same, count, 0.0))
    return rows


def three_dots(high, low, mh, ml):
    rows = high.shape[0]
    both = dot(jnp.concatenate([high, low], axis=0), mh)
    return both[:rows] + both[rows:] + dot(high, ml)


def fields_kernel(cfg, me_ref, shift_ref, *refs):
    n, slots, tiles, wide = cfg.n, cfg.slots, cfg.tiles, cfg.lanes
    pieces = refs[:n]
    mh_ref, ml_ref, gh_ref, gl_ref, tj_ref = refs[n : n + 5]
    outs = refs[n + 5 : 2 * n + 5]
    bp_ref, halo_ref, polar_ref, rows_ref = refs[2 * n + 5 :]
    me = me_ref[0]
    first = (me * cfg.rows) // BS
    per = wide // LANES
    ids = jnp.concatenate([p[3 * tiles] for p in pieces] * 3, axis=0)
    ids = jnp.transpose(ids)[0:1].astype(jnp.int32)

    def source(c, al):
        x = jnp.concatenate(
            [
                jnp.concatenate([p[c * tiles + al * per + t] for p in pieces], axis=0)
                for t in range(per)
            ],
            axis=1,
        )
        return jnp.concatenate(thirds(x), axis=0)

    lane = lax.broadcasted_iota(jnp.int32, (slots, wide), 1)
    lower = (lax.broadcasted_iota(jnp.int32, (slots, wide), 0) >> 2) & 1 == 0
    total = []
    for al in range(cfg.radii):
        whole, _ = nearest_blocks(shift_ref[first + al])
        rows = gather_matrix(cfg, me, ids, whole)
        taken = jnp.concatenate(rows, axis=0).astype(BF16)
        rows_ref[al] = taken[: 3 * slots]
        own = taken[3 * slots : 4 * slots]
        y = [dot(taken, source(c, al)) for c in range(2)]
        part = [
            halves(jnp.concatenate([y[c][j * slots : (j + 1) * slots] for c in range(2)], axis=0))
            for j in range(5)
        ]
        remap = jnp.zeros((2 * slots, wide), F32)
        flux = jnp.zeros((2 * slots, wide), F32)
        for d in range(3):
            remap = remap + three_dots(*part[d], mh_ref[al, d], ml_ref[al, d])
            flux = flux + three_dots(*part[d], gh_ref[al, d], gl_ref[al, d])
        for j in range(2):
            both = dot(jnp.concatenate(part[3 + j], axis=0), tj_ref[j])
            flux = flux + (both[: 2 * slots] + both[2 * slots :])
        for c in range(2):
            for k in range(n):
                for t in range(per):
                    outs[cfg.order.index(k)][c, al * per + t] = remap[
                        c * slots + k * SUB : c * slots + (k + 1) * SUB,
                        t * LANES : (t + 1) * LANES,
                    ]
        radial, polar = flux[:slots], flux[slots:]
        if cfg.split == 1:
            up = jnp.where(lower, jnp.concatenate([polar[4:], polar[:4]], axis=0), 0.0)
            after = pltpu.roll(jnp.where(lane < BS, up, polar), wide - BS, 1)
        else:
            after = jnp.where(lane < wide - BS, pltpu.roll(polar, wide - BS, 1), 0.0)
        azimuthal = dot(own, source(2, al))
        total.append((azimuthal + (after - polar) - radial, radial))
        if al == 0:
            for k in range(n):
                at = pl.ds(pl.multiple_of(jnp.bitwise_xor(me, k) * SUB, SUB), SUB)
                for t in range(per):
                    cut = (slice(k * SUB, (k + 1) * SUB), slice(t * LANES, (t + 1) * LANES))
                    halo_ref[t, at, :] = radial[cut]
                    if cfg.split > 1:
                        polar_ref[t, at, :] = polar[cut]
            if cfg.split == 1:
                polar_ref[...] = jnp.zeros_like(polar_ref)
    for al in range(cfg.radii):
        bp = total[al][0]
        if al + 1 < cfg.radii:
            bp = bp + total[al + 1][1]
        for t in range(per):
            bp_ref[al * per + t] = bp[:, t * LANES : (t + 1) * LANES]


def conserved_kernel(cfg, me_ref, *refs):
    n, slots, tiles, wide = cfg.n, cfg.slots, cfg.tiles, cfg.lanes
    pieces = refs[:n]
    mh_ref, ml_ref, rows_ref, bp_ref, halo_ref, polar_ref = refs[n : n + 6]
    remapped = refs[n + 6 : 2 * n + 6]
    outs = refs[2 * n + 6 :]
    me = me_ref[0]
    for k in range(n):
        outs[k][5:7] = remapped[k][...]
    per = wide // LANES
    for al in range(cfg.radii):
        taken = rows_ref[al]
        ys = []
        for c in range(5):
            x = jnp.concatenate(
                [
                    jnp.concatenate([p[c * tiles + al * per + t] for p in pieces], axis=0)
                    for t in range(per)
                ],
                axis=1,
            )
            ys.append(dot(taken, jnp.concatenate(thirds(x), axis=0)))
        out = jnp.zeros((5 * slots, wide), F32)
        for d in range(3):
            part = halves(
                jnp.concatenate([y[d * slots : (d + 1) * slots] for y in ys], axis=0)
            )
            out = out + three_dots(*part, mh_ref[al, d], ml_ref[al, d])
        for c in range(5):
            for k in range(n):
                for t in range(per):
                    outs[cfg.order.index(k)][c, al * per + t] = out[
                        c * slots + k * SUB : c * slots + (k + 1) * SUB,
                        t * LANES : (t + 1) * LANES,
                    ]
    for k in range(n):
        at = pl.ds(pl.multiple_of(jnp.bitwise_xor(me, k) * SUB, SUB), SUB)
        for t in range(cfg.tiles):
            bp = bp_ref[t, k * SUB : (k + 1) * SUB, :]
            if t >= cfg.tiles - per:
                bp = bp + halo_ref[t - (cfg.tiles - per), at, :]
                if cfg.split > 1 and t == cfg.tiles - 1:
                    after = polar_ref[0, at, :]
                    low = (lax.broadcasted_iota(jnp.int32, after.shape, 0) >> 2) == 0
                    up = jnp.where(low, jnp.concatenate([after[4:], after[:4]], axis=0), 0.0)
                    here = lax.rem(me, cfg.split)
                    after = jnp.where(here == cfg.split - 1, up, after)
                    lane = lax.broadcasted_iota(jnp.int32, after.shape, 1)
                    after = jnp.where(lane < BS, after, 0.0)
                    bp = bp + pltpu.roll(after, LANES - BS, 1)
            outs[cfg.order.index(k)][7, t] = bp


class Sizes:
    def __init__(self, n):
        self.n = n
        self.order = list(range(n // 2, n)) + list(range(n // 2 - 1, -1, -1))
        self.rows = BS * BS // n
        self.tiles = self.rows * BS // LANES
        self.lanes = min(self.rows, BS) * BS
        self.radii = max(1, self.rows // BS)
        self.split = max(1, BS // self.rows)
        self.slots = n * SUB


def shape(*dims, dtype=F32):
    return jax.ShapeDtypeStruct(dims, dtype)


def shards(conserved, face_field, block_ids, int_shift, frac_shift):
    n = lax.axis_size("phi")
    cfg = Sizes(n)
    count = lax.axis_size("tile") * n
    tiles, slots = cfg.tiles, cfg.slots
    per = cfg.lanes // LANES
    smem = pl.BlockSpec(memory_space=pltpu.SMEM)
    vmem = pl.BlockSpec(memory_space=pltpu.VMEM)
    hbm = pl.BlockSpec(memory_space=pltpu.MemorySpace.HBM)

    def grant(mib):
        return pltpu.CompilerParams(vmem_limit_bytes=min(mib, 48) * 2**20)

    me = lax.axis_index("phi").astype(jnp.int32).reshape(1)

    def tiled(x):
        return x.reshape(SUB, x.shape[1], n * tiles, LANES).transpose(1, 2, 0, 3)

    def untiled(x):
        return x.transpose(2, 0, 1, 3).reshape(SUB, x.shape[0], n * tiles * LANES)

    def exchange(pieces):
        return [
            lax.ppermute(piece, "phi", [(s, s ^ k) for s in range(n)]) if k else piece
            for piece, k in zip(pieces, cfg.order)
        ]

    def pack(kernel, count, name, *operands):
        return pl.pallas_call(
            functools.partial(kernel, cfg),
            out_shape=[shape(count, SUB, LANES)] * n,
            in_specs=[smem] * (len(operands) - 1) + [hbm],
            out_specs=[vmem] * n,
            scratch_shapes=[pltpu.SemaphoreType.DMA((n, 5))],
            compiler_params=grant(2),
            name=name,
        )(*operands)

    fields = exchange(
        pack(pack_fields_kernel, 3 * tiles + 1, "pack_fields", me, block_ids, tiled(face_field))
    )
    fluid = exchange(pack(pack_kernel, 5 * tiles, "pack_conserved", me, tiled(conserved)))

    square = shape(cfg.radii, 3, cfg.lanes, cfg.lanes, dtype=BF16)
    mh, ml, gh, gl, tj = pl.pallas_call(
        functools.partial(operators_kernel, cfg),
        out_shape=[square] * 4 + [shape(2, cfg.lanes, cfg.lanes, dtype=BF16)],
        in_specs=[smem] * 3,
        out_specs=[vmem] * 5,
        compiler_params=grant(8),
        name="operators",
    )(me, int_shift, frac_shift)

    *first, bp, halo, polar, taken = pl.pallas_call(
        functools.partial(fields_kernel, cfg),
        out_shape=[shape(2, tiles, SUB, LANES)] * n
        + [
            shape(tiles, slots, LANES),
            shape(per, slots, LANES),
            shape(per, slots, LANES) if cfg.split > 1 else shape(1, SUB, LANES),
            shape(cfg.radii, 3 * slots, 3 * slots, dtype=BF16),
        ],
        in_specs=[smem] * 2 + [vmem] * (n + 5),
        out_specs=[vmem] * (n + 4),
        compiler_params=grant(2 * n),
        name="fields",
    )(me, int_shift, *fields, mh, ml, gh, gl, tj)
    halo = lax.ppermute(
        halo, ("tile", "phi"), [(s, s - cfg.split) for s in range(cfg.split, count)]
    )
    if cfg.split > 1:
        polar = lax.ppermute(
            polar,
            "phi",
            [(s, s - 1 if s % cfg.split else s + cfg.split - 1) for s in range(n)],
        )
    done = pl.pallas_call(
        functools.partial(conserved_kernel, cfg),
        out_shape=[shape(8, tiles, SUB, LANES)] * n,
        in_specs=[smem] + [vmem] * (2 * n + 6),
        out_specs=[vmem] * n,
        compiler_params=grant(2 * n),
        name="conserved",
    )(me, *fluid, mh, ml, taken, bp, halo, polar, *first)
    conserved_out, field_out = pl.pallas_call(
        functools.partial(unpack_kernel, cfg),
        out_shape=[shape(5, n * tiles, SUB, LANES), shape(3, n * tiles, SUB, LANES)],
        in_specs=[smem] + [vmem] * n,
        out_specs=[hbm] * 2,
        scratch_shapes=[pltpu.SemaphoreType.DMA((n, 2))],
        compiler_params=grant(2),
        name="unpack",
    )(me, *exchange(done))
    return untiled(conserved_out), untiled(field_out)


def solution(mesh):
    return jax.shard_map(
        shards,
        mesh=mesh,
        in_specs=(
            P(("tile", "phi"), None, None),
            P(("tile", "phi"), None, None),
            P(("tile", "phi")),
            P("tile"),
            P("tile"),
        ),
        out_specs=(P(("tile", "phi"), None, None), P(("tile", "phi"), None, None)),
        check_vma=False,
    )
```

```python
import functools

import jax
import jax.numpy as jnp
from jax import lax
from jax.experimental import pallas as pl
from jax.experimental.pallas import tpu as pltpu
from jax.sharding import PartitionSpec as P

BS = 16
TB = 2
PB = 4
LANES = 128
SUB = 8
NODES = (-3, -2, -1, 0, 1, 2, 3)
F32 = jnp.float32
BF16 = jnp.bfloat16


def halves(x):
    hi = x.astype(BF16)
    return hi, (x - hi.astype(F32)).astype(BF16)


def thirds(x):
    hi = x.astype(BF16)
    rest = x - hi.astype(F32)
    mid = rest.astype(BF16)
    return hi, mid, (rest - mid.astype(F32)).astype(BF16)


def dot(a, b):
    return jnp.dot(a, b, preferred_element_type=F32)


def nearest_blocks(shift):
    whole = (shift + BS // 2) // BS
    return whole, shift - whole * BS


def start_all(copies):
    for copy in copies:
        copy.start()
    return copies


def wait_all(copies):
    for copy in copies:
        copy.wait()


def copy_in(cfg, source_ref, count, dest, out_ref, at, sem):
    return [
        pltpu.make_async_copy(
            source_ref.at[c, pl.ds(dest * cfg.tiles, cfg.tiles)],
            out_ref.at[pl.ds(at + c * cfg.tiles, cfg.tiles)],
            sem.at[c],
        )
        for c in range(count)
    ]


def id_tile(ids_ref):
    rows = lax.broadcasted_iota(jnp.int32, (SUB, LANES), 0)
    ids = jnp.zeros((SUB, LANES), jnp.int32)
    for slot in range(SUB):
        ids = jnp.where(rows == slot, ids_ref[slot], ids)
    return ids.astype(F32)


def pack_kernel(cfg, me_ref, ids_ref, face_ref, conserved_ref, *refs):
    outs, sem = refs[: cfg.n], refs[cfg.n]
    copies = []
    for out, k in zip(outs, cfg.order):
        dest = jnp.bitwise_xor(me_ref[0], k)
        copies += copy_in(cfg, face_ref, 3, dest, out, 0, sem.at[k, 0])
        copies += copy_in(cfg, conserved_ref, 5, dest, out, 3 * cfg.tiles, sem.at[k, 1])
    start_all(copies)
    ids = id_tile(ids_ref)
    for out in outs:
        out[8 * cfg.tiles] = ids
    wait_all(copies)


def unpack_kernel(cfg, me_ref, *refs):
    pieces, last_ref = refs[: cfg.n], refs[cfg.n]
    conserved_ref, field_ref, sem, last_sem = refs[cfg.n + 1 :]
    tiles, rest = cfg.tiles, cfg.tiles - cfg.per
    copies = []

    def put(source, out, sem):
        copies.append(pltpu.make_async_copy(source, out, sem))

    for piece, k in zip(pieces, cfg.order):
        source = jnp.bitwise_xor(me_ref[0], k)
        at = pl.ds(source * tiles, tiles)
        whole = piece.at[pl.ds(0, 7 * tiles)].reshape(7, tiles, SUB, LANES)
        put(whole.at[pl.ds(0, 5)], conserved_ref.at[:, at], sem.at[k, 0])
        put(whole.at[pl.ds(5, 2)], field_ref.at[pl.ds(0, 2), at], sem.at[k, 1])
        if rest:
            put(
                piece.at[pl.ds(7 * tiles, rest)],
                field_ref.at[2, pl.ds(source * tiles, rest)],
                sem.at[k, 2],
            )
    for source in range(cfg.n):
        put(
            last_ref.at[source],
            field_ref.at[2, pl.ds(source * tiles + rest, cfg.per)],
            last_sem.at[source],
        )
    wait_all(start_all(copies))


def operators_kernel(cfg, me_ref, shift_ref, frac_ref, mh_ref, ml_ref, gh_ref, gl_ref, tj_ref):
    size = cfg.lanes
    first = (me_ref[0] * cfg.rows) // BS
    row = lax.broadcasted_iota(jnp.int32, (size, size), 0)
    col = lax.broadcasted_iota(jnp.int32, (size, size), 1)
    same = (row // BS) == (col // BS)
    e_in, e_out = row % BS, col % BS
    zero = jnp.zeros((size, size), F32)
    tj_ref[0] = jnp.where(same & (e_in < e_out), 1.0, zero).astype(BF16)
    tj_ref[1] = jnp.where(same, 1.0, zero).astype(BF16)
    for al in range(cfg.radii):
        _, rest = nearest_blocks(shift_ref[first + al])
        position = -jnp.full((1, size), frac_ref[first + al], F32)
        lagrange = []
        for a in NODES:
            product = jnp.ones_like(position)
            for b in NODES:
                if b != a:
                    product = product * ((position - float(b)) * (1.0 / float(a - b)))
            lagrange.append(product)
        weights = []
        for m in range(-3, 3):
            total = jnp.zeros_like(position)
            if m >= 0:
                for a in range(m + 1, 4):
                    total = total - lagrange[a + 3]
            else:
                for a in range(-3, m + 1):
                    total = total + lagrange[a + 3]
            weights.append(total)
        for d in range(3):
            at = e_in + BS * (d - 1)
            tap = jnp.where(same, at - e_out + rest, 100)
            remap, flux = zero, zero
            for a in NODES:
                hit = tap == a
                remap = jnp.where(hit, lagrange[a + 3], remap)
                if a < 3:
                    flux = jnp.where(hit, weights[a + 3], flux)
            flux = flux - jnp.where(same & (at < e_out - rest), 1.0, zero)
            mh_ref[al, d], ml_ref[al, d] = halves(remap)
            gh_ref[al, d], gl_ref[al, d] = halves(flux)


def gather_matrix(cfg, me, ids, whole):
    shape = (cfg.slots, 3 * cfg.slots)
    target = lax.broadcasted_iota(jnp.int32, shape, 0)
    owner = jnp.bitwise_xor(target >> 3, me)
    q_out, b_out = owner * PB + (target & 3), (target >> 2) & 1
    v = jnp.broadcast_to(ids, shape)
    q_in, b_in = (v >> 3) * PB + (v & 3), (v >> 2) & 1
    same = b_in == b_out
    cells = cfg.n * PB
    rows = []
    for d in (-1, 0, 1):
        hit = same & (((q_out - whole + d - q_in + 2 * cells) & (cells - 1)) == 0)
        rows.append(jnp.where(hit, 1.0, 0.0))
    rows.append(jnp.where(same & (q_in == q_out), 1.0, 0.0))
    back = (q_out - 1 - q_in + cells) & (cells - 1)
    count = jnp.where(back <= whole, 1.0, 0.0) + jnp.where(back + cells <= whole, 1.0, 0.0)
    rows.append(jnp.where(same, count, 0.0))
    return rows


def three_dots(high, low, mh, ml):
    rows = high.shape[0]
    both = dot(jnp.concatenate([high, low], axis=0), mh)
    return both[:rows] + both[rows:] + dot(high, ml)


def rows_kernel(cfg, me_ref, shift_ref, *refs):
    n, slots, tiles, wide, per = cfg.n, cfg.slots, cfg.tiles, cfg.lanes, cfg.per
    pieces = refs[:n]
    mh_ref, ml_ref, gh_ref, gl_ref, tj_ref = refs[n : n + 5]
    outs = refs[n + 5 : 2 * n + 5]
    last_ref, halo_ref, polar_ref = refs[2 * n + 5 :]
    me = me_ref[0]
    first = (me * cfg.rows) // BS
    ids = jnp.concatenate([p[8 * tiles] for p in pieces] * 3, axis=0)
    ids = jnp.transpose(ids)[0:1].astype(jnp.int32)

    def source(c, al):
        x = jnp.concatenate(
            [
                jnp.concatenate([p[c * tiles + al * per + t] for p in pieces], axis=0)
                for t in range(per)
            ],
            axis=1,
        )
        return jnp.concatenate(thirds(x), axis=0)

    def by_owner(out_ref, value):
        for k in range(n):
            for t in range(per):
                out_ref[jnp.bitwise_xor(me, k), t] = value[
                    k * SUB : (k + 1) * SUB, t * LANES : (t + 1) * LANES
                ]

    def block(y, j):
        return y[j * slots : (j + 1) * slots]

    lane = lax.broadcasted_iota(jnp.int32, (slots, wide), 1)
    lower = (lax.broadcasted_iota(jnp.int32, (slots, wide), 0) >> 2) & 1 == 0
    total = []
    for al in range(cfg.radii):
        whole, _ = nearest_blocks(shift_ref[first + al])
        taken = jnp.concatenate(gather_matrix(cfg, me, ids, whole), axis=0).astype(BF16)
        ys = [dot(taken, source(c, al)) for c in range(2)]
        part = [halves(jnp.concatenate([block(y, j) for y in ys], axis=0)) for j in range(5)]
        flux = jnp.zeros((2 * slots, wide), F32)
        for d in range(3):
            flux = flux + three_dots(*part[d], gh_ref[al, d], gl_ref[al, d])
        for j in range(2):
            both = dot(jnp.concatenate(part[3 + j], axis=0), tj_ref[j])
            flux = flux + (both[: 2 * slots] + both[2 * slots :])
        radial, polar = flux[:slots], flux[slots:]
        if cfg.split == 1:
            up = jnp.where(lower, jnp.concatenate([polar[4:], polar[:4]], axis=0), 0.0)
            after = pltpu.roll(jnp.where(lane < BS, up, polar), wide - BS, 1)
        else:
            after = jnp.where(lane < wide - BS, pltpu.roll(polar, wide - BS, 1), 0.0)
        azimuthal = dot(taken[3 * slots : 4 * slots], source(2, al))
        total.append((azimuthal + (after - polar) - radial, radial))
        if al == 0:
            by_owner(halo_ref, radial)
            if cfg.split > 1:
                by_owner(polar_ref, polar)
            else:
                polar_ref[...] = jnp.zeros_like(polar_ref)
        ys = [dot(taken[: 3 * slots], source(3 + c, al)) for c in range(5)] + ys
        remap = jnp.zeros((7 * slots, wide), F32)
        for d in range(3):
            high, low = halves(jnp.concatenate([block(y, d) for y in ys], axis=0))
            remap = remap + three_dots(high, low, mh_ref[al, d], ml_ref[al, d])
        for out, k in zip(outs, cfg.order):
            for c in range(7):
                for t in range(per):
                    out[c * tiles + al * per + t] = remap[
                        c * slots + k * SUB : c * slots + (k + 1) * SUB,
                        t * LANES : (t + 1) * LANES,
                    ]
    for al in range(cfg.radii - 1):
        bp = total[al][0] + total[al + 1][1]
        for out, k in zip(outs, cfg.order):
            for t in range(per):
                out[7 * tiles + al * per + t] = bp[
                    k * SUB : (k + 1) * SUB, t * LANES : (t + 1) * LANES
                ]
    by_owner(last_ref, total[-1][0])


class Sizes:
    def __init__(self, n):
        self.n = n
        self.order = list(range(n // 2, n)) + list(range(n // 2 - 1, -1, -1))
        self.rows = BS * BS // n
        self.tiles = self.rows * BS // LANES
        self.lanes = min(self.rows, BS) * BS
        self.radii = max(1, self.rows // BS)
        self.per = self.lanes // LANES
        self.split = max(1, BS // self.rows)
        self.slots = n * SUB


def shape(*dims, dtype=F32):
    return jax.ShapeDtypeStruct(dims, dtype)


def shards(conserved, face_field, block_ids, int_shift, frac_shift):
    n = lax.axis_size("phi")
    cfg = Sizes(n)
    count = lax.axis_size("tile") * n
    tiles, per = cfg.tiles, cfg.per
    smem = pl.BlockSpec(memory_space=pltpu.SMEM)
    vmem = pl.BlockSpec(memory_space=pltpu.VMEM)
    hbm = pl.BlockSpec(memory_space=pltpu.MemorySpace.HBM)

    def grant(mib):
        return pltpu.CompilerParams(vmem_limit_bytes=min(mib, 48) * 2**20)

    me = lax.axis_index("phi").astype(jnp.int32).reshape(1)

    def tiled(x):
        return x.reshape(SUB, x.shape[1], n * tiles, LANES).transpose(1, 2, 0, 3)

    def untiled(x):
        return x.transpose(2, 0, 1, 3).reshape(SUB, x.shape[0], n * tiles * LANES)

    def exchange(pieces):
        return [
            lax.ppermute(piece, "phi", [(s, s ^ k) for s in range(n)]) if k else piece
            for piece, k in zip(pieces, cfg.order)
        ]

    packed = pl.pallas_call(
        functools.partial(pack_kernel, cfg),
        out_shape=[shape(8 * tiles + 1, SUB, LANES)] * n,
        in_specs=[smem, smem, hbm, hbm],
        out_specs=[vmem] * n,
        scratch_shapes=[pltpu.SemaphoreType.DMA((n, 2, 5))],
        compiler_params=grant(2),
        name="pack",
    )(me, block_ids, tiled(face_field), tiled(conserved))
    blocks = exchange(packed)

    square = shape(cfg.radii, 3, cfg.lanes, cfg.lanes, dtype=BF16)
    mh, ml, gh, gl, tj = pl.pallas_call(
        functools.partial(operators_kernel, cfg),
        out_shape=[square] * 4 + [shape(2, cfg.lanes, cfg.lanes, dtype=BF16)],
        in_specs=[smem] * 3,
        out_specs=[vmem] * 5,
        compiler_params=grant(8),
        name="operators",
    )(me, int_shift, frac_shift)

    by_owner = shape(n, per, SUB, LANES)
    *done, last, halo, polar = pl.pallas_call(
        functools.partial(rows_kernel, cfg),
        out_shape=[shape(8 * tiles - per, SUB, LANES)] * n
        + [by_owner, by_owner, by_owner if cfg.split > 1 else shape(1, 1, SUB, LANES)],
        in_specs=[smem] * 2 + [vmem] * (n + 5),
        out_specs=[vmem] * (n + 3),
        compiler_params=grant(2 * n),
        name="rows",
    )(me, int_shift, *blocks, mh, ml, gh, gl, tj)
    done = exchange(done)
    last = last + lax.ppermute(
        halo, ("tile", "phi"), [(s, s - cfg.split) for s in range(cfg.split, count)]
    )
    if cfg.split > 1:
        polar = lax.ppermute(
            polar,
            "phi",
            [(s, s - 1 if s % cfg.split else s + cfg.split - 1) for s in range(n)],
        )[:, 0, :, :BS]
        up = jnp.concatenate([polar[:, 4:], jnp.zeros_like(polar[:, :4])], axis=1)
        polar = jnp.where(me[0] % cfg.split == cfg.split - 1, up, polar)
        last = last.at[:, per - 1, :, LANES - BS :].add(polar)
    last = lax.all_to_all(last, "phi", split_axis=0, concat_axis=0, tiled=True)
    conserved_out, field_out = pl.pallas_call(
        functools.partial(unpack_kernel, cfg),
        out_shape=[shape(5, n * tiles, SUB, LANES), shape(3, n * tiles, SUB, LANES)],
        in_specs=[smem] + [vmem] * (n + 1),
        out_specs=[hbm] * 2,
        scratch_shapes=[pltpu.SemaphoreType.DMA((n, 3)), pltpu.SemaphoreType.DMA((n,))],
        compiler_params=grant(2),
        name="unpack",
    )(me, *done, last)
    return untiled(conserved_out), untiled(field_out)


def solution(mesh):
    return jax.shard_map(
        shards,
        mesh=mesh,
        in_specs=(
            P(("tile", "phi"), None, None),
            P(("tile", "phi"), None, None),
            P(("tile", "phi")),
            P("tile"),
            P("tile"),
        ),
        out_specs=(P(("tile", "phi"), None, None), P(("tile", "phi"), None, None)),
        check_vma=False,
    )
```

```python
import functools

import jax
import jax.numpy as jnp
from jax import lax
from jax.experimental import pallas as pl
from jax.experimental.pallas import tpu as pltpu
from jax.sharding import PartitionSpec as P

BS = 16
TB = 2
PB = 4
LANES = 128
SUB = 8
NODES = (-3, -2, -1, 0, 1, 2, 3)
F32 = jnp.float32
BF16 = jnp.bfloat16


def halves(x):
    hi = x.astype(BF16)
    return hi, (x - hi.astype(F32)).astype(BF16)


def thirds(x):
    hi = x.astype(BF16)
    rest = x - hi.astype(F32)
    mid = rest.astype(BF16)
    return hi, mid, (rest - mid.astype(F32)).astype(BF16)


def dot(a, b):
    return jnp.dot(a, b, preferred_element_type=F32)


def nearest_blocks(shift):
    whole = (shift + BS // 2) // BS
    return whole, shift - whole * BS


def start_all(copies):
    for copy in copies:
        copy.start()
    return copies


def wait_all(copies):
    for copy in copies:
        copy.wait()


def pack_kernel(cfg, me_ref, ids_ref, face_ref, conserved_ref, *refs):
    outs, (all_ref, id_ref, sem) = refs[: cfg.n], refs[cfg.n :]
    copies = [pltpu.make_async_copy(ids_ref, id_ref, sem.at[8])]
    for c in range(8):
        source = face_ref.at[c] if c < 3 else conserved_ref.at[c - 3]
        copies.append(pltpu.make_async_copy(source, all_ref.at[c], sem.at[c]))
    start_all(copies)
    dests = [jnp.bitwise_xor(me_ref[0], k) * cfg.tiles for k in cfg.order]
    copies[0].wait()
    rows = lax.broadcasted_iota(jnp.int32, (SUB, LANES), 0)
    ids = jnp.zeros((SUB, LANES), jnp.int32)
    for slot in range(SUB):
        ids = jnp.where(rows == slot, id_ref[slot], ids)
    for out in outs:
        out[8 * cfg.tiles] = ids.astype(F32)
    for c in range(8):
        copies[1 + c].wait()
        for out, dest in zip(outs, dests):
            out[c * cfg.tiles : (c + 1) * cfg.tiles] = all_ref[c, pl.ds(dest, cfg.tiles)]


def unpack_kernel(cfg, me_ref, *refs):
    pieces, (conserved_ref, field_ref, sem) = refs[: cfg.n], refs[cfg.n :]
    copies = []
    for piece, k in zip(pieces, cfg.order):
        at = pl.ds(jnp.bitwise_xor(me_ref[0], k) * cfg.tiles, cfg.tiles)
        for j, (first, count, out) in enumerate(((0, 5, conserved_ref), (5, 3, field_ref))):
            copies.append(
                pltpu.make_async_copy(
                    piece.at[pl.ds(first, count)], out.at[:, at], sem.at[k, j]
                )
            )
    wait_all(start_all(copies))


def operators_kernel(cfg, me_ref, shift_ref, frac_ref, mh_ref, ml_ref, gh_ref, gl_ref, tj_ref):
    size = cfg.lanes
    first = (me_ref[0] * cfg.rows) // BS
    row = lax.broadcasted_iota(jnp.int32, (size, size), 0)
    col = lax.broadcasted_iota(jnp.int32, (size, size), 1)
    same = (row // BS) == (col // BS)
    e_in, e_out = row % BS, col % BS
    zero = jnp.zeros((size, size), F32)
    tj_ref[0] = jnp.where(same & (e_in < e_out), 1.0, zero).astype(BF16)
    tj_ref[1] = jnp.where(same, 1.0, zero).astype(BF16)
    for al in range(cfg.radii):
        _, rest = nearest_blocks(shift_ref[first + al])
        position = -jnp.full((1, size), frac_ref[first + al], F32)
        lagrange = []
        for a in NODES:
            product = jnp.ones_like(position)
            for b in NODES:
                if b != a:
                    product = product * ((position - float(b)) * (1.0 / float(a - b)))
            lagrange.append(product)
        weights = []
        for m in range(-3, 3):
            total = jnp.zeros_like(position)
            if m >= 0:
                for a in range(m + 1, 4):
                    total = total - lagrange[a + 3]
            else:
                for a in range(-3, m + 1):
                    total = total + lagrange[a + 3]
            weights.append(total)
        for d in range(3):
            at = e_in + BS * (d - 1)
            tap = jnp.where(same, at - e_out + rest, 100)
            remap, flux = zero, zero
            for a in NODES:
                hit = tap == a
                remap = jnp.where(hit, lagrange[a + 3], remap)
                if a < 3:
                    flux = jnp.where(hit, weights[a + 3], flux)
            flux = flux - jnp.where(same & (at < e_out - rest), 1.0, zero)
            mh_ref[al, d], ml_ref[al, d] = halves(remap)
            gh_ref[al, d], gl_ref[al, d] = halves(flux)


def gather_matrix(cfg, me, ids, whole):
    shape = (cfg.slots, 3 * cfg.slots)
    target = lax.broadcasted_iota(jnp.int32, shape, 0)
    owner = jnp.bitwise_xor(target >> 3, me)
    q_out, b_out = owner * PB + (target & 3), (target >> 2) & 1
    v = jnp.broadcast_to(ids, shape)
    q_in, b_in = (v >> 3) * PB + (v & 3), (v >> 2) & 1
    same = b_in == b_out
    cells = cfg.n * PB
    rows = []
    for d in (-1, 0, 1):
        hit = same & (((q_out - whole + d - q_in + 2 * cells) & (cells - 1)) == 0)
        rows.append(jnp.where(hit, 1.0, 0.0))
    rows.append(jnp.where(same & (q_in == q_out), 1.0, 0.0))
    back = (q_out - 1 - q_in + cells) & (cells - 1)
    count = jnp.where(back <= whole, 1.0, 0.0) + jnp.where(back + cells <= whole, 1.0, 0.0)
    rows.append(jnp.where(same, count, 0.0))
    return rows


def three_dots(high, low, mh, ml):
    rows = high.shape[0]
    both = dot(jnp.concatenate([high, low], axis=0), mh)
    return both[:rows] + both[rows:] + dot(high, ml)


def source(cfg, pieces, c, al):
    x = jnp.concatenate(
        [
            jnp.concatenate([p[c * cfg.tiles + al * cfg.per + t] for p in pieces], axis=0)
            for t in range(cfg.per)
        ],
        axis=1,
    )
    return jnp.concatenate(thirds(x), axis=0)


def numbers(cfg, pieces):
    ids = jnp.concatenate([p[8 * cfg.tiles] for p in pieces] * 3, axis=0)
    return jnp.transpose(ids)[0:1].astype(jnp.int32)


def whole_fluxes(cfg, ys, al, gh_ref, gl_ref, tj_ref):
    slots = cfg.slots
    part = [
        halves(jnp.concatenate([y[j * slots : (j + 1) * slots] for y in ys], axis=0))
        for j in range(5)
    ]
    flux = 0.0
    for d in range(3):
        flux = flux + three_dots(*part[d], gh_ref[al, d], gl_ref[al, d])
    for j in range(2):
        both = dot(jnp.concatenate(part[3 + j], axis=0), tj_ref[j])
        rows = both.shape[0] // 2
        flux = flux + (both[:rows] + both[rows:])
    return flux


def by_owner(cfg, me, out_ref, value):
    for k in range(cfg.n):
        for t in range(cfg.per):
            out_ref[jnp.bitwise_xor(me, k), t] = value[
                k * SUB : (k + 1) * SUB, t * LANES : (t + 1) * LANES
            ]


def edge_kernel(cfg, me_ref, shift_ref, *refs):
    pieces, (gh_ref, gl_ref, tj_ref, halo_ref) = refs[: cfg.n], refs[cfg.n :]
    me = me_ref[0]
    whole, _ = nearest_blocks(shift_ref[(me * cfg.rows) // BS])
    taken = gather_matrix(cfg, me, numbers(cfg, pieces), whole)
    y = dot(jnp.concatenate(taken, axis=0).astype(BF16), source(cfg, pieces, 0, 0))
    by_owner(cfg, me, halo_ref, whole_fluxes(cfg, [y], 0, gh_ref, gl_ref, tj_ref))


def rows_kernel(cfg, me_ref, shift_ref, *refs):
    n, slots, tiles, wide, per = cfg.n, cfg.slots, cfg.tiles, cfg.lanes, cfg.per
    pieces = refs[:n]
    mh_ref, ml_ref, gh_ref, gl_ref, tj_ref, out_ref, polar_ref = refs[n:]
    me = me_ref[0]
    first = (me * cfg.rows) // BS
    ids = numbers(cfg, pieces)

    def put(c, al, value):
        for k in range(n):
            for t in range(per):
                out_ref[k, c, al * per + t] = value[
                    k * SUB : (k + 1) * SUB, t * LANES : (t + 1) * LANES
                ]

    lane = lax.broadcasted_iota(jnp.int32, (slots, wide), 1)
    lower = (lax.broadcasted_iota(jnp.int32, (slots, wide), 0) >> 2) & 1 == 0
    total = []
    for al in range(cfg.radii):
        whole, _ = nearest_blocks(shift_ref[first + al])
        taken = jnp.concatenate(gather_matrix(cfg, me, ids, whole), axis=0).astype(BF16)
        ys = [dot(taken, source(cfg, pieces, c, al)) for c in range(2)]
        flux = whole_fluxes(cfg, ys, al, gh_ref, gl_ref, tj_ref)
        radial, polar = flux[:slots], flux[slots:]
        if cfg.split == 1:
            up = jnp.where(lower, jnp.concatenate([polar[4:], polar[:4]], axis=0), 0.0)
            after = pltpu.roll(jnp.where(lane < BS, up, polar), wide - BS, 1)
            polar_ref[...] = jnp.zeros_like(polar_ref)
        else:
            after = jnp.where(lane < wide - BS, pltpu.roll(polar, wide - BS, 1), 0.0)
            by_owner(cfg, me, polar_ref, polar)
        azimuthal = dot(taken[3 * slots : 4 * slots], source(cfg, pieces, 2, al))
        total.append((azimuthal + (after - polar) - radial, radial))
        ys = [dot(taken[: 3 * slots], source(cfg, pieces, 3 + c, al)) for c in range(5)] + ys
        remap = 0.0
        for d in range(3):
            high, low = halves(
                jnp.concatenate([y[d * slots : (d + 1) * slots] for y in ys], axis=0)
            )
            remap = remap + three_dots(high, low, mh_ref[al, d], ml_ref[al, d])
        for c in range(7):
            put(c, al, remap[c * slots : (c + 1) * slots])
    for al in range(cfg.radii):
        bp = total[al][0]
        put(7, al, bp + total[al + 1][1] if al + 1 < cfg.radii else bp)


def finish_kernel(cfg, me_ref, rows_ref, halo_ref, polar_ref, *outs):
    me, rest = me_ref[0], cfg.tiles - cfg.per
    for out, k in zip(outs, cfg.order):
        owner = jnp.bitwise_xor(me, k)
        out[...] = rows_ref[k]
        out[7, rest:] = rows_ref[k, 7, rest:] + halo_ref[owner]
        if cfg.split > 1:
            after = polar_ref[owner, 0]
            row = lax.broadcasted_iota(jnp.int32, after.shape, 0)
            lane = lax.broadcasted_iota(jnp.int32, after.shape, 1)
            up = jnp.where(row < 4, jnp.concatenate([after[4:], after[:4]], axis=0), 0.0)
            after = jnp.where(lax.rem(me, cfg.split) == cfg.split - 1, up, after)
            after = pltpu.roll(jnp.where(lane < BS, after, 0.0), LANES - BS, 1)
            out[7, cfg.tiles - 1] = out[7, cfg.tiles - 1] + after


class Sizes:
    def __init__(self, n):
        self.n = n
        self.order = list(range(n // 2, n)) + list(range(n // 2 - 1, -1, -1))
        self.rows = BS * BS // n
        self.tiles = self.rows * BS // LANES
        self.lanes = min(self.rows, BS) * BS
        self.radii = max(1, self.rows // BS)
        self.per = self.lanes // LANES
        self.split = max(1, BS // self.rows)
        self.slots = n * SUB


def shape(*dims, dtype=F32):
    return jax.ShapeDtypeStruct(dims, dtype)


def shards(conserved, face_field, block_ids, int_shift, frac_shift):
    n = lax.axis_size("phi")
    cfg = Sizes(n)
    count = lax.axis_size("tile") * n
    tiles, per = cfg.tiles, cfg.per
    smem = pl.BlockSpec(memory_space=pltpu.SMEM)
    vmem = pl.BlockSpec(memory_space=pltpu.VMEM)
    hbm = pl.BlockSpec(memory_space=pltpu.MemorySpace.HBM)

    def grant(mib):
        return pltpu.CompilerParams(vmem_limit_bytes=min(mib, 48) * 2**20)

    me = lax.axis_index("phi").astype(jnp.int32).reshape(1)

    def tiled(x):
        return x.reshape(SUB, x.shape[1], n * tiles, LANES).transpose(1, 2, 0, 3)

    def untiled(x):
        return x.transpose(2, 0, 1, 3).reshape(SUB, x.shape[0], n * tiles * LANES)

    def exchange(pieces):
        return [
            lax.ppermute(piece, "phi", [(s, s ^ k) for s in range(n)]) if k else piece
            for piece, k in zip(pieces, cfg.order)
        ]

    def in_hbm(x):
        return pltpu.with_memory_space_constraint(x, pltpu.MemorySpace.HBM)

    packed = pl.pallas_call(
        functools.partial(pack_kernel, cfg),
        out_shape=[shape(8 * tiles + 1, SUB, LANES)] * n,
        in_specs=[smem, hbm, hbm, hbm],
        out_specs=[vmem] * n,
        scratch_shapes=[
            pltpu.VMEM((8, n * tiles, SUB, LANES), F32),
            pltpu.SMEM((SUB,), jnp.int32),
            pltpu.SemaphoreType.DMA((9,)),
        ],
        compiler_params=grant(3),
        name="pack",
    )(me, in_hbm(block_ids), in_hbm(tiled(face_field)), in_hbm(tiled(conserved)))
    blocks = exchange(packed)

    square = shape(cfg.radii, 3, cfg.lanes, cfg.lanes, dtype=BF16)
    mh, ml, gh, gl, tj = pl.pallas_call(
        functools.partial(operators_kernel, cfg),
        out_shape=[square] * 4 + [shape(2, cfg.lanes, cfg.lanes, dtype=BF16)],
        in_specs=[smem] * 3,
        out_specs=[vmem] * 5,
        compiler_params=grant(8),
        name="operators",
    )(me, int_shift, frac_shift)

    owners = shape(n, per, SUB, LANES)
    halo = pl.pallas_call(
        functools.partial(edge_kernel, cfg),
        out_shape=owners,
        in_specs=[smem] * 2 + [vmem] * (n + 3),
        out_specs=vmem,
        compiler_params=grant(2 * n),
        name="edge",
    )(me, int_shift, *blocks, gh, gl, tj)
    halo = lax.ppermute(
        halo, ("tile", "phi"), [(s, s - cfg.split) for s in range(cfg.split, count)]
    )
    rows, polar = pl.pallas_call(
        functools.partial(rows_kernel, cfg),
        out_shape=[
            shape(n, 8, tiles, SUB, LANES),
            owners if cfg.split > 1 else shape(1, 1, SUB, LANES),
        ],
        in_specs=[smem] * 2 + [vmem] * (n + 5),
        out_specs=[vmem] * 2,
        compiler_params=grant(2 * n),
        name="rows",
    )(me, int_shift, *blocks, mh, ml, gh, gl, tj)
    if cfg.split > 1:
        polar = lax.ppermute(
            polar,
            "phi",
            [(s, s - 1 if s % cfg.split else s + cfg.split - 1) for s in range(n)],
        )
    done = pl.pallas_call(
        functools.partial(finish_kernel, cfg),
        out_shape=[shape(8, tiles, SUB, LANES)] * n,
        in_specs=[smem] + [vmem] * 3,
        out_specs=[vmem] * n,
        compiler_params=grant(2),
        name="finish",
    )(me, rows, halo, polar)
    conserved_out, field_out = pl.pallas_call(
        functools.partial(unpack_kernel, cfg),
        out_shape=[shape(5, n * tiles, SUB, LANES), shape(3, n * tiles, SUB, LANES)],
        in_specs=[smem] + [vmem] * n,
        out_specs=[hbm] * 2,
        scratch_shapes=[pltpu.SemaphoreType.DMA((n, 2))],
        compiler_params=grant(2),
        name="unpack",
    )(me, *exchange(done))
    return untiled(conserved_out), untiled(field_out)


def solution(mesh):
    return jax.shard_map(
        shards,
        mesh=mesh,
        in_specs=(
            P(("tile", "phi"), None, None),
            P(("tile", "phi"), None, None),
            P(("tile", "phi")),
            P("tile"),
            P("tile"),
        ),
        out_specs=(P(("tile", "phi"), None, None), P(("tile", "phi"), None, None)),
        check_vma=False,
    )
```

```python
import functools

import jax
import jax.numpy as jnp
from jax import lax
from jax.experimental import pallas as pl
from jax.experimental.pallas import tpu as pltpu
from jax.sharding import PartitionSpec as P

BS = 16
TB = 2
PB = 4
LANES = 128
SUB = 8
NODES = (-3, -2, -1, 0, 1, 2, 3)
F32 = jnp.float32
BF16 = jnp.bfloat16


def halves(x):
    hi = x.astype(BF16)
    return hi, (x - hi.astype(F32)).astype(BF16)


def thirds(x):
    hi = x.astype(BF16)
    rest = x - hi.astype(F32)
    mid = rest.astype(BF16)
    return hi, mid, (rest - mid.astype(F32)).astype(BF16)


def dot(a, b):
    return jnp.dot(a, b, preferred_element_type=F32)


def nearest_blocks(shift):
    whole = (shift + BS // 2) // BS
    return whole, shift - whole * BS


def start_all(copies):
    for copy in copies:
        copy.start()
    return copies


def wait_all(copies):
    for copy in copies:
        copy.wait()


def pack_kernel(cfg, me_ref, ids_ref, face_ref, conserved_ref, *refs):
    n, tiles = cfg.n, cfg.tiles
    half = n // 2
    outs, (all_ref, id_ref, sem) = refs[: n + half], refs[n + half :]
    copies = [pltpu.make_async_copy(ids_ref, id_ref, sem.at[8])]
    for c in range(8):
        from_ref = face_ref.at[c] if c < 3 else conserved_ref.at[c - 3]
        copies.append(pltpu.make_async_copy(from_ref, all_ref.at[c], sem.at[c]))
    start_all(copies)
    dests = [jnp.bitwise_xor(me_ref[0], k) * tiles for k in cfg.order]
    copies[0].wait()
    rows = lax.broadcasted_iota(jnp.int32, (SUB, LANES), 0)
    ids = jnp.zeros((SUB, LANES), jnp.int32)
    for slot in range(SUB):
        ids = jnp.where(rows == slot, id_ref[slot], ids)
    for out in outs[:n]:
        out[4 * tiles] = ids.astype(F32)
    for c in range(8):
        copies[1 + c].wait()
        for j, dest in enumerate(dests):
            out, at = outs[j], c * tiles + (c >= 4)
            if c >= 4 and j < half:
                out, at = outs[n + j], (c - 4) * tiles
            out[at : at + tiles] = all_ref[c, pl.ds(dest, tiles)]


def unpack_kernel(cfg, me_ref, *refs):
    pieces, (conserved_ref, field_ref, sem) = refs[: cfg.n], refs[cfg.n :]
    copies = []
    for piece, k in zip(pieces, cfg.order):
        at = pl.ds(jnp.bitwise_xor(me_ref[0], k) * cfg.tiles, cfg.tiles)
        for j, (first, count, out) in enumerate(((0, 5, conserved_ref), (5, 3, field_ref))):
            copies.append(
                pltpu.make_async_copy(
                    piece.at[pl.ds(first, count)], out.at[:, at], sem.at[k, j]
                )
            )
    wait_all(start_all(copies))


def operators_kernel(cfg, me_ref, shift_ref, frac_ref, mh_ref, ml_ref, gh_ref, gl_ref, tj_ref):
    size = cfg.lanes
    first = (me_ref[0] * cfg.rows) // BS
    row = lax.broadcasted_iota(jnp.int32, (size, size), 0)
    col = lax.broadcasted_iota(jnp.int32, (size, size), 1)
    same = (row // BS) == (col // BS)
    e_in, e_out = row % BS, col % BS
    zero = jnp.zeros((size, size), F32)
    tj_ref[0] = jnp.where(same & (e_in < e_out), 1.0, zero).astype(BF16)
    tj_ref[1] = jnp.where(same, 1.0, zero).astype(BF16)
    for al in range(cfg.radii):
        _, rest = nearest_blocks(shift_ref[first + al])
        position = -jnp.full((1, size), frac_ref[first + al], F32)
        lagrange = []
        for a in NODES:
            product = jnp.ones_like(position)
            for b in NODES:
                if b != a:
                    product = product * ((position - float(b)) * (1.0 / float(a - b)))
            lagrange.append(product)
        weights = []
        for m in range(-3, 3):
            total = jnp.zeros_like(position)
            if m >= 0:
                for a in range(m + 1, 4):
                    total = total - lagrange[a + 3]
            else:
                for a in range(-3, m + 1):
                    total = total + lagrange[a + 3]
            weights.append(total)
        for d in range(3):
            at = e_in + BS * (d - 1)
            tap = jnp.where(same, at - e_out + rest, 100)
            remap, flux = zero, zero
            for a in NODES:
                hit = tap == a
                remap = jnp.where(hit, lagrange[a + 3], remap)
                if a < 3:
                    flux = jnp.where(hit, weights[a + 3], flux)
            flux = flux - jnp.where(same & (at < e_out - rest), 1.0, zero)
            mh_ref[al, d], ml_ref[al, d] = halves(remap)
            gh_ref[al, d], gl_ref[al, d] = halves(flux)


def gather_matrix(cfg, me, ids, whole):
    shape = (cfg.slots, 3 * cfg.slots)
    target = lax.broadcasted_iota(jnp.int32, shape, 0)
    owner = jnp.bitwise_xor(target >> 3, me)
    q_out, b_out = owner * PB + (target & 3), (target >> 2) & 1
    v = jnp.broadcast_to(ids, shape)
    q_in, b_in = (v >> 3) * PB + (v & 3), (v >> 2) & 1
    same = b_in == b_out
    cells = cfg.n * PB
    rows = []
    for d in (-1, 0, 1):
        hit = same & (((q_out - whole + d - q_in + 2 * cells) & (cells - 1)) == 0)
        rows.append(jnp.where(hit, 1.0, 0.0))
    rows.append(jnp.where(same & (q_in == q_out), 1.0, 0.0))
    back = (q_out - 1 - q_in + cells) & (cells - 1)
    count = jnp.where(back <= whole, 1.0, 0.0) + jnp.where(back + cells <= whole, 1.0, 0.0)
    rows.append(jnp.where(same, count, 0.0))
    return rows


def three_dots(high, low, mh, ml):
    rows = high.shape[0]
    both = dot(jnp.concatenate([high, low], axis=0), mh)
    return both[:rows] + both[rows:] + dot(high, ml)


def source(cfg, tiles_of, al):
    x = jnp.concatenate(
        [
            jnp.concatenate([p[at + al * cfg.per + t] for p, at in tiles_of], axis=0)
            for t in range(cfg.per)
        ],
        axis=1,
    )
    return jnp.concatenate(thirds(x), axis=0)


def first_half(cfg, pieces, c):
    return [(p, c * cfg.tiles) for p in pieces]


def second_half(cfg, pieces, c):
    near = [0] * (cfg.n // 2) + [4 * cfg.tiles + 1] * (cfg.n // 2)
    return [(p, at + c * cfg.tiles) for p, at in zip(pieces, near)]


def numbers(cfg, pieces):
    ids = jnp.concatenate([p[4 * cfg.tiles] for p in pieces] * 3, axis=0)
    return jnp.transpose(ids)[0:1].astype(jnp.int32)


def whole_fluxes(cfg, ys, al, gh_ref, gl_ref, tj_ref):
    slots = cfg.slots
    part = [
        halves(jnp.concatenate([y[j * slots : (j + 1) * slots] for y in ys], axis=0))
        for j in range(5)
    ]
    flux = 0.0
    for d in range(3):
        flux = flux + three_dots(*part[d], gh_ref[al, d], gl_ref[al, d])
    for j in range(2):
        both = dot(jnp.concatenate(part[3 + j], axis=0), tj_ref[j])
        rows = both.shape[0] // 2
        flux = flux + (both[:rows] + both[rows:])
    return flux


def by_owner(cfg, me, out_ref, value):
    for k in range(cfg.n):
        for t in range(cfg.per):
            out_ref[jnp.bitwise_xor(me, k), t] = value[
                k * SUB : (k + 1) * SUB, t * LANES : (t + 1) * LANES
            ]


def edge_kernel(cfg, me_ref, shift_ref, *refs):
    pieces, (gh_ref, gl_ref, tj_ref, halo_ref) = refs[: cfg.n], refs[cfg.n :]
    me = me_ref[0]
    whole, _ = nearest_blocks(shift_ref[(me * cfg.rows) // BS])
    taken = gather_matrix(cfg, me, numbers(cfg, pieces), whole)
    y = dot(jnp.concatenate(taken, axis=0).astype(BF16), source(cfg, first_half(cfg, pieces, 0), 0))
    by_owner(cfg, me, halo_ref, whole_fluxes(cfg, [y], 0, gh_ref, gl_ref, tj_ref))


def remapped(cfg, ys, al, mh_ref, ml_ref):
    total = 0.0
    for d in range(3):
        at = slice(d * cfg.slots, (d + 1) * cfg.slots)
        high, low = halves(jnp.concatenate([y[at] for y in ys], axis=0))
        total = total + three_dots(high, low, mh_ref[al, d], ml_ref[al, d])
    return total


def fields_kernel(cfg, me_ref, shift_ref, *refs):
    n, slots, wide, per = cfg.n, cfg.slots, cfg.lanes, cfg.per
    pieces = refs[:n]
    mh_ref, ml_ref, gh_ref, gl_ref, tj_ref, out_ref, taken_ref, polar_ref = refs[n:]
    me = me_ref[0]
    first = (me * cfg.rows) // BS
    ids = numbers(cfg, pieces)

    def put(c, al, value):
        for k in range(n):
            for t in range(per):
                out_ref[k, c, al * per + t] = value[
                    k * SUB : (k + 1) * SUB, t * LANES : (t + 1) * LANES
                ]

    lane = lax.broadcasted_iota(jnp.int32, (slots, wide), 1)
    lower = (lax.broadcasted_iota(jnp.int32, (slots, wide), 0) >> 2) & 1 == 0
    total = []
    for al in range(cfg.radii):
        whole, _ = nearest_blocks(shift_ref[first + al])
        taken = jnp.concatenate(gather_matrix(cfg, me, ids, whole), axis=0).astype(BF16)
        taken_ref[al] = taken[: 3 * slots]
        ys = [dot(taken, source(cfg, first_half(cfg, pieces, c), al)) for c in range(2)]
        flux = whole_fluxes(cfg, ys, al, gh_ref, gl_ref, tj_ref)
        radial, polar = flux[:slots], flux[slots:]
        if cfg.split == 1:
            up = jnp.where(lower, jnp.concatenate([polar[4:], polar[:4]], axis=0), 0.0)
            after = pltpu.roll(jnp.where(lane < BS, up, polar), wide - BS, 1)
            polar_ref[...] = jnp.zeros_like(polar_ref)
        else:
            after = jnp.where(lane < wide - BS, pltpu.roll(polar, wide - BS, 1), 0.0)
            by_owner(cfg, me, polar_ref, polar)
        azimuthal = dot(
            taken[3 * slots : 4 * slots], source(cfg, first_half(cfg, pieces, 2), al)
        )
        total.append((azimuthal + (after - polar) - radial, radial))
        ys.append(dot(taken[: 3 * slots], source(cfg, first_half(cfg, pieces, 3), al)))
        remap = remapped(cfg, ys, al, mh_ref, ml_ref)
        for c, at in enumerate((1, 2, 0)):
            put(at, al, remap[c * slots : (c + 1) * slots])
    for al in range(cfg.radii):
        bp = total[al][0]
        put(3, al, bp + total[al + 1][1] if al + 1 < cfg.radii else bp)


def finish_kernel(cfg, me_ref, *refs):
    n, slots, per = cfg.n, cfg.slots, cfg.per
    pieces = refs[:n]
    mh_ref, ml_ref, taken_ref, rows_ref, halo_ref, polar_ref = refs[n : n + 6]
    outs = refs[n + 6 :]
    me, rest = me_ref[0], cfg.tiles - cfg.per
    for al in range(cfg.radii):
        taken = taken_ref[al]
        ys = [dot(taken, source(cfg, second_half(cfg, pieces, c), al)) for c in range(4)]
        remap = remapped(cfg, ys, al, mh_ref, ml_ref)
        for out, k in zip(outs, cfg.order):
            for c in range(4):
                for t in range(per):
                    out[1 + c, al * per + t] = remap[
                        c * slots + k * SUB : c * slots + (k + 1) * SUB,
                        t * LANES : (t + 1) * LANES,
                    ]
    for out, k in zip(outs, cfg.order):
        owner = jnp.bitwise_xor(me, k)
        out[0] = rows_ref[k, 0]
        out[5:8] = rows_ref[k, 1:4]
        out[7, rest:] = rows_ref[k, 3, rest:] + halo_ref[owner]
        if cfg.split > 1:
            after = polar_ref[owner, 0]
            row = lax.broadcasted_iota(jnp.int32, after.shape, 0)
            lane = lax.broadcasted_iota(jnp.int32, after.shape, 1)
            up = jnp.where(row < 4, jnp.concatenate([after[4:], after[:4]], axis=0), 0.0)
            after = jnp.where(lax.rem(me, cfg.split) == cfg.split - 1, up, after)
            after = pltpu.roll(jnp.where(lane < BS, after, 0.0), LANES - BS, 1)
            out[7, cfg.tiles - 1] = out[7, cfg.tiles - 1] + after


class Sizes:
    def __init__(self, n):
        self.n = n
        self.order = list(range(n // 2, n)) + list(range(n // 2 - 1, -1, -1))
        self.rows = BS * BS // n
        self.tiles = self.rows * BS // LANES
        self.lanes = min(self.rows, BS) * BS
        self.radii = max(1, self.rows // BS)
        self.per = self.lanes // LANES
        self.split = max(1, BS // self.rows)
        self.slots = n * SUB


def shape(*dims, dtype=F32):
    return jax.ShapeDtypeStruct(dims, dtype)


def shards(conserved, face_field, block_ids, int_shift, frac_shift):
    n = lax.axis_size("phi")
    cfg = Sizes(n)
    count = lax.axis_size("tile") * n
    tiles, per = cfg.tiles, cfg.per
    smem = pl.BlockSpec(memory_space=pltpu.SMEM)
    vmem = pl.BlockSpec(memory_space=pltpu.VMEM)
    hbm = pl.BlockSpec(memory_space=pltpu.MemorySpace.HBM)

    def grant(mib):
        return pltpu.CompilerParams(vmem_limit_bytes=min(mib, 48) * 2**20)

    me = lax.axis_index("phi").astype(jnp.int32).reshape(1)

    def tiled(x):
        return x.reshape(SUB, x.shape[1], n * tiles, LANES).transpose(1, 2, 0, 3)

    def untiled(x):
        return x.transpose(2, 0, 1, 3).reshape(SUB, x.shape[0], n * tiles * LANES)

    half = n // 2

    def exchange(pieces, order):
        return [
            lax.ppermute(piece, "phi", [(s, s ^ k) for s in range(n)]) if k else piece
            for piece, k in zip(pieces, order)
        ]

    def in_hbm(x):
        return pltpu.with_memory_space_constraint(x, pltpu.MemorySpace.HBM)

    packed = pl.pallas_call(
        functools.partial(pack_kernel, cfg),
        out_shape=[shape(4 * tiles + 1, SUB, LANES)] * half
        + [shape(8 * tiles + 1, SUB, LANES)] * half
        + [shape(4 * tiles, SUB, LANES)] * half,
        in_specs=[smem] + [hbm] * 3,
        out_specs=[vmem] * (n + half),
        scratch_shapes=[
            pltpu.VMEM((8, n * tiles, SUB, LANES), F32),
            pltpu.SMEM((SUB,), jnp.int32),
            pltpu.SemaphoreType.DMA((9,)),
        ],
        compiler_params=grant(3),
        name="pack",
    )(me, in_hbm(block_ids), in_hbm(tiled(face_field)), in_hbm(tiled(conserved)))
    first = exchange(packed[:n], cfg.order)
    far_second = exchange(packed[n:], cfg.order)

    square = shape(cfg.radii, 3, cfg.lanes, cfg.lanes, dtype=BF16)
    mh, ml, gh, gl, tj = pl.pallas_call(
        functools.partial(operators_kernel, cfg),
        out_shape=[square] * 4 + [shape(2, cfg.lanes, cfg.lanes, dtype=BF16)],
        in_specs=[smem] * 3,
        out_specs=[vmem] * 5,
        compiler_params=grant(8),
        name="operators",
    )(me, int_shift, frac_shift)

    owners = shape(n, per, SUB, LANES)
    halo = pl.pallas_call(
        functools.partial(edge_kernel, cfg),
        out_shape=owners,
        in_specs=[smem] * 2 + [vmem] * (n + 3),
        out_specs=vmem,
        compiler_params=grant(2 * n),
        name="edge",
    )(me, int_shift, *first, gh, gl, tj)
    halo = lax.ppermute(
        halo, ("tile", "phi"), [(s, s - cfg.split) for s in range(cfg.split, count)]
    )
    rows, taken, polar = pl.pallas_call(
        functools.partial(fields_kernel, cfg),
        out_shape=[
            shape(n, 4, tiles, SUB, LANES),
            shape(cfg.radii, 3 * cfg.slots, 3 * cfg.slots, dtype=BF16),
            owners if cfg.split > 1 else shape(1, 1, SUB, LANES),
        ],
        in_specs=[smem] * 2 + [vmem] * (n + 5),
        out_specs=[vmem] * 3,
        compiler_params=grant(2 * n),
        name="fields",
    )(me, int_shift, *first, mh, ml, gh, gl, tj)
    if cfg.split > 1:
        polar = lax.ppermute(
            polar,
            "phi",
            [(s, s - 1 if s % cfg.split else s + cfg.split - 1) for s in range(n)],
        )
    done = pl.pallas_call(
        functools.partial(finish_kernel, cfg),
        out_shape=[shape(8, tiles, SUB, LANES)] * n,
        in_specs=[smem] + [vmem] * (n + 6),
        out_specs=[vmem] * n,
        compiler_params=grant(2 * n),
        name="finish",
    )(me, *far_second, *first[half:], mh, ml, taken, rows, halo, polar)
    conserved_out, field_out = pl.pallas_call(
        functools.partial(unpack_kernel, cfg),
        out_shape=[shape(5, n * tiles, SUB, LANES), shape(3, n * tiles, SUB, LANES)],
        in_specs=[smem] + [vmem] * n,
        out_specs=[hbm] * 2,
        scratch_shapes=[pltpu.SemaphoreType.DMA((n, 2))],
        compiler_params=grant(2),
        name="unpack",
    )(me, *exchange(done, cfg.order))
    return untiled(conserved_out), untiled(field_out)


def solution(mesh):
    return jax.shard_map(
        shards,
        mesh=mesh,
        in_specs=(
            P(("tile", "phi"), None, None),
            P(("tile", "phi"), None, None),
            P(("tile", "phi")),
            P("tile"),
            P("tile"),
        ),
        out_specs=(P(("tile", "phi"), None, None), P(("tile", "phi"), None, None)),
        check_vma=False,
    )
```

```python
import functools

import jax
import jax.numpy as jnp
from jax import lax
from jax.experimental import pallas as pl
from jax.experimental.pallas import tpu as pltpu
from jax.sharding import PartitionSpec as P

BS = 16
TB = 2
PB = 4
LANES = 128
SUB = 8
NODES = (-3, -2, -1, 0, 1, 2, 3)
F32 = jnp.float32
BF16 = jnp.bfloat16


def halves(x):
    hi = x.astype(BF16)
    return hi, (x - hi.astype(F32)).astype(BF16)


def thirds(x):
    hi = x.astype(BF16)
    rest = x - hi.astype(F32)
    mid = rest.astype(BF16)
    return hi, mid, (rest - mid.astype(F32)).astype(BF16)


def dot(a, b):
    return jnp.dot(a, b, preferred_element_type=F32)


def nearest_blocks(shift):
    whole = (shift + BS // 2) // BS
    return whole, shift - whole * BS


def start_all(copies):
    for copy in copies:
        copy.start()
    return copies


def wait_all(copies):
    for copy in copies:
        copy.wait()


def pack_kernel(cfg, me_ref, ids_ref, face_ref, conserved_ref, *refs):
    n, tiles = cfg.n, cfg.tiles
    half = n // 2
    outs, (all_ref, id_ref, sem) = refs[: n + half], refs[n + half :]
    copies = [pltpu.make_async_copy(ids_ref, id_ref, sem.at[8])]
    for c in range(8):
        from_ref = face_ref.at[c] if c < 3 else conserved_ref.at[c - 3]
        copies.append(pltpu.make_async_copy(from_ref, all_ref.at[c], sem.at[c]))
    start_all(copies)
    dests = [jnp.bitwise_xor(me_ref[0], k) * tiles for k in cfg.order]
    copies[0].wait()
    rows = lax.broadcasted_iota(jnp.int32, (SUB, LANES), 0)
    ids = jnp.zeros((SUB, LANES), jnp.int32)
    for slot in range(SUB):
        ids = jnp.where(rows == slot, id_ref[slot], ids)
    for out in outs[:n]:
        out[4 * tiles] = ids.astype(F32)
    for c in range(8):
        copies[1 + c].wait()
        for j, dest in enumerate(dests):
            out, at = outs[j], c * tiles + (c >= 4)
            if c >= 4 and j < half:
                out, at = outs[n + j], (c - 4) * tiles
            out[at : at + tiles] = all_ref[c, pl.ds(dest, tiles)]


def unpack_kernel(cfg, me_ref, *refs):
    n, tiles, rest = cfg.n, cfg.tiles, cfg.tiles - cfg.per
    half = n // 2
    pieces, (conserved_ref, field_ref, sem) = refs[: n + half], refs[n + half :]
    copies = []
    for j, k in enumerate(cfg.order):
        at = jnp.bitwise_xor(me_ref[0], k) * tiles
        here = pl.ds(at, tiles)
        first, second = pieces[j], pieces[n + j] if j < half else pieces[j]
        skip = 0 if j < half else 3 * tiles + rest
        parts = [
            (first.at[pl.ds(0, tiles)], conserved_ref.at[0, here]),
            (
                first.at[pl.ds(tiles, 2 * tiles)].reshape(2, tiles, SUB, LANES),
                field_ref.at[pl.ds(0, 2), here],
            ),
            (
                second.at[pl.ds(skip, 4 * tiles)].reshape(4, tiles, SUB, LANES),
                conserved_ref.at[pl.ds(1, 4), here],
            ),
            (
                second.at[pl.ds(skip + 4 * tiles, cfg.per)],
                field_ref.at[2, pl.ds(at + rest, cfg.per)],
            ),
        ]
        if rest:
            parts.append((first.at[pl.ds(3 * tiles, rest)], field_ref.at[2, pl.ds(at, rest)]))
        for i, (piece, out) in enumerate(parts):
            copies.append(pltpu.make_async_copy(piece, out, sem.at[j, i]))
    wait_all(start_all(copies))


def operators_kernel(cfg, me_ref, shift_ref, frac_ref, mh_ref, ml_ref, gh_ref, gl_ref, tj_ref):
    size = cfg.lanes
    first = (me_ref[0] * cfg.rows) // BS
    row = lax.broadcasted_iota(jnp.int32, (size, size), 0)
    col = lax.broadcasted_iota(jnp.int32, (size, size), 1)
    same = (row // BS) == (col // BS)
    e_in = lax.broadcasted_iota(jnp.int32, (BS, size), 0)
    e_out = lax.broadcasted_iota(jnp.int32, (BS, size), 1) % BS
    zero = jnp.zeros((BS, size), F32)

    def spread(pattern):
        return jnp.where(same, jnp.concatenate([pattern] * (size // BS), axis=0), 0.0)

    tj_ref[0] = spread(jnp.where(e_in < e_out, 1.0, zero)).astype(BF16)
    tj_ref[1] = spread(zero + 1.0).astype(BF16)
    for al in range(cfg.radii):
        _, rest = nearest_blocks(shift_ref[first + al])
        position = -jnp.full((1, size), frac_ref[first + al], F32)
        lagrange = []
        for a in NODES:
            product = jnp.ones_like(position)
            for b in NODES:
                if b != a:
                    product = product * ((position - float(b)) * (1.0 / float(a - b)))
            lagrange.append(product)
        weights = []
        for m in range(-3, 3):
            total = jnp.zeros_like(position)
            if m >= 0:
                for a in range(m + 1, 4):
                    total = total - lagrange[a + 3]
            else:
                for a in range(-3, m + 1):
                    total = total + lagrange[a + 3]
            weights.append(total)
        for d in range(3):
            at = e_in + BS * (d - 1)
            tap = at - e_out + rest
            remap, flux = zero, zero
            for a in NODES:
                hit = tap == a
                remap = jnp.where(hit, lagrange[a + 3], remap)
                if a < 3:
                    flux = jnp.where(hit, weights[a + 3], flux)
            flux = flux - jnp.where(at < e_out - rest, 1.0, zero)
            for value, high_ref, low_ref in ((remap, mh_ref, ml_ref), (flux, gh_ref, gl_ref)):
                high = value.astype(BF16).astype(F32)
                high_ref[al, d] = spread(high).astype(BF16)
                low_ref[al, d] = spread(value - high).astype(BF16)


def gather_matrix(cfg, me, ids, whole):
    shape = (cfg.slots, 3 * cfg.slots)
    target = lax.broadcasted_iota(jnp.int32, shape, 0)
    owner = jnp.bitwise_xor(target >> 3, me)
    q_out, b_out = owner * PB + (target & 3), (target >> 2) & 1
    v = jnp.broadcast_to(ids, shape)
    q_in, b_in = (v >> 3) * PB + (v & 3), (v >> 2) & 1
    same = b_in == b_out
    cells = cfg.n * PB
    rows = []
    for d in (-1, 0, 1):
        hit = same & (((q_out - whole + d - q_in + 2 * cells) & (cells - 1)) == 0)
        rows.append(jnp.where(hit, 1.0, 0.0))
    rows.append(jnp.where(same & (q_in == q_out), 1.0, 0.0))
    back = (q_out - 1 - q_in + cells) & (cells - 1)
    count = jnp.where(back <= whole, 1.0, 0.0) + jnp.where(back + cells <= whole, 1.0, 0.0)
    rows.append(jnp.where(same, count, 0.0))
    return rows


def three_dots(high, low, mh, ml):
    rows = high.shape[0]
    both = dot(jnp.concatenate([high, low], axis=0), mh)
    return both[:rows] + both[rows:] + dot(high, ml)


def source(cfg, tiles_of, al):
    x = jnp.concatenate(
        [
            jnp.concatenate([p[at + al * cfg.per + t] for p, at in tiles_of], axis=0)
            for t in range(cfg.per)
        ],
        axis=1,
    )
    return jnp.concatenate(thirds(x), axis=0)


def first_half(cfg, pieces, c):
    return [(p, c * cfg.tiles) for p in pieces]


def second_half(cfg, pieces, c):
    near = [0] * (cfg.n // 2) + [4 * cfg.tiles + 1] * (cfg.n // 2)
    return [(p, at + c * cfg.tiles) for p, at in zip(pieces, near)]


def numbers(cfg, pieces):
    ids = jnp.concatenate([p[4 * cfg.tiles] for p in pieces] * 3, axis=0)
    return jnp.transpose(ids)[0:1].astype(jnp.int32)


def whole_fluxes(cfg, ys, al, gh_ref, gl_ref, tj_ref):
    slots = cfg.slots
    part = [
        halves(jnp.concatenate([y[j * slots : (j + 1) * slots] for y in ys], axis=0))
        for j in range(5)
    ]
    flux = 0.0
    for d in range(3):
        flux = flux + three_dots(*part[d], gh_ref[al, d], gl_ref[al, d])
    for j in range(2):
        both = dot(jnp.concatenate(part[3 + j], axis=0), tj_ref[j])
        rows = both.shape[0] // 2
        flux = flux + (both[:rows] + both[rows:])
    return flux


def by_owner(cfg, me, out_ref, value):
    for k in range(cfg.n):
        for t in range(cfg.per):
            out_ref[jnp.bitwise_xor(me, k), t] = value[
                k * SUB : (k + 1) * SUB, t * LANES : (t + 1) * LANES
            ]


def edge_kernel(cfg, me_ref, shift_ref, *refs):
    pieces, (gh_ref, gl_ref, tj_ref, halo_ref) = refs[: cfg.n], refs[cfg.n :]
    me = me_ref[0]
    whole, _ = nearest_blocks(shift_ref[(me * cfg.rows) // BS])
    taken = gather_matrix(cfg, me, numbers(cfg, pieces), whole)
    y = dot(jnp.concatenate(taken, axis=0).astype(BF16), source(cfg, first_half(cfg, pieces, 0), 0))
    by_owner(cfg, me, halo_ref, whole_fluxes(cfg, [y], 0, gh_ref, gl_ref, tj_ref))


def remapped(cfg, ys, al, mh_ref, ml_ref):
    total = 0.0
    for d in range(3):
        at = slice(d * cfg.slots, (d + 1) * cfg.slots)
        high, low = halves(jnp.concatenate([y[at] for y in ys], axis=0))
        total = total + three_dots(high, low, mh_ref[al, d], ml_ref[al, d])
    return total


def fields_kernel(cfg, me_ref, shift_ref, *refs):
    n, slots, tiles, wide, per = cfg.n, cfg.slots, cfg.tiles, cfg.lanes, cfg.per
    half = n // 2
    pieces = refs[:n]
    mh_ref, ml_ref, gh_ref, gl_ref, tj_ref = refs[n : n + 5]
    outs = refs[n + 5 : n + 5 + half]
    near_ref, last_ref, taken_ref, polar_ref = refs[n + 5 + half :]
    me = me_ref[0]
    first = (me * cfg.rows) // BS
    ids = numbers(cfg, pieces)

    def put(c, al, value):
        for j, k in enumerate(cfg.order):
            for t in range(per):
                tile = value[k * SUB : (k + 1) * SUB, t * LANES : (t + 1) * LANES]
                if c == 3 and al == cfg.radii - 1:
                    last_ref[j, t] = tile
                elif j < half:
                    outs[j][c * tiles + al * per + t] = tile
                else:
                    near_ref[j - half, c * tiles + al * per + t] = tile

    lane = lax.broadcasted_iota(jnp.int32, (slots, wide), 1)
    lower = (lax.broadcasted_iota(jnp.int32, (slots, wide), 0) >> 2) & 1 == 0
    total = []
    for al in range(cfg.radii):
        whole, _ = nearest_blocks(shift_ref[first + al])
        taken = jnp.concatenate(gather_matrix(cfg, me, ids, whole), axis=0).astype(BF16)
        taken_ref[al] = taken[: 3 * slots]
        ys = [dot(taken, source(cfg, first_half(cfg, pieces, c), al)) for c in range(2)]
        flux = whole_fluxes(cfg, ys, al, gh_ref, gl_ref, tj_ref)
        radial, polar = flux[:slots], flux[slots:]
        if cfg.split == 1:
            up = jnp.where(lower, jnp.concatenate([polar[4:], polar[:4]], axis=0), 0.0)
            after = pltpu.roll(jnp.where(lane < BS, up, polar), wide - BS, 1)
            polar_ref[...] = jnp.zeros_like(polar_ref)
        else:
            after = jnp.where(lane < wide - BS, pltpu.roll(polar, wide - BS, 1), 0.0)
            by_owner(cfg, me, polar_ref, polar)
        azimuthal = dot(
            taken[3 * slots : 4 * slots], source(cfg, first_half(cfg, pieces, 2), al)
        )
        total.append((azimuthal + (after - polar) - radial, radial))
        ys.append(dot(taken[: 3 * slots], source(cfg, first_half(cfg, pieces, 3), al)))
        remap = remapped(cfg, ys, al, mh_ref, ml_ref)
        for c, at in enumerate((1, 2, 0)):
            put(at, al, remap[c * slots : (c + 1) * slots])
    for al in range(cfg.radii):
        bp = total[al][0]
        put(3, al, bp + total[al + 1][1] if al + 1 < cfg.radii else bp)


def finish_kernel(cfg, me_ref, *refs):
    n, slots, tiles, per = cfg.n, cfg.slots, cfg.tiles, cfg.per
    half, first = n // 2, 4 * cfg.tiles - cfg.per
    pieces = refs[:n]
    mh_ref, ml_ref, taken_ref, near_ref, last_ref, halo_ref, polar_ref = refs[n : n + 7]
    outs = refs[n + 7 :]
    me = me_ref[0]
    skip = [0] * half + [first] * half
    for al in range(cfg.radii):
        taken = taken_ref[al]
        ys = [dot(taken, source(cfg, second_half(cfg, pieces, c), al)) for c in range(4)]
        remap = remapped(cfg, ys, al, mh_ref, ml_ref)
        for out, k, at in zip(outs, cfg.order, skip):
            for c in range(4):
                for t in range(per):
                    out[at + c * tiles + al * per + t] = remap[
                        c * slots + k * SUB : c * slots + (k + 1) * SUB,
                        t * LANES : (t + 1) * LANES,
                    ]
    for j, (out, k, at) in enumerate(zip(outs, cfg.order, skip)):
        owner = jnp.bitwise_xor(me, k)
        if j >= half:
            out[:first] = near_ref[j - half]
        bp = last_ref[j] + halo_ref[owner]
        if cfg.split > 1:
            after = polar_ref[owner, 0]
            row = lax.broadcasted_iota(jnp.int32, after.shape, 0)
            lane = lax.broadcasted_iota(jnp.int32, after.shape, 1)
            up = jnp.where(row < 4, jnp.concatenate([after[4:], after[:4]], axis=0), 0.0)
            after = jnp.where(lax.rem(me, cfg.split) == cfg.split - 1, up, after)
            bp = bp + pltpu.roll(jnp.where(lane < BS, after, 0.0), LANES - BS, 1)[None]
        out[at + 4 * tiles : at + 4 * tiles + per] = bp


class Sizes:
    def __init__(self, n):
        self.n = n
        self.order = list(range(n // 2, n)) + list(range(n // 2 - 1, -1, -1))
        self.rows = BS * BS // n
        self.tiles = self.rows * BS // LANES
        self.lanes = min(self.rows, BS) * BS
        self.radii = max(1, self.rows // BS)
        self.per = self.lanes // LANES
        self.split = max(1, BS // self.rows)
        self.slots = n * SUB


def shape(*dims, dtype=F32):
    return jax.ShapeDtypeStruct(dims, dtype)


def shards(conserved, face_field, block_ids, int_shift, frac_shift):
    n = lax.axis_size("phi")
    cfg = Sizes(n)
    count = lax.axis_size("tile") * n
    tiles, per = cfg.tiles, cfg.per
    smem = pl.BlockSpec(memory_space=pltpu.SMEM)
    vmem = pl.BlockSpec(memory_space=pltpu.VMEM)
    hbm = pl.BlockSpec(memory_space=pltpu.MemorySpace.HBM)

    def grant(mib):
        return pltpu.CompilerParams(vmem_limit_bytes=min(mib, 48) * 2**20)

    me = lax.axis_index("phi").astype(jnp.int32).reshape(1)

    def tiled(x):
        return x.reshape(SUB, x.shape[1], n * tiles, LANES).transpose(1, 2, 0, 3)

    def untiled(x):
        return x.transpose(2, 0, 1, 3).reshape(SUB, x.shape[0], n * tiles * LANES)

    half = n // 2

    def exchange(pieces, order):
        return [
            lax.ppermute(piece, "phi", [(s, s ^ k) for s in range(n)]) if k else piece
            for piece, k in zip(pieces, order)
        ]

    def in_hbm(x):
        return pltpu.with_memory_space_constraint(x, pltpu.MemorySpace.HBM)

    packed = pl.pallas_call(
        functools.partial(pack_kernel, cfg),
        out_shape=[shape(4 * tiles + 1, SUB, LANES)] * half
        + [shape(8 * tiles + 1, SUB, LANES)] * half
        + [shape(4 * tiles, SUB, LANES)] * half,
        in_specs=[smem] + [hbm] * 3,
        out_specs=[vmem] * (n + half),
        scratch_shapes=[
            pltpu.VMEM((8, n * tiles, SUB, LANES), F32),
            pltpu.SMEM((SUB,), jnp.int32),
            pltpu.SemaphoreType.DMA((9,)),
        ],
        compiler_params=grant(3),
        name="pack",
    )(me, in_hbm(block_ids), in_hbm(tiled(face_field)), in_hbm(tiled(conserved)))
    first = exchange(packed[:n], cfg.order)
    far_second = exchange(packed[n:], cfg.order)

    square = shape(cfg.radii, 3, cfg.lanes, cfg.lanes, dtype=BF16)
    mh, ml, gh, gl, tj = pl.pallas_call(
        functools.partial(operators_kernel, cfg),
        out_shape=[square] * 4 + [shape(2, cfg.lanes, cfg.lanes, dtype=BF16)],
        in_specs=[smem] * 3,
        out_specs=[vmem] * 5,
        compiler_params=grant(8),
        name="operators",
    )(me, int_shift, frac_shift)

    owners = shape(n, per, SUB, LANES)
    halo = pl.pallas_call(
        functools.partial(edge_kernel, cfg),
        out_shape=owners,
        in_specs=[smem] * 2 + [vmem] * (n + 3),
        out_specs=vmem,
        compiler_params=grant(2 * n),
        name="edge",
    )(me, int_shift, *first, gh, gl, tj)
    halo = lax.ppermute(
        halo, ("tile", "phi"), [(s, s - cfg.split) for s in range(cfg.split, count)]
    )
    early = 4 * tiles - per
    *far_early, near_early, last, taken, polar = pl.pallas_call(
        functools.partial(fields_kernel, cfg),
        out_shape=[shape(early, SUB, LANES)] * half
        + [
            shape(half, early, SUB, LANES),
            owners,
            shape(cfg.radii, 3 * cfg.slots, 3 * cfg.slots, dtype=BF16),
            owners if cfg.split > 1 else shape(1, 1, SUB, LANES),
        ],
        in_specs=[smem] * 2 + [vmem] * (n + 5),
        out_specs=[vmem] * (half + 4),
        compiler_params=grant(2 * n),
        name="fields",
    )(me, int_shift, *first, mh, ml, gh, gl, tj)
    if cfg.split > 1:
        polar = lax.ppermute(
            polar,
            "phi",
            [(s, s - 1 if s % cfg.split else s + cfg.split - 1) for s in range(n)],
        )
    late = pl.pallas_call(
        functools.partial(finish_kernel, cfg),
        out_shape=[shape(4 * tiles + per, SUB, LANES)] * half
        + [shape(8 * tiles, SUB, LANES)] * half,
        in_specs=[smem] + [vmem] * (n + 7),
        out_specs=[vmem] * n,
        compiler_params=grant(2 * n),
        name="finish",
    )(me, *far_second, *first[half:], mh, ml, taken, near_early, last, halo, polar)
    far_early = exchange(far_early, cfg.order)
    late = exchange(late, cfg.order)
    conserved_out, field_out = pl.pallas_call(
        functools.partial(unpack_kernel, cfg),
        out_shape=[shape(5, n * tiles, SUB, LANES), shape(3, n * tiles, SUB, LANES)],
        in_specs=[smem] + [vmem] * (n + half),
        out_specs=[hbm] * 2,
        scratch_shapes=[pltpu.SemaphoreType.DMA((n, 5))],
        compiler_params=grant(2),
        name="unpack",
    )(me, *far_early, *late[half:], *late[:half])
    return untiled(conserved_out), untiled(field_out)


def solution(mesh):
    return jax.shard_map(
        shards,
        mesh=mesh,
        in_specs=(
            P(("tile", "phi"), None, None),
            P(("tile", "phi"), None, None),
            P(("tile", "phi")),
            P("tile"),
            P("tile"),
        ),
        out_specs=(P(("tile", "phi"), None, None), P(("tile", "phi"), None, None)),
        check_vma=False,
    )
```

```python
import functools

import jax
import jax.numpy as jnp
from jax import lax
from jax.experimental import pallas as pl
from jax.experimental.pallas import tpu as pltpu
from jax.sharding import PartitionSpec as P

BS = 16
TB = 2
PB = 4
LANES = 128
SUB = 8
NODES = (-3, -2, -1, 0, 1, 2, 3)
F32 = jnp.float32
BF16 = jnp.bfloat16


def halves(x):
    hi = x.astype(BF16)
    return hi, (x - hi.astype(F32)).astype(BF16)


def thirds(x):
    hi = x.astype(BF16)
    rest = x - hi.astype(F32)
    mid = rest.astype(BF16)
    return hi, mid, (rest - mid.astype(F32)).astype(BF16)


def dot(a, b):
    return jnp.dot(a, b, preferred_element_type=F32)


def nearest_blocks(shift):
    whole = (shift + BS // 2) // BS
    return whole, shift - whole * BS


def place(cfg, me_ref):
    phi, tile = lax.rem(me_ref[0], cfg.n), lax.div(me_ref[0], cfg.n)
    return phi, jnp.bitwise_xor(phi, lax.rem(tile, 2) * (cfg.n - 1))


def start_all(copies):
    for copy in copies:
        copy.start()
    return copies


def wait_all(copies):
    for copy in copies:
        copy.wait()


def pack_kernel(cfg, me_ref, ids_ref, face_ref, conserved_ref, *refs):
    me, group = place(cfg, me_ref)
    n, tiles = cfg.n, cfg.tiles
    half = n // 2
    outs, (all_ref, id_ref, sem) = refs[: n + half], refs[n + half :]
    copies = [pltpu.make_async_copy(ids_ref, id_ref, sem.at[8])]
    for c in range(8):
        from_ref = face_ref.at[c] if c < 3 else conserved_ref.at[c - 3]
        copies.append(pltpu.make_async_copy(from_ref, all_ref.at[c], sem.at[c]))
    start_all(copies)
    dests = [jnp.bitwise_xor(group, k) * tiles for k in cfg.order]
    copies[0].wait()
    rows = lax.broadcasted_iota(jnp.int32, (SUB, LANES), 0)
    ids = jnp.zeros((SUB, LANES), jnp.int32)
    for slot in range(SUB):
        ids = jnp.where(rows == slot, id_ref[slot], ids)
    for out in outs[:n]:
        out[4 * tiles] = ids.astype(F32)
    for c in range(8):
        copies[1 + c].wait()
        for j, dest in enumerate(dests):
            out, at = outs[j], c * tiles + (c >= 4)
            if c >= 4 and j < half:
                out, at = outs[n + j], (c - 4) * tiles
            out[at : at + tiles] = all_ref[c, pl.ds(dest, tiles)]


def unpack_kernel(cfg, me_ref, *refs):
    me, group = place(cfg, me_ref)
    pieces, (conserved_ref, field_ref, sem) = refs[: cfg.n], refs[cfg.n :]
    copies = []
    for piece, k in zip(pieces, cfg.order):
        at = pl.ds(jnp.bitwise_xor(group, k) * cfg.tiles, cfg.tiles)
        for j, (first, count, out) in enumerate(((0, 5, conserved_ref), (5, 3, field_ref))):
            copies.append(
                pltpu.make_async_copy(
                    piece.at[pl.ds(first, count)], out.at[:, at], sem.at[k, j]
                )
            )
    wait_all(start_all(copies))


def operators_kernel(cfg, me_ref, shift_ref, frac_ref, mh_ref, ml_ref, gh_ref, gl_ref, tj_ref):
    me, group = place(cfg, me_ref)
    size = cfg.lanes
    first = (group * cfg.rows) // BS
    row = lax.broadcasted_iota(jnp.int32, (size, size), 0)
    col = lax.broadcasted_iota(jnp.int32, (size, size), 1)
    same = (row // BS) == (col // BS)
    e_in = lax.broadcasted_iota(jnp.int32, (BS, size), 0)
    e_out = lax.broadcasted_iota(jnp.int32, (BS, size), 1) % BS
    zero = jnp.zeros((BS, size), F32)

    def spread(pattern):
        return jnp.where(same, jnp.concatenate([pattern] * (size // BS), axis=0), 0.0)

    tj_ref[0] = spread(jnp.where(e_in < e_out, 1.0, zero)).astype(BF16)
    tj_ref[1] = spread(zero + 1.0).astype(BF16)
    for al in range(cfg.radii):
        _, rest = nearest_blocks(shift_ref[first + al])
        position = -jnp.full((1, size), frac_ref[first + al], F32)
        lagrange = []
        for a in NODES:
            product = jnp.ones_like(position)
            for b in NODES:
                if b != a:
                    product = product * ((position - float(b)) * (1.0 / float(a - b)))
            lagrange.append(product)
        weights = []
        for m in range(-3, 3):
            total = jnp.zeros_like(position)
            if m >= 0:
                for a in range(m + 1, 4):
                    total = total - lagrange[a + 3]
            else:
                for a in range(-3, m + 1):
                    total = total + lagrange[a + 3]
            weights.append(total)
        for d in range(3):
            at = e_in + BS * (d - 1)
            tap = at - e_out + rest
            remap, flux = zero, zero
            for a in NODES:
                hit = tap == a
                remap = jnp.where(hit, lagrange[a + 3], remap)
                if a < 3:
                    flux = jnp.where(hit, weights[a + 3], flux)
            flux = flux - jnp.where(at < e_out - rest, 1.0, zero)
            for value, high_ref, low_ref in ((remap, mh_ref, ml_ref), (flux, gh_ref, gl_ref)):
                high = value.astype(BF16).astype(F32)
                high_ref[al, d] = spread(high).astype(BF16)
                low_ref[al, d] = spread(value - high).astype(BF16)


def gather_matrix(cfg, me, ids, whole):
    shape = (cfg.slots, 3 * cfg.slots)
    target = lax.broadcasted_iota(jnp.int32, shape, 0)
    owner = jnp.bitwise_xor(target >> 3, me)
    q_out, b_out = owner * PB + (target & 3), (target >> 2) & 1
    v = jnp.broadcast_to(ids, shape)
    q_in, b_in = (v >> 3) * PB + (v & 3), (v >> 2) & 1
    same = b_in == b_out
    cells = cfg.n * PB
    rows = []
    for d in (-1, 0, 1):
        hit = same & (((q_out - whole + d - q_in + 2 * cells) & (cells - 1)) == 0)
        rows.append(jnp.where(hit, 1.0, 0.0))
    rows.append(jnp.where(same & (q_in == q_out), 1.0, 0.0))
    back = (q_out - 1 - q_in + cells) & (cells - 1)
    count = jnp.where(back <= whole, 1.0, 0.0) + jnp.where(back + cells <= whole, 1.0, 0.0)
    rows.append(jnp.where(same, count, 0.0))
    return rows


def three_dots(high, low, mh, ml):
    rows = high.shape[0]
    both = dot(jnp.concatenate([high, low], axis=0), mh)
    return both[:rows] + both[rows:] + dot(high, ml)


def source(cfg, tiles_of, al):
    x = jnp.concatenate(
        [
            jnp.concatenate([p[at + al * cfg.per + t] for p, at in tiles_of], axis=0)
            for t in range(cfg.per)
        ],
        axis=1,
    )
    return jnp.concatenate(thirds(x), axis=0)


def first_half(cfg, pieces, c):
    return [(p, c * cfg.tiles) for p in pieces]


def second_half(cfg, pieces, c):
    near = [0] * (cfg.n // 2) + [4 * cfg.tiles + 1] * (cfg.n // 2)
    return [(p, at + c * cfg.tiles) for p, at in zip(pieces, near)]


def numbers(cfg, pieces):
    ids = jnp.concatenate([p[4 * cfg.tiles] for p in pieces] * 3, axis=0)
    return jnp.transpose(ids)[0:1].astype(jnp.int32)


def whole_fluxes(cfg, ys, al, gh_ref, gl_ref, tj_ref):
    slots = cfg.slots
    part = [
        halves(jnp.concatenate([y[j * slots : (j + 1) * slots] for y in ys], axis=0))
        for j in range(5)
    ]
    flux = 0.0
    for d in range(3):
        flux = flux + three_dots(*part[d], gh_ref[al, d], gl_ref[al, d])
    for j in range(2):
        both = dot(jnp.concatenate(part[3 + j], axis=0), tj_ref[j])
        rows = both.shape[0] // 2
        flux = flux + (both[:rows] + both[rows:])
    return flux


def by_owner(cfg, me, out_ref, value):
    for k in range(cfg.n):
        for t in range(cfg.per):
            out_ref[jnp.bitwise_xor(me, k), t] = value[
                k * SUB : (k + 1) * SUB, t * LANES : (t + 1) * LANES
            ]


def edge_kernel(cfg, me_ref, shift_ref, *refs):
    me, group = place(cfg, me_ref)
    pieces, (gh_ref, gl_ref, tj_ref, halo_ref) = refs[: cfg.n], refs[cfg.n :]
    whole, _ = nearest_blocks(shift_ref[(group * cfg.rows) // BS])
    taken = gather_matrix(cfg, me, numbers(cfg, pieces), whole)
    y = dot(jnp.concatenate(taken, axis=0).astype(BF16), source(cfg, first_half(cfg, pieces, 0), 0))
    by_owner(cfg, me, halo_ref, whole_fluxes(cfg, [y], 0, gh_ref, gl_ref, tj_ref))


def remapped(cfg, ys, al, mh_ref, ml_ref):
    total = 0.0
    for d in range(3):
        at = slice(d * cfg.slots, (d + 1) * cfg.slots)
        high, low = halves(jnp.concatenate([y[at] for y in ys], axis=0))
        total = total + three_dots(high, low, mh_ref[al, d], ml_ref[al, d])
    return total


def fields_kernel(cfg, me_ref, shift_ref, *refs):
    me, group = place(cfg, me_ref)
    n, slots, wide, per = cfg.n, cfg.slots, cfg.lanes, cfg.per
    pieces = refs[:n]
    mh_ref, ml_ref, gh_ref, gl_ref, tj_ref, out_ref, taken_ref, polar_ref = refs[n:]
    first = (group * cfg.rows) // BS
    ids = numbers(cfg, pieces)

    def put(c, al, value):
        for k in range(n):
            for t in range(per):
                out_ref[k, c, al * per + t] = value[
                    k * SUB : (k + 1) * SUB, t * LANES : (t + 1) * LANES
                ]

    lane = lax.broadcasted_iota(jnp.int32, (slots, wide), 1)
    lower = (lax.broadcasted_iota(jnp.int32, (slots, wide), 0) >> 2) & 1 == 0
    total = []
    for al in range(cfg.radii):
        whole, _ = nearest_blocks(shift_ref[first + al])
        taken = jnp.concatenate(gather_matrix(cfg, me, ids, whole), axis=0).astype(BF16)
        taken_ref[al] = taken[: 3 * slots]
        ys = [dot(taken, source(cfg, first_half(cfg, pieces, c), al)) for c in range(2)]
        flux = whole_fluxes(cfg, ys, al, gh_ref, gl_ref, tj_ref)
        radial, polar = flux[:slots], flux[slots:]
        if cfg.split == 1:
            up = jnp.where(lower, jnp.concatenate([polar[4:], polar[:4]], axis=0), 0.0)
            after = pltpu.roll(jnp.where(lane < BS, up, polar), wide - BS, 1)
            polar_ref[...] = jnp.zeros_like(polar_ref)
        else:
            after = jnp.where(lane < wide - BS, pltpu.roll(polar, wide - BS, 1), 0.0)
            by_owner(cfg, me, polar_ref, polar)
        azimuthal = dot(
            taken[3 * slots : 4 * slots], source(cfg, first_half(cfg, pieces, 2), al)
        )
        total.append((azimuthal + (after - polar) - radial, radial))
        ys.append(dot(taken[: 3 * slots], source(cfg, first_half(cfg, pieces, 3), al)))
        remap = remapped(cfg, ys, al, mh_ref, ml_ref)
        for c, at in enumerate((1, 2, 0)):
            put(at, al, remap[c * slots : (c + 1) * slots])
    for al in range(cfg.radii):
        bp = total[al][0]
        put(3, al, bp + total[al + 1][1] if al + 1 < cfg.radii else bp)


def finish_kernel(cfg, me_ref, *refs):
    me, group = place(cfg, me_ref)
    n, slots, per = cfg.n, cfg.slots, cfg.per
    pieces = refs[:n]
    mh_ref, ml_ref, taken_ref, rows_ref, halo_ref, polar_ref = refs[n : n + 6]
    outs = refs[n + 6 :]
    rest = cfg.tiles - cfg.per
    for al in range(cfg.radii):
        taken = taken_ref[al]
        ys = [dot(taken, source(cfg, second_half(cfg, pieces, c), al)) for c in range(4)]
        remap = remapped(cfg, ys, al, mh_ref, ml_ref)
        for out, k in zip(outs, cfg.order):
            for c in range(4):
                for t in range(per):
                    out[1 + c, al * per + t] = remap[
                        c * slots + k * SUB : c * slots + (k + 1) * SUB,
                        t * LANES : (t + 1) * LANES,
                    ]
    for out, k in zip(outs, cfg.order):
        owner = jnp.bitwise_xor(me, k)
        out[0] = rows_ref[k, 0]
        out[5:8] = rows_ref[k, 1:4]
        out[7, rest:] = rows_ref[k, 3, rest:] + halo_ref[owner]
        if cfg.split > 1:
            after = polar_ref[owner, 0]
            row = lax.broadcasted_iota(jnp.int32, after.shape, 0)
            lane = lax.broadcasted_iota(jnp.int32, after.shape, 1)
            up = jnp.where(row < 4, jnp.concatenate([after[4:], after[:4]], axis=0), 0.0)
            after = jnp.where(lax.rem(group, cfg.split) == cfg.split - 1, up, after)
            after = pltpu.roll(jnp.where(lane < BS, after, 0.0), LANES - BS, 1)
            out[7, cfg.tiles - 1] = out[7, cfg.tiles - 1] + after


class Sizes:
    def __init__(self, n):
        self.n = n
        self.order = list(range(n // 2, n)) + list(range(n // 2 - 1, -1, -1))
        self.rows = BS * BS // n
        self.tiles = self.rows * BS // LANES
        self.lanes = min(self.rows, BS) * BS
        self.radii = max(1, self.rows // BS)
        self.per = self.lanes // LANES
        self.split = max(1, BS // self.rows)
        self.slots = n * SUB


def shape(*dims, dtype=F32):
    return jax.ShapeDtypeStruct(dims, dtype)


def shards(conserved, face_field, block_ids, int_shift, frac_shift):
    n = lax.axis_size("phi")
    cfg = Sizes(n)
    count = lax.axis_size("tile") * n
    tiles, per = cfg.tiles, cfg.per
    smem = pl.BlockSpec(memory_space=pltpu.SMEM)
    vmem = pl.BlockSpec(memory_space=pltpu.VMEM)
    hbm = pl.BlockSpec(memory_space=pltpu.MemorySpace.HBM)

    def grant(mib):
        return pltpu.CompilerParams(vmem_limit_bytes=min(mib, 48) * 2**20)

    me = lax.axis_index(("tile", "phi")).astype(jnp.int32).reshape(1)

    def holder(group):
        tile, place = divmod(group, n)
        return tile * n + (place ^ (tile % 2 * (n - 1)))

    def tiled(x):
        return x.reshape(SUB, x.shape[1], n * tiles, LANES).transpose(1, 2, 0, 3)

    def untiled(x):
        return x.transpose(2, 0, 1, 3).reshape(SUB, x.shape[0], n * tiles * LANES)

    half = n // 2

    def exchange(pieces, order):
        return [
            lax.ppermute(piece, "phi", [(s, s ^ k) for s in range(n)]) if k else piece
            for piece, k in zip(pieces, order)
        ]

    def in_hbm(x):
        return pltpu.with_memory_space_constraint(x, pltpu.MemorySpace.HBM)

    packed = pl.pallas_call(
        functools.partial(pack_kernel, cfg),
        out_shape=[shape(4 * tiles + 1, SUB, LANES)] * half
        + [shape(8 * tiles + 1, SUB, LANES)] * half
        + [shape(4 * tiles, SUB, LANES)] * half,
        in_specs=[smem] + [hbm] * 3,
        out_specs=[vmem] * (n + half),
        scratch_shapes=[
            pltpu.VMEM((8, n * tiles, SUB, LANES), F32),
            pltpu.SMEM((SUB,), jnp.int32),
            pltpu.SemaphoreType.DMA((9,)),
        ],
        compiler_params=grant(3),
        name="pack",
    )(me, in_hbm(block_ids), in_hbm(tiled(face_field)), in_hbm(tiled(conserved)))
    first = exchange(packed[:n], cfg.order)
    far_second = exchange(packed[n:], cfg.order)

    square = shape(cfg.radii, 3, cfg.lanes, cfg.lanes, dtype=BF16)
    mh, ml, gh, gl, tj = pl.pallas_call(
        functools.partial(operators_kernel, cfg),
        out_shape=[square] * 4 + [shape(2, cfg.lanes, cfg.lanes, dtype=BF16)],
        in_specs=[smem] * 3,
        out_specs=[vmem] * 5,
        compiler_params=grant(8),
        name="operators",
    )(me, int_shift, frac_shift)

    owners = shape(n, per, SUB, LANES)
    halo = pl.pallas_call(
        functools.partial(edge_kernel, cfg),
        out_shape=owners,
        in_specs=[smem] * 2 + [vmem] * (n + 3),
        out_specs=vmem,
        compiler_params=grant(2 * n),
        name="edge",
    )(me, int_shift, *first, gh, gl, tj)
    halo = lax.ppermute(
        halo,
        ("tile", "phi"),
        [(holder(s), holder(s - cfg.split)) for s in range(cfg.split, count)],
    )
    rows, taken, polar = pl.pallas_call(
        functools.partial(fields_kernel, cfg),
        out_shape=[
            shape(n, 4, tiles, SUB, LANES),
            shape(cfg.radii, 3 * cfg.slots, 3 * cfg.slots, dtype=BF16),
            owners if cfg.split > 1 else shape(1, 1, SUB, LANES),
        ],
        in_specs=[smem] * 2 + [vmem] * (n + 5),
        out_specs=[vmem] * 3,
        compiler_params=grant(2 * n),
        name="fields",
    )(me, int_shift, *first, mh, ml, gh, gl, tj)
    if cfg.split > 1:
        polar = lax.ppermute(
            polar,
            ("tile", "phi"),
            [
                (holder(s), holder(s - 1 if s % cfg.split else s + cfg.split - 1))
                for s in range(count)
            ],
        )
    done = pl.pallas_call(
        functools.partial(finish_kernel, cfg),
        out_shape=[shape(8, tiles, SUB, LANES)] * n,
        in_specs=[smem] + [vmem] * (n + 6),
        out_specs=[vmem] * n,
        compiler_params=grant(2 * n),
        name="finish",
    )(me, *far_second, *first[half:], mh, ml, taken, rows, halo, polar)
    conserved_out, field_out = pl.pallas_call(
        functools.partial(unpack_kernel, cfg),
        out_shape=[shape(5, n * tiles, SUB, LANES), shape(3, n * tiles, SUB, LANES)],
        in_specs=[smem] + [vmem] * n,
        out_specs=[hbm] * 2,
        scratch_shapes=[pltpu.SemaphoreType.DMA((n, 2))],
        compiler_params=grant(2),
        name="unpack",
    )(me, *exchange(done, cfg.order))
    return untiled(conserved_out), untiled(field_out)


def solution(mesh):
    return jax.shard_map(
        shards,
        mesh=mesh,
        in_specs=(
            P(("tile", "phi"), None, None),
            P(("tile", "phi"), None, None),
            P(("tile", "phi")),
            P("tile"),
            P("tile"),
        ),
        out_specs=(P(("tile", "phi"), None, None), P(("tile", "phi"), None, None)),
        check_vma=False,
    )
```

```python
import functools

import jax
import jax.numpy as jnp
from jax import lax
from jax.experimental import pallas as pl
from jax.experimental.pallas import tpu as pltpu
from jax.sharding import PartitionSpec as P

BS = 16
TB = 2
PB = 4
LANES = 128
SUB = 8
NODES = (-3, -2, -1, 0, 1, 2, 3)
F32 = jnp.float32
BF16 = jnp.bfloat16


def halves(x):
    hi = x.astype(BF16)
    return hi, (x - hi.astype(F32)).astype(BF16)


def thirds(x):
    hi = x.astype(BF16)
    rest = x - hi.astype(F32)
    mid = rest.astype(BF16)
    return hi, mid, (rest - mid.astype(F32)).astype(BF16)


def dot(a, b):
    return jnp.dot(a, b, preferred_element_type=F32)


def nearest_blocks(shift):
    whole = (shift + BS // 2) // BS
    return whole, shift - whole * BS


def place(cfg, me_ref):
    phi, tile = lax.rem(me_ref[0], cfg.n), lax.div(me_ref[0], cfg.n)
    return phi, jnp.bitwise_xor(phi, lax.rem(tile, 2) * (cfg.n - 1))


def start_all(copies):
    for copy in copies:
        copy.start()
    return copies


def wait_all(copies):
    for copy in copies:
        copy.wait()


def pack_kernel(cfg, me_ref, ids_ref, face_ref, conserved_ref, *refs):
    me, group = place(cfg, me_ref)
    n, tiles = cfg.n, cfg.tiles
    half = n // 2
    outs, (all_ref, id_ref, sem) = refs[: n + half], refs[n + half :]
    copies = [pltpu.make_async_copy(ids_ref, id_ref, sem.at[8])]
    for c in range(8):
        from_ref = face_ref.at[c] if c < 3 else conserved_ref.at[c - 3]
        copies.append(pltpu.make_async_copy(from_ref, all_ref.at[c], sem.at[c]))
    start_all(copies)
    dests = [jnp.bitwise_xor(group, k) * tiles for k in cfg.order]
    copies[0].wait()
    rows = lax.broadcasted_iota(jnp.int32, (SUB, LANES), 0)
    ids = jnp.zeros((SUB, LANES), jnp.int32)
    for slot in range(SUB):
        ids = jnp.where(rows == slot, id_ref[slot], ids)
    for out in outs[:n]:
        out[4 * tiles] = ids.astype(F32)
    for c in range(8):
        copies[1 + c].wait()
        for j, dest in enumerate(dests):
            out, at = outs[j], c * tiles + (c >= 4)
            if c >= 4 and j < half:
                out, at = outs[n + j], (c - 4) * tiles
            out[at : at + tiles] = all_ref[c, pl.ds(dest, tiles)]


def unpack_kernel(cfg, orders, me_ref, *refs):
    me, group = place(cfg, me_ref)
    pieces, (conserved_ref, field_ref, sem) = refs[: len(orders)], refs[-3:]
    copies = []
    for i, (piece, k) in enumerate(zip(pieces, orders)):
        at = pl.ds(jnp.bitwise_xor(group, k) * cfg.tiles, cfg.tiles)
        for j, (first, count, out) in enumerate(((0, 5, conserved_ref), (5, 3, field_ref))):
            copies.append(
                pltpu.make_async_copy(
                    piece.at[pl.ds(first, count)], out.at[:, at], sem.at[i, j]
                )
            )
    wait_all(start_all(copies))


def operators_kernel(cfg, me_ref, shift_ref, frac_ref, *refs):
    me, group = place(cfg, me_ref)
    mh_ref, ml_ref, gh_ref, gl_ref, tj_ref, whole_ref = refs
    size = cfg.lanes
    first = (group * cfg.rows) // BS
    row = lax.broadcasted_iota(jnp.int32, (size, size), 0)
    col = lax.broadcasted_iota(jnp.int32, (size, size), 1)
    same = (row // BS) == (col // BS)
    e_in = lax.broadcasted_iota(jnp.int32, (BS, size), 0)
    e_out = lax.broadcasted_iota(jnp.int32, (BS, size), 1) % BS
    zero = jnp.zeros((BS, size), F32)

    def spread(pattern):
        return jnp.where(same, jnp.concatenate([pattern] * (size // BS), axis=0), 0.0)

    tj_ref[0] = spread(jnp.where(e_in < e_out, 1.0, zero)).astype(BF16)
    tj_ref[1] = spread(zero + 1.0).astype(BF16)
    for al in range(cfg.radii):
        whole, rest = nearest_blocks(shift_ref[first + al])
        whole_ref[al] = jnp.full((SUB, 3 * cfg.slots), whole, jnp.int32)
        position = -jnp.full((1, size), frac_ref[first + al], F32)
        lagrange = []
        for a in NODES:
            product = jnp.ones_like(position)
            for b in NODES:
                if b != a:
                    product = product * ((position - float(b)) * (1.0 / float(a - b)))
            lagrange.append(product)
        weights = []
        for m in range(-3, 3):
            total = jnp.zeros_like(position)
            if m >= 0:
                for a in range(m + 1, 4):
                    total = total - lagrange[a + 3]
            else:
                for a in range(-3, m + 1):
                    total = total + lagrange[a + 3]
            weights.append(total)
        for d in range(3):
            at = e_in + BS * (d - 1)
            tap = at - e_out + rest
            remap, flux = zero, zero
            for a in NODES:
                hit = tap == a
                remap = jnp.where(hit, lagrange[a + 3], remap)
                if a < 3:
                    flux = jnp.where(hit, weights[a + 3], flux)
            flux = flux - jnp.where(at < e_out - rest, 1.0, zero)
            for value, high_ref, low_ref in ((remap, mh_ref, ml_ref), (flux, gh_ref, gl_ref)):
                high = value.astype(BF16).astype(F32)
                high_ref[al, d] = spread(high).astype(BF16)
                low_ref[al, d] = spread(value - high).astype(BF16)


def gather_matrix(cfg, me, ids, whole):
    shape = (cfg.slots, 3 * cfg.slots)
    target = lax.broadcasted_iota(jnp.int32, shape, 0)
    owner = jnp.bitwise_xor(target >> 3, me)
    q_out, b_out = owner * PB + (target & 3), (target >> 2) & 1
    v = jnp.broadcast_to(ids, shape)
    q_in, b_in = (v >> 3) * PB + (v & 3), (v >> 2) & 1
    same = b_in == b_out
    cells = cfg.n * PB
    rows = []
    for d in (-1, 0, 1):
        hit = same & (((q_out - whole + d - q_in + 2 * cells) & (cells - 1)) == 0)
        rows.append(jnp.where(hit, 1.0, 0.0))
    rows.append(jnp.where(same & (q_in == q_out), 1.0, 0.0))
    back = (q_out - 1 - q_in + cells) & (cells - 1)
    count = jnp.where(back <= whole, 1.0, 0.0) + jnp.where(back + cells <= whole, 1.0, 0.0)
    rows.append(jnp.where(same, count, 0.0))
    return rows


def three_dots(high, low, mh, ml):
    rows = high.shape[0]
    both = dot(jnp.concatenate([high, low], axis=0), mh)
    return both[:rows] + both[rows:] + dot(high, ml)


def source(cfg, tiles_of, al):
    x = jnp.concatenate(
        [
            jnp.concatenate([p[at + al * cfg.per + t] for p, at in tiles_of], axis=0)
            for t in range(cfg.per)
        ],
        axis=1,
    )
    return jnp.concatenate(thirds(x), axis=0)


def first_half(cfg, pieces, c):
    return [(p, c * cfg.tiles) for p in pieces]


def second_half(cfg, pieces, c):
    near = [0] * (cfg.n // 2) + [4 * cfg.tiles + 1] * (cfg.n // 2)
    return [(p, at + c * cfg.tiles) for p, at in zip(pieces, near)]


def numbers(cfg, pieces):
    ids = jnp.concatenate([p[4 * cfg.tiles] for p in pieces] * 3, axis=0)
    return jnp.transpose(ids)[0:1].astype(jnp.int32)


def whole_fluxes(cfg, ys, al, gh_ref, gl_ref, tj_ref):
    slots = cfg.slots
    part = [
        halves(jnp.concatenate([y[j * slots : (j + 1) * slots] for y in ys], axis=0))
        for j in range(5)
    ]
    flux = 0.0
    for d in range(3):
        flux = flux + three_dots(*part[d], gh_ref[al, d], gl_ref[al, d])
    for j in range(2):
        both = dot(jnp.concatenate(part[3 + j], axis=0), tj_ref[j])
        rows = both.shape[0] // 2
        flux = flux + (both[:rows] + both[rows:])
    return flux


def by_owner(cfg, me, out_ref, value):
    for k in range(cfg.n):
        for t in range(cfg.per):
            out_ref[jnp.bitwise_xor(me, k), t] = value[
                k * SUB : (k + 1) * SUB, t * LANES : (t + 1) * LANES
            ]


def edge_kernel(cfg, me_ref, *refs):
    me, group = place(cfg, me_ref)
    pieces, (gh_ref, gl_ref, tj_ref, whole_ref, halo_ref) = refs[: cfg.n], refs[cfg.n :]
    taken = gather_matrix(cfg, me, numbers(cfg, pieces), whole_ref[0, 0:1])
    y = dot(jnp.concatenate(taken, axis=0).astype(BF16), source(cfg, first_half(cfg, pieces, 0), 0))
    by_owner(cfg, me, halo_ref, whole_fluxes(cfg, [y], 0, gh_ref, gl_ref, tj_ref))


def remapped(count, ys, al, mh_ref, ml_ref):
    total = 0.0
    for d in range(3):
        at = slice(d * count, (d + 1) * count)
        high, low = halves(jnp.concatenate([y[at] for y in ys], axis=0))
        total = total + three_dots(high, low, mh_ref[al, d], ml_ref[al, d])
    return total


def fields_kernel(cfg, me_ref, *refs):
    me, group = place(cfg, me_ref)
    n, slots, wide, per = cfg.n, cfg.slots, cfg.lanes, cfg.per
    pieces = refs[:n]
    mh_ref, ml_ref, gh_ref, gl_ref, tj_ref, whole_ref, out_ref, taken_ref, polar_ref = refs[n:]
    ids = numbers(cfg, pieces)

    def put(c, al, value):
        for k in range(n):
            for t in range(per):
                out_ref[k, c, al * per + t] = value[
                    k * SUB : (k + 1) * SUB, t * LANES : (t + 1) * LANES
                ]

    lane = lax.broadcasted_iota(jnp.int32, (slots, wide), 1)
    lower = (lax.broadcasted_iota(jnp.int32, (slots, wide), 0) >> 2) & 1 == 0
    total = []
    for al in range(cfg.radii):
        taken = gather_matrix(cfg, me, ids, whole_ref[al, 0:1])
        taken = jnp.concatenate(taken, axis=0).astype(BF16)
        taken_ref[al] = taken[: 3 * slots]
        ys = [dot(taken, source(cfg, first_half(cfg, pieces, c), al)) for c in range(2)]
        flux = whole_fluxes(cfg, ys, al, gh_ref, gl_ref, tj_ref)
        radial, polar = flux[:slots], flux[slots:]
        if cfg.split == 1:
            up = jnp.where(lower, jnp.concatenate([polar[4:], polar[:4]], axis=0), 0.0)
            after = pltpu.roll(jnp.where(lane < BS, up, polar), wide - BS, 1)
            polar_ref[...] = jnp.zeros_like(polar_ref)
        else:
            after = jnp.where(lane < wide - BS, pltpu.roll(polar, wide - BS, 1), 0.0)
            by_owner(cfg, me, polar_ref, polar)
        azimuthal = dot(
            taken[3 * slots : 4 * slots], source(cfg, first_half(cfg, pieces, 2), al)
        )
        total.append((azimuthal + (after - polar) - radial, radial))
        ys.append(dot(taken[: 3 * slots], source(cfg, first_half(cfg, pieces, 3), al)))
        remap = remapped(slots, ys, al, mh_ref, ml_ref)
        for c, at in enumerate((1, 2, 0)):
            put(at, al, remap[c * slots : (c + 1) * slots])
    for al in range(cfg.radii):
        bp = total[al][0]
        put(3, al, bp + total[al + 1][1] if al + 1 < cfg.radii else bp)


def finish_kernel(cfg, orders, me_ref, *refs):
    me, group = place(cfg, me_ref)
    n, slots, per = cfg.n, cfg.slots, cfg.per
    pieces = refs[:n]
    mh_ref, ml_ref, taken_ref, rows_ref, halo_ref, polar_ref = refs[n : n + 6]
    outs, mark_ref = refs[-len(orders) - 1 : -1], refs[-1]
    mark_ref[...] = jnp.zeros_like(mark_ref)
    rest = cfg.tiles - per
    low, count = min(orders) * SUB, len(orders) * SUB
    for al in range(cfg.radii):
        taken = jnp.concatenate(
            [taken_ref[al, d * slots + low : d * slots + low + count] for d in range(3)], axis=0
        )
        ys = [dot(taken, source(cfg, second_half(cfg, pieces, c), al)) for c in range(4)]
        remap = remapped(count, ys, al, mh_ref, ml_ref)
        for out, k in zip(outs, orders):
            for c in range(4):
                for t in range(per):
                    at = c * count + k * SUB - low
                    out[1 + c, al * per + t] = remap[
                        at : at + SUB, t * LANES : (t + 1) * LANES
                    ]
    for out, k in zip(outs, orders):
        owner = jnp.bitwise_xor(me, k)
        out[0] = rows_ref[k, 0]
        out[5:8] = rows_ref[k, 1:4]
        out[7, rest:] = rows_ref[k, 3, rest:] + halo_ref[owner]
        if cfg.split > 1:
            after = polar_ref[owner, 0]
            row = lax.broadcasted_iota(jnp.int32, after.shape, 0)
            lane = lax.broadcasted_iota(jnp.int32, after.shape, 1)
            up = jnp.where(row < 4, jnp.concatenate([after[4:], after[:4]], axis=0), 0.0)
            after = jnp.where(lax.rem(group, cfg.split) == cfg.split - 1, up, after)
            after = pltpu.roll(jnp.where(lane < BS, after, 0.0), LANES - BS, 1)
            out[7, cfg.tiles - 1] = out[7, cfg.tiles - 1] + after


class Sizes:
    def __init__(self, n):
        self.n = n
        self.order = list(range(n // 2, n)) + list(range(n // 2 - 1, -1, -1))
        self.rows = BS * BS // n
        self.tiles = self.rows * BS // LANES
        self.lanes = min(self.rows, BS) * BS
        self.radii = max(1, self.rows // BS)
        self.last = self.order[n // 4 : n // 2]
        self.per = self.lanes // LANES
        self.split = max(1, BS // self.rows)
        self.slots = n * SUB


def shape(*dims, dtype=F32):
    return jax.ShapeDtypeStruct(dims, dtype)


def shards(conserved, face_field, block_ids, int_shift, frac_shift):
    n = lax.axis_size("phi")
    cfg = Sizes(n)
    count = lax.axis_size("tile") * n
    tiles, per = cfg.tiles, cfg.per
    smem = pl.BlockSpec(memory_space=pltpu.SMEM)
    vmem = pl.BlockSpec(memory_space=pltpu.VMEM)
    hbm = pl.BlockSpec(memory_space=pltpu.MemorySpace.HBM)

    def grant(mib):
        return pltpu.CompilerParams(vmem_limit_bytes=min(mib, 48) * 2**20)

    me = lax.axis_index(("tile", "phi")).astype(jnp.int32).reshape(1)

    def holder(group):
        tile, place = divmod(group, n)
        return tile * n + (place ^ (tile % 2 * (n - 1)))

    def tiled(x):
        return x.reshape(SUB, x.shape[1], n * tiles, LANES).transpose(1, 2, 0, 3)

    def untiled(x):
        return x.transpose(2, 0, 1, 3).reshape(SUB, x.shape[0], n * tiles * LANES)

    half = n // 2

    def exchange(pieces, order):
        return [
            lax.ppermute(piece, "phi", [(s, s ^ k) for s in range(n)]) if k else piece
            for piece, k in zip(pieces, order)
        ]

    def in_hbm(x):
        return pltpu.with_memory_space_constraint(x, pltpu.MemorySpace.HBM)

    packed = pl.pallas_call(
        functools.partial(pack_kernel, cfg),
        out_shape=[shape(4 * tiles + 1, SUB, LANES)] * half
        + [shape(8 * tiles + 1, SUB, LANES)] * half
        + [shape(4 * tiles, SUB, LANES)] * half,
        in_specs=[smem] + [hbm] * 3,
        out_specs=[vmem] * (n + half),
        scratch_shapes=[
            pltpu.VMEM((8, n * tiles, SUB, LANES), F32),
            pltpu.SMEM((SUB,), jnp.int32),
            pltpu.SemaphoreType.DMA((9,)),
        ],
        compiler_params=grant(3),
        name="pack",
    )(me, in_hbm(block_ids), in_hbm(tiled(face_field)), in_hbm(tiled(conserved)))
    first = exchange(packed[:n], cfg.order)
    far_second = exchange(packed[n:], cfg.order)

    square = shape(cfg.radii, 3, cfg.lanes, cfg.lanes, dtype=BF16)
    mh, ml, gh, gl, tj, whole = pl.pallas_call(
        functools.partial(operators_kernel, cfg),
        out_shape=[square] * 4
        + [
            shape(2, cfg.lanes, cfg.lanes, dtype=BF16),
            shape(cfg.radii, SUB, 3 * cfg.slots, dtype=jnp.int32),
        ],
        in_specs=[smem] * 3,
        out_specs=[vmem] * 6,
        compiler_params=grant(8),
        name="operators",
    )(me, int_shift, frac_shift)

    owners = shape(n, per, SUB, LANES)
    halo = pl.pallas_call(
        functools.partial(edge_kernel, cfg),
        out_shape=owners,
        in_specs=[smem] + [vmem] * (n + 4),
        out_specs=vmem,
        compiler_params=grant(2 * n),
        name="edge",
    )(me, *first, gh, gl, tj, whole)
    halo = lax.ppermute(
        halo,
        ("tile", "phi"),
        [(holder(s), holder(s - cfg.split)) for s in range(cfg.split, count)],
    )
    rows, taken, polar = pl.pallas_call(
        functools.partial(fields_kernel, cfg),
        out_shape=[
            shape(n, 4, tiles, SUB, LANES),
            shape(cfg.radii, 3 * cfg.slots, 3 * cfg.slots, dtype=BF16),
            owners if cfg.split > 1 else shape(1, 1, SUB, LANES),
        ],
        in_specs=[smem] + [vmem] * (n + 6),
        out_specs=[vmem] * 3,
        compiler_params=grant(2 * n),
        name="fields",
    )(me, *first, mh, ml, gh, gl, tj, whole)
    if cfg.split > 1:
        polar = lax.ppermute(
            polar,
            ("tile", "phi"),
            [
                (holder(s), holder(s - 1 if s % cfg.split else s + cfg.split - 1))
                for s in range(count)
            ],
        )
    done, token = [], []
    for name, orders in (("finish_far", cfg.order[:half]), ("finish_near", cfg.order[half:])):
        *pieces, mark = pl.pallas_call(
            functools.partial(finish_kernel, cfg, orders),
            out_shape=[shape(8, tiles, SUB, LANES)] * half + [shape(SUB, LANES)],
            in_specs=[smem] + [vmem] * (n + 6 + len(token)),
            out_specs=[vmem] * (half + 1),
            compiler_params=grant(2 * n),
            name=name,
        )(me, *far_second, *first[half:], mh, ml, taken, rows, halo, polar, *token)
        done, token = done + pieces, [mark]
    back = exchange(done, cfg.order)
    outs = ()
    for name, late in (("unpack_early", False), ("unpack_late", True)):
        orders = [k for k in cfg.order if (k in cfg.last) == late]
        outs = pl.pallas_call(
            functools.partial(unpack_kernel, cfg, orders),
            out_shape=[shape(5, n * tiles, SUB, LANES), shape(3, n * tiles, SUB, LANES)],
            in_specs=[smem] + [vmem] * len(orders) + [hbm] * len(outs),
            out_specs=[hbm] * 2,
            input_output_aliases={1 + len(orders) + i: i for i in range(len(outs))},
            scratch_shapes=[pltpu.SemaphoreType.DMA((n, 2))],
            compiler_params=grant(2),
            name=name,
        )(me, *[back[cfg.order.index(k)] for k in orders], *outs)
    conserved_out, field_out = outs
    return untiled(conserved_out), untiled(field_out)


def solution(mesh):
    return jax.shard_map(
        shards,
        mesh=mesh,
        in_specs=(
            P(("tile", "phi"), None, None),
            P(("tile", "phi"), None, None),
            P(("tile", "phi")),
            P("tile"),
            P("tile"),
        ),
        out_specs=(P(("tile", "phi"), None, None), P(("tile", "phi"), None, None)),
        check_vma=False,
    )
```

```python
import functools

import jax
import jax.numpy as jnp
from jax import lax
from jax.experimental import pallas as pl
from jax.experimental.pallas import tpu as pltpu
from jax.sharding import PartitionSpec as P

BS = 16
TB = 2
PB = 4
LANES = 128
SUB = 8
NODES = (-3, -2, -1, 0, 1, 2, 3)
F32 = jnp.float32
BF16 = jnp.bfloat16


def halves(x):
    hi = x.astype(BF16)
    return hi, (x - hi.astype(F32)).astype(BF16)


def thirds(x):
    hi = x.astype(BF16)
    rest = x - hi.astype(F32)
    mid = rest.astype(BF16)
    return hi, mid, (rest - mid.astype(F32)).astype(BF16)


def dot(a, b):
    return jnp.dot(a, b, preferred_element_type=F32)


def nearest_blocks(shift):
    whole = (shift + BS // 2) // BS
    return whole, shift - whole * BS


def place(cfg, me_ref):
    phi, tile = lax.rem(me_ref[0], cfg.n), lax.div(me_ref[0], cfg.n)
    return phi, jnp.bitwise_xor(phi, lax.rem(tile, 2) * (cfg.n - 1))


def start_all(copies):
    for copy in copies:
        copy.start()
    return copies


def wait_all(copies):
    for copy in copies:
        copy.wait()


def pack_kernel(cfg, late, me_ref, ids_ref, face_ref, conserved_ref, *refs):
    me, group = place(cfg, me_ref)
    n, tiles = cfg.n, cfg.tiles
    half = n // 2
    all_ref, id_ref, sem = refs[-3:]
    outs = refs[1:-3] if late else refs[:half]
    copies = [pltpu.make_async_copy(ids_ref, id_ref, sem.at[8])]
    for c in range(8 if late else 4):
        from_ref = face_ref.at[c] if c < 3 else conserved_ref.at[c - 3]
        copies.append(pltpu.make_async_copy(from_ref, all_ref.at[c], sem.at[c]))
    start_all(copies)
    dests = [jnp.bitwise_xor(group, k) * tiles for k in cfg.order]
    copies[0].wait()
    rows = lax.broadcasted_iota(jnp.int32, (SUB, LANES), 0)
    ids = jnp.zeros((SUB, LANES), jnp.int32)
    for slot in range(SUB):
        ids = jnp.where(rows == slot, id_ref[slot], ids)
    for out in outs[:half]:
        out[4 * tiles] = ids.astype(F32)
    if not late:
        refs[half][...] = jnp.zeros((SUB, LANES), F32)
    for c, copy in enumerate(copies[1:]):
        copy.wait()
        for j in range(half):
            at = c * tiles + (c >= 4)
            dest = dests[half + j] if late else dests[j]
            outs[j][at : at + tiles] = all_ref[c, pl.ds(dest, tiles)]
            if late and c >= 4:
                at = (c - 4) * tiles
                outs[half + j][at : at + tiles] = all_ref[c, pl.ds(dests[j], tiles)]


def unpack_kernel(cfg, orders, me_ref, *refs):
    me, group = place(cfg, me_ref)
    pieces, (conserved_ref, field_ref, sem) = refs[: len(orders)], refs[-3:]
    copies = []
    for i, (piece, k) in enumerate(zip(pieces, orders)):
        at = pl.ds(jnp.bitwise_xor(group, k) * cfg.tiles, cfg.tiles)
        for j, (first, count, out) in enumerate(((0, 5, conserved_ref), (5, 3, field_ref))):
            copies.append(
                pltpu.make_async_copy(
                    piece.at[pl.ds(first, count)], out.at[:, at], sem.at[i, j]
                )
            )
    wait_all(start_all(copies))


def operators_kernel(cfg, me_ref, shift_ref, frac_ref, *refs):
    me, group = place(cfg, me_ref)
    mh_ref, ml_ref, gh_ref, gl_ref, tj_ref, whole_ref, side_ref = refs
    size = cfg.lanes
    first = (group * cfg.rows) // BS
    row = lax.broadcasted_iota(jnp.int32, (size, size), 0)
    col = lax.broadcasted_iota(jnp.int32, (size, size), 1)
    same = (row // BS) == (col // BS)
    e_in = lax.broadcasted_iota(jnp.int32, (BS, size), 0)
    e_out = lax.broadcasted_iota(jnp.int32, (BS, size), 1) % BS
    zero = jnp.zeros((BS, size), F32)

    def spread(pattern):
        return jnp.where(same, jnp.concatenate([pattern] * (size // BS), axis=0), 0.0)

    def store(value, high_ref, low_ref, al, j):
        high = value.astype(BF16).astype(F32)
        high_ref[al, j] = spread(high).astype(BF16)
        low_ref[al, j] = spread(value - high).astype(BF16)

    tj_ref[0] = spread(jnp.where(e_in < e_out, 1.0, zero)).astype(BF16)
    tj_ref[1] = spread(zero + 1.0).astype(BF16)
    for al in range(cfg.radii):
        whole, rest = nearest_blocks(shift_ref[first + al])
        whole_ref[al] = jnp.full((SUB, 3 * cfg.slots), whole, jnp.int32)
        position = -jnp.full((1, size), frac_ref[first + al], F32)
        lagrange = []
        for a in NODES:
            product = jnp.ones_like(position)
            for b in NODES:
                if b != a:
                    product = product * ((position - float(b)) * (1.0 / float(a - b)))
            lagrange.append(product)
        weights = []
        for m in range(-3, 3):
            total = jnp.zeros_like(position)
            if m >= 0:
                for a in range(m + 1, 4):
                    total = total - lagrange[a + 3]
            else:
                for a in range(-3, m + 1):
                    total = total + lagrange[a + 3]
            weights.append(total)
        before = lax.broadcasted_iota(jnp.int32, (SUB, size), 1) % BS >= BS // 2 - rest
        side_ref[al] = before.astype(jnp.int32)
        beside = zero
        for d in range(3):
            at = e_in + BS * (d - 1)
            tap = at - e_out + rest
            remap, flux = zero, zero
            for a in NODES:
                hit = tap == a
                remap = jnp.where(hit, lagrange[a + 3], remap)
                if a < 3:
                    flux = jnp.where(hit, weights[a + 3], flux)
            flux = flux - jnp.where(at < e_out - rest, 1.0, zero)
            store(flux, gh_ref, gl_ref, al, d)
            if d == 1:
                store(remap, mh_ref, ml_ref, al, 0)
            else:
                beside = beside + remap
        store(beside, mh_ref, ml_ref, al, 1)


def gather_matrix(cfg, me, ids, whole):
    shape = (cfg.slots, 3 * cfg.slots)
    target = lax.broadcasted_iota(jnp.int32, shape, 0)
    owner = jnp.bitwise_xor(target >> 3, me)
    q_out, b_out = owner * PB + (target & 3), (target >> 2) & 1
    v = jnp.broadcast_to(ids, shape)
    q_in, b_in = (v >> 3) * PB + (v & 3), (v >> 2) & 1
    same = b_in == b_out
    cells = cfg.n * PB
    rows = []
    for d in (-1, 0, 1):
        hit = same & (((q_out - whole + d - q_in + 2 * cells) & (cells - 1)) == 0)
        rows.append(jnp.where(hit, 1.0, 0.0))
    rows.append(jnp.where(same & (q_in == q_out), 1.0, 0.0))
    back = (q_out - 1 - q_in + cells) & (cells - 1)
    count = jnp.where(back <= whole, 1.0, 0.0) + jnp.where(back + cells <= whole, 1.0, 0.0)
    rows.append(jnp.where(same, count, 0.0))
    return rows


def three_dots(high, low, mh, ml):
    rows = high.shape[0]
    both = dot(jnp.concatenate([high, low], axis=0), mh)
    return both[:rows] + both[rows:] + dot(high, ml)


def source(cfg, tiles_of, al):
    x = jnp.concatenate(
        [
            jnp.concatenate([p[at + al * cfg.per + t] for p, at in tiles_of], axis=0)
            for t in range(cfg.per)
        ],
        axis=1,
    )
    return jnp.concatenate(thirds(x), axis=0)


def first_half(cfg, pieces, c):
    return [(p, c * cfg.tiles) for p in pieces]


def second_half(cfg, pieces, c):
    near = [0] * (cfg.n // 2) + [4 * cfg.tiles + 1] * (cfg.n // 2)
    return [(p, at + c * cfg.tiles) for p, at in zip(pieces, near)]


def numbers(cfg, pieces):
    ids = jnp.concatenate([p[4 * cfg.tiles] for p in pieces] * 3, axis=0)
    return jnp.transpose(ids)[0:1].astype(jnp.int32)


def whole_fluxes(cfg, ys, al, gh_ref, gl_ref, tj_ref):
    slots = cfg.slots
    part = [
        halves(jnp.concatenate([y[j * slots : (j + 1) * slots] for y in ys], axis=0))
        for j in range(5)
    ]
    flux = 0.0
    for d in range(3):
        flux = flux + three_dots(*part[d], gh_ref[al, d], gl_ref[al, d])
    for j in range(2):
        both = dot(jnp.concatenate(part[3 + j], axis=0), tj_ref[j])
        rows = both.shape[0] // 2
        flux = flux + (both[:rows] + both[rows:])
    return flux


def by_owner(cfg, me, out_ref, value):
    for k in range(cfg.n):
        for t in range(cfg.per):
            out_ref[jnp.bitwise_xor(me, k), t] = value[
                k * SUB : (k + 1) * SUB, t * LANES : (t + 1) * LANES
            ]


def edge_kernel(cfg, me_ref, *refs):
    me, group = place(cfg, me_ref)
    pieces, (gh_ref, gl_ref, tj_ref, whole_ref, halo_ref) = refs[: cfg.n], refs[cfg.n :]
    taken = gather_matrix(cfg, me, numbers(cfg, pieces), whole_ref[0, 0:1])
    y = dot(jnp.concatenate(taken, axis=0).astype(BF16), source(cfg, first_half(cfg, pieces, 0), 0))
    by_owner(cfg, me, halo_ref, whole_fluxes(cfg, [y], 0, gh_ref, gl_ref, tj_ref))


def remapped(count, ys, al, mh_ref, ml_ref, side_ref):
    before = side_ref[al, 0:1] > 0

    def rows(d):
        return jnp.concatenate([y[d * count : (d + 1) * count] for y in ys], axis=0)

    own = three_dots(*halves(rows(1)), mh_ref[al, 0], ml_ref[al, 0])
    beside = halves(jnp.where(before, rows(0), rows(2)))
    return own + three_dots(*beside, mh_ref[al, 1], ml_ref[al, 1])


def fields_kernel(cfg, me_ref, *refs):
    me, group = place(cfg, me_ref)
    n, slots, wide, per = cfg.n, cfg.slots, cfg.lanes, cfg.per
    pieces = refs[:n]
    mh_ref, ml_ref, gh_ref, gl_ref, tj_ref, whole_ref = refs[n : n + 6]
    side_ref, out_ref, taken_ref, polar_ref = refs[n + 6 :]
    ids = numbers(cfg, pieces)

    def put(c, al, value):
        for k in range(n):
            for t in range(per):
                out_ref[k, c, al * per + t] = value[
                    k * SUB : (k + 1) * SUB, t * LANES : (t + 1) * LANES
                ]

    lane = lax.broadcasted_iota(jnp.int32, (slots, wide), 1)
    lower = (lax.broadcasted_iota(jnp.int32, (slots, wide), 0) >> 2) & 1 == 0
    total = []
    for al in range(cfg.radii):
        taken = gather_matrix(cfg, me, ids, whole_ref[al, 0:1])
        taken = jnp.concatenate(taken, axis=0).astype(BF16)
        taken_ref[al] = taken[: 3 * slots]
        ys = [dot(taken, source(cfg, first_half(cfg, pieces, c), al)) for c in range(2)]
        flux = whole_fluxes(cfg, ys, al, gh_ref, gl_ref, tj_ref)
        radial, polar = flux[:slots], flux[slots:]
        if cfg.split == 1:
            up = jnp.where(lower, jnp.concatenate([polar[4:], polar[:4]], axis=0), 0.0)
            after = pltpu.roll(jnp.where(lane < BS, up, polar), wide - BS, 1)
            polar_ref[...] = jnp.zeros_like(polar_ref)
        else:
            after = jnp.where(lane < wide - BS, pltpu.roll(polar, wide - BS, 1), 0.0)
            by_owner(cfg, me, polar_ref, polar)
        azimuthal = dot(
            taken[3 * slots : 4 * slots], source(cfg, first_half(cfg, pieces, 2), al)
        )
        total.append((azimuthal + (after - polar) - radial, radial))
        ys.append(dot(taken[: 3 * slots], source(cfg, first_half(cfg, pieces, 3), al)))
        remap = remapped(slots, ys, al, mh_ref, ml_ref, side_ref)
        for c, at in enumerate((1, 2, 0)):
            put(at, al, remap[c * slots : (c + 1) * slots])
    for al in range(cfg.radii):
        bp = total[al][0]
        put(3, al, bp + total[al + 1][1] if al + 1 < cfg.radii else bp)


def finish_kernel(cfg, orders, me_ref, *refs):
    me, group = place(cfg, me_ref)
    n, slots, per = cfg.n, cfg.slots, cfg.per
    pieces = refs[:n]
    mh_ref, ml_ref, side_ref, taken_ref, rows_ref, halo_ref, polar_ref = refs[n : n + 7]
    outs, mark_ref = refs[-len(orders) - 1 : -1], refs[-1]
    mark_ref[...] = jnp.zeros_like(mark_ref)
    rest = cfg.tiles - per
    low, count = min(orders) * SUB, len(orders) * SUB
    for al in range(cfg.radii):
        taken = jnp.concatenate(
            [taken_ref[al, d * slots + low : d * slots + low + count] for d in range(3)], axis=0
        )
        ys = [dot(taken, source(cfg, second_half(cfg, pieces, c), al)) for c in range(4)]
        remap = remapped(count, ys, al, mh_ref, ml_ref, side_ref)
        for out, k in zip(outs, orders):
            for c in range(4):
                for t in range(per):
                    at = c * count + k * SUB - low
                    out[1 + c, al * per + t] = remap[
                        at : at + SUB, t * LANES : (t + 1) * LANES
                    ]
    for out, k in zip(outs, orders):
        owner = jnp.bitwise_xor(me, k)
        out[0] = rows_ref[k, 0]
        out[5:8] = rows_ref[k, 1:4]
        out[7, rest:] = rows_ref[k, 3, rest:] + halo_ref[owner]
        if cfg.split > 1:
            after = polar_ref[owner, 0]
            row = lax.broadcasted_iota(jnp.int32, after.shape, 0)
            lane = lax.broadcasted_iota(jnp.int32, after.shape, 1)
            up = jnp.where(row < 4, jnp.concatenate([after[4:], after[:4]], axis=0), 0.0)
            after = jnp.where(lax.rem(group, cfg.split) == cfg.split - 1, up, after)
            after = pltpu.roll(jnp.where(lane < BS, after, 0.0), LANES - BS, 1)
            out[7, cfg.tiles - 1] = out[7, cfg.tiles - 1] + after


class Sizes:
    def __init__(self, n):
        self.n = n
        self.order = list(range(n // 2, n)) + list(range(n // 2 - 1, -1, -1))
        self.rows = BS * BS // n
        self.tiles = self.rows * BS // LANES
        self.lanes = min(self.rows, BS) * BS
        self.radii = max(1, self.rows // BS)
        self.last = self.order[n // 4 : n // 2]
        self.per = self.lanes // LANES
        self.split = max(1, BS // self.rows)
        self.slots = n * SUB


def shape(*dims, dtype=F32):
    return jax.ShapeDtypeStruct(dims, dtype)


def shards(conserved, face_field, block_ids, int_shift, frac_shift):
    n = lax.axis_size("phi")
    cfg = Sizes(n)
    count = lax.axis_size("tile") * n
    tiles, per = cfg.tiles, cfg.per
    smem = pl.BlockSpec(memory_space=pltpu.SMEM)
    vmem = pl.BlockSpec(memory_space=pltpu.VMEM)
    hbm = pl.BlockSpec(memory_space=pltpu.MemorySpace.HBM)

    def grant(mib):
        return pltpu.CompilerParams(vmem_limit_bytes=min(mib, 48) * 2**20)

    me = lax.axis_index(("tile", "phi")).astype(jnp.int32).reshape(1)

    def holder(group):
        tile, place = divmod(group, n)
        return tile * n + (place ^ (tile % 2 * (n - 1)))

    def tiled(x):
        return x.reshape(SUB, x.shape[1], n * tiles, LANES).transpose(1, 2, 0, 3)

    def untiled(x):
        return x.transpose(2, 0, 1, 3).reshape(SUB, x.shape[0], n * tiles * LANES)

    half = n // 2

    def exchange(pieces, order):
        return [
            lax.ppermute(piece, "phi", [(s, s ^ k) for s in range(n)]) if k else piece
            for piece, k in zip(pieces, order)
        ]

    def in_hbm(x):
        return pltpu.with_memory_space_constraint(x, pltpu.MemorySpace.HBM)

    sources = (in_hbm(block_ids), in_hbm(tiled(face_field)), in_hbm(tiled(conserved)))
    packed, token = [], []
    for late, shapes in (
        (False, [shape(4 * tiles + 1, SUB, LANES)] * half + [shape(SUB, LANES)]),
        (
            True,
            [shape(8 * tiles + 1, SUB, LANES)] * half + [shape(4 * tiles, SUB, LANES)] * half,
        ),
    ):
        pieces = pl.pallas_call(
            functools.partial(pack_kernel, cfg, late),
            out_shape=shapes,
            in_specs=[smem] + [hbm] * 3 + [vmem] * len(token),
            out_specs=[vmem] * len(shapes),
            scratch_shapes=[
                pltpu.VMEM((8, n * tiles, SUB, LANES), F32),
                pltpu.SMEM((SUB,), jnp.int32),
                pltpu.SemaphoreType.DMA((9,)),
            ],
            compiler_params=grant(3),
            name="pack_late" if late else "pack_early",
        )(me, *sources, *token)
        packed, token = packed + list(pieces[: None if late else half]), list(pieces[half:])[:1]
    first = exchange(packed[:n], cfg.order)
    far_second = exchange(packed[n:], cfg.order)

    def square(count):
        return shape(cfg.radii, count, cfg.lanes, cfg.lanes, dtype=BF16)

    mh, ml, gh, gl, tj, whole, side = pl.pallas_call(
        functools.partial(operators_kernel, cfg),
        out_shape=[square(2)] * 2
        + [square(3)] * 2
        + [
            shape(2, cfg.lanes, cfg.lanes, dtype=BF16),
            shape(cfg.radii, SUB, 3 * cfg.slots, dtype=jnp.int32),
            shape(cfg.radii, SUB, cfg.lanes, dtype=jnp.int32),
        ],
        in_specs=[smem] * 3,
        out_specs=[vmem] * 7,
        compiler_params=grant(8),
        name="operators",
    )(me, int_shift, frac_shift)

    owners = shape(n, per, SUB, LANES)
    halo = pl.pallas_call(
        functools.partial(edge_kernel, cfg),
        out_shape=owners,
        in_specs=[smem] + [vmem] * (n + 4),
        out_specs=vmem,
        compiler_params=grant(2 * n),
        name="edge",
    )(me, *first, gh, gl, tj, whole)
    halo = lax.ppermute(
        halo,
        ("tile", "phi"),
        [(holder(s), holder(s - cfg.split)) for s in range(cfg.split, count)],
    )
    rows, taken, polar = pl.pallas_call(
        functools.partial(fields_kernel, cfg),
        out_shape=[
            shape(n, 4, tiles, SUB, LANES),
            shape(cfg.radii, 3 * cfg.slots, 3 * cfg.slots, dtype=BF16),
            owners if cfg.split > 1 else shape(1, 1, SUB, LANES),
        ],
        in_specs=[smem] + [vmem] * (n + 7),
        out_specs=[vmem] * 3,
        compiler_params=grant(2 * n),
        name="fields",
    )(me, *first, mh, ml, gh, gl, tj, whole, side)
    if cfg.split > 1:
        polar = lax.ppermute(
            polar,
            ("tile", "phi"),
            [
                (holder(s), holder(s - 1 if s % cfg.split else s + cfg.split - 1))
                for s in range(count)
            ],
        )
    done, token = [], []
    for name, orders in (("finish_far", cfg.order[:half]), ("finish_near", cfg.order[half:])):
        *pieces, mark = pl.pallas_call(
            functools.partial(finish_kernel, cfg, orders),
            out_shape=[shape(8, tiles, SUB, LANES)] * half + [shape(SUB, LANES)],
            in_specs=[smem] + [vmem] * (n + 7 + len(token)),
            out_specs=[vmem] * (half + 1),
            compiler_params=grant(2 * n),
            name=name,
        )(me, *far_second, *first[half:], mh, ml, side, taken, rows, halo, polar, *token)
        done, token = done + pieces, [mark]
    back = exchange(done, cfg.order)
    outs = ()
    for name, late in (("unpack_early", False), ("unpack_late", True)):
        orders = [k for k in cfg.order if (k in cfg.last) == late]
        outs = pl.pallas_call(
            functools.partial(unpack_kernel, cfg, orders),
            out_shape=[shape(5, n * tiles, SUB, LANES), shape(3, n * tiles, SUB, LANES)],
            in_specs=[smem] + [vmem] * len(orders) + [hbm] * len(outs),
            out_specs=[hbm] * 2,
            input_output_aliases={1 + len(orders) + i: i for i in range(len(outs))},
            scratch_shapes=[pltpu.SemaphoreType.DMA((n, 2))],
            compiler_params=grant(2),
            name=name,
        )(me, *[back[cfg.order.index(k)] for k in orders], *outs)
    conserved_out, field_out = outs
    return untiled(conserved_out), untiled(field_out)


def solution(mesh):
    return jax.shard_map(
        shards,
        mesh=mesh,
        in_specs=(
            P(("tile", "phi"), None, None),
            P(("tile", "phi"), None, None),
            P(("tile", "phi")),
            P("tile"),
            P("tile"),
        ),
        out_specs=(P(("tile", "phi"), None, None), P(("tile", "phi"), None, None)),
        check_vma=False,
    )
```

```python
import functools

import jax
import jax.numpy as jnp
from jax import lax
from jax.experimental import pallas as pl
from jax.experimental.pallas import tpu as pltpu
from jax.sharding import PartitionSpec as P

BS = 16
TB = 2
PB = 4
LANES = 128
SUB = 8
NODES = (-3, -2, -1, 0, 1, 2, 3)
F32 = jnp.float32
BF16 = jnp.bfloat16


def halves(x):
    hi = x.astype(BF16)
    return hi, (x - hi.astype(F32)).astype(BF16)


def thirds(x):
    hi = x.astype(BF16)
    rest = x - hi.astype(F32)
    mid = rest.astype(BF16)
    return hi, mid, (rest - mid.astype(F32)).astype(BF16)


def dot(a, b):
    return jnp.dot(a, b, preferred_element_type=F32)


def nearest_blocks(shift):
    whole = (shift + BS // 2) // BS
    return whole, shift - whole * BS


def place(cfg, me_ref):
    phi, tile = lax.rem(me_ref[0], cfg.n), lax.div(me_ref[0], cfg.n)
    return phi, jnp.bitwise_xor(phi, lax.rem(tile, 2) * (cfg.n - 1))


def start_all(copies):
    for copy in copies:
        copy.start()
    return copies


def wait_all(copies):
    for copy in copies:
        copy.wait()


def pack_kernel(cfg, late, me_ref, ids_ref, face_ref, conserved_ref, *refs):
    me, group = place(cfg, me_ref)
    n, tiles = cfg.n, cfg.tiles
    half = n // 2
    all_ref, id_ref, sem = refs[-3:]
    outs = refs[1:-3] if late else refs[:half]
    copies = [pltpu.make_async_copy(ids_ref, id_ref, sem.at[8])]
    for c in range(8 if late else 4):
        from_ref = face_ref.at[c] if c < 3 else conserved_ref.at[c - 3]
        copies.append(pltpu.make_async_copy(from_ref, all_ref.at[c], sem.at[c]))
    start_all(copies)
    dests = [jnp.bitwise_xor(group, k) * tiles for k in cfg.order]
    copies[0].wait()
    rows = lax.broadcasted_iota(jnp.int32, (SUB, LANES), 0)
    ids = jnp.zeros((SUB, LANES), jnp.int32)
    for slot in range(SUB):
        ids = jnp.where(rows == slot, id_ref[slot], ids)
    for out in outs[:half]:
        out[4 * tiles] = ids.astype(F32)
    if not late:
        refs[half][...] = jnp.zeros((SUB, LANES), F32)
    for c, copy in enumerate(copies[1:]):
        copy.wait()
        for j in range(half):
            at = c * tiles + (c >= 4)
            dest = dests[half + j] if late else dests[j]
            outs[j][at : at + tiles] = all_ref[c, pl.ds(dest, tiles)]
            if late and c >= 4:
                at = (c - 4) * tiles
                outs[half + j][at : at + tiles] = all_ref[c, pl.ds(dests[j], tiles)]


def unpack_kernel(cfg, orders, me_ref, *refs):
    me, group = place(cfg, me_ref)
    pieces, (conserved_ref, field_ref, sem) = refs[: len(orders)], refs[-3:]
    copies = []
    for i, (piece, k) in enumerate(zip(pieces, orders)):
        at = pl.ds(jnp.bitwise_xor(group, k) * cfg.tiles, cfg.tiles)
        for j, (first, count, out) in enumerate(((0, 5, conserved_ref), (5, 3, field_ref))):
            copies.append(
                pltpu.make_async_copy(
                    piece.at[pl.ds(first, count)], out.at[:, at], sem.at[i, j]
                )
            )
    wait_all(start_all(copies))


def operators_kernel(cfg, me_ref, shift_ref, frac_ref, *refs):
    me, group = place(cfg, me_ref)
    mh_ref, ml_ref, gh_ref, gl_ref, tj_ref, whole_ref, side_ref = refs
    size = cfg.lanes
    first = (group * cfg.rows) // BS
    row = lax.broadcasted_iota(jnp.int32, (size, size), 0)
    col = lax.broadcasted_iota(jnp.int32, (size, size), 1)
    same = (row // BS) == (col // BS)
    e_in = lax.broadcasted_iota(jnp.int32, (BS, size), 0)
    e_out = lax.broadcasted_iota(jnp.int32, (BS, size), 1) % BS
    zero = jnp.zeros((BS, size), F32)

    def spread(pattern):
        return jnp.where(same, jnp.concatenate([pattern] * (size // BS), axis=0), 0.0)

    def store(value, high_ref, low_ref, al, j):
        high = value.astype(BF16).astype(F32)
        high_ref[al, j] = spread(high).astype(BF16)
        low_ref[al, j] = spread(value - high).astype(BF16)

    tj_ref[0] = spread(jnp.where(e_in < e_out, 1.0, zero)).astype(BF16)
    tj_ref[1] = spread(zero + 1.0).astype(BF16)
    for al in range(cfg.radii):
        whole, rest = nearest_blocks(shift_ref[first + al])
        whole_ref[al] = jnp.full((SUB, 3 * cfg.slots), whole, jnp.int32)
        position = -jnp.full((1, size), frac_ref[first + al], F32)
        lagrange = []
        for a in NODES:
            product = jnp.ones_like(position)
            for b in NODES:
                if b != a:
                    product = product * ((position - float(b)) * (1.0 / float(a - b)))
            lagrange.append(product)
        weights = []
        for m in range(-3, 3):
            total = jnp.zeros_like(position)
            if m >= 0:
                for a in range(m + 1, 4):
                    total = total - lagrange[a + 3]
            else:
                for a in range(-3, m + 1):
                    total = total + lagrange[a + 3]
            weights.append(total)
        before = lax.broadcasted_iota(jnp.int32, (SUB, size), 1) % BS >= BS // 2 - rest
        side_ref[al] = before.astype(jnp.int32)
        beside = zero
        for d in range(3):
            at = e_in + BS * (d - 1)
            tap = at - e_out + rest
            remap, flux = zero, zero
            for a in NODES:
                hit = tap == a
                remap = jnp.where(hit, lagrange[a + 3], remap)
                if a < 3:
                    flux = jnp.where(hit, weights[a + 3], flux)
            flux = flux - jnp.where(at < e_out - rest, 1.0, zero)
            store(flux, gh_ref, gl_ref, al, d)
            if d == 1:
                store(remap, mh_ref, ml_ref, al, 0)
            else:
                beside = beside + remap
        store(beside, mh_ref, ml_ref, al, 1)


def gather_matrix(cfg, me, ids, whole):
    shape = (cfg.slots, 3 * cfg.slots)
    target = lax.broadcasted_iota(jnp.int32, shape, 0)
    owner = jnp.bitwise_xor(target >> 3, me)
    q_out, b_out = owner * PB + (target & 3), (target >> 2) & 1
    v = jnp.broadcast_to(ids, shape)
    q_in, b_in = (v >> 3) * PB + (v & 3), (v >> 2) & 1
    same = b_in == b_out
    cells = cfg.n * PB
    rows = []
    for d in (-1, 0, 1):
        hit = same & (((q_out - whole + d - q_in + 2 * cells) & (cells - 1)) == 0)
        rows.append(jnp.where(hit, 1.0, 0.0))
    rows.append(jnp.where(same & (q_in == q_out), 1.0, 0.0))
    back = (q_out - 1 - q_in + cells) & (cells - 1)
    count = jnp.where(back <= whole, 1.0, 0.0) + jnp.where(back + cells <= whole, 1.0, 0.0)
    rows.append(jnp.where(same, count, 0.0))
    return rows


def three_dots(high, low, mh, ml):
    rows = high.shape[0]
    both = dot(jnp.concatenate([high, low], axis=0), mh)
    return both[:rows] + both[rows:] + dot(high, ml)


def source(cfg, tiles_of, al):
    x = jnp.concatenate(
        [
            jnp.concatenate([p[at + al * cfg.per + t] for p, at in tiles_of], axis=0)
            for t in range(cfg.per)
        ],
        axis=1,
    )
    return jnp.concatenate(thirds(x), axis=0)


def first_half(cfg, pieces, c):
    return [(p, c * cfg.tiles) for p in pieces]


def second_half(cfg, pieces, c):
    near = [0] * (cfg.n // 2) + [4 * cfg.tiles + 1] * (cfg.n // 2)
    return [(p, at + c * cfg.tiles) for p, at in zip(pieces, near)]


def numbers(cfg, pieces):
    ids = jnp.concatenate([p[4 * cfg.tiles] for p in pieces] * 3, axis=0)
    return jnp.transpose(ids)[0:1].astype(jnp.int32)


def whole_fluxes(cfg, ys, al, gh_ref, gl_ref, tj_ref):
    slots = cfg.slots
    part = [
        halves(jnp.concatenate([y[j * slots : (j + 1) * slots] for y in ys], axis=0))
        for j in range(5)
    ]
    flux = 0.0
    for d in range(3):
        flux = flux + three_dots(*part[d], gh_ref[al, d], gl_ref[al, d])
    for j in range(2):
        both = dot(jnp.concatenate(part[3 + j], axis=0), tj_ref[j])
        rows = both.shape[0] // 2
        flux = flux + (both[:rows] + both[rows:])
    return flux


def by_owner(cfg, me, out_ref, value):
    for k in range(cfg.n):
        for t in range(cfg.per):
            out_ref[jnp.bitwise_xor(me, k), t] = value[
                k * SUB : (k + 1) * SUB, t * LANES : (t + 1) * LANES
            ]


def edge_kernel(cfg, me_ref, *refs):
    me, group = place(cfg, me_ref)
    pieces, (gh_ref, gl_ref, tj_ref, whole_ref, halo_ref) = refs[: cfg.n], refs[cfg.n :]
    taken = gather_matrix(cfg, me, numbers(cfg, pieces), whole_ref[0, 0:1])
    y = dot(jnp.concatenate(taken, axis=0).astype(BF16), source(cfg, first_half(cfg, pieces, 0), 0))
    by_owner(cfg, me, halo_ref, whole_fluxes(cfg, [y], 0, gh_ref, gl_ref, tj_ref))


def remapped(count, ys, al, mh_ref, ml_ref, side_ref):
    before = side_ref[al, 0:1] > 0

    def rows(d):
        return jnp.concatenate([y[d * count : (d + 1) * count] for y in ys], axis=0)

    own = three_dots(*halves(rows(1)), mh_ref[al, 0], ml_ref[al, 0])
    beside = halves(jnp.where(before, rows(0), rows(2)))
    return own + three_dots(*beside, mh_ref[al, 1], ml_ref[al, 1])


def fields_kernel(cfg, me_ref, *refs):
    me, group = place(cfg, me_ref)
    n, slots, wide, per = cfg.n, cfg.slots, cfg.lanes, cfg.per
    pieces = refs[:n]
    mh_ref, ml_ref, gh_ref, gl_ref, tj_ref, whole_ref = refs[n : n + 6]
    side_ref, out_ref, taken_ref, polar_ref = refs[n + 6 :]
    ids = numbers(cfg, pieces)

    def put(c, al, value):
        for k in range(n):
            for t in range(per):
                out_ref[k, c, al * per + t] = value[
                    k * SUB : (k + 1) * SUB, t * LANES : (t + 1) * LANES
                ]

    lane = lax.broadcasted_iota(jnp.int32, (slots, wide), 1)
    lower = (lax.broadcasted_iota(jnp.int32, (slots, wide), 0) >> 2) & 1 == 0
    total = []
    for al in range(cfg.radii):
        taken = gather_matrix(cfg, me, ids, whole_ref[al, 0:1])
        taken = jnp.concatenate(taken, axis=0).astype(BF16)
        taken_ref[al] = taken[: 3 * slots]
        ys = [dot(taken, source(cfg, first_half(cfg, pieces, c), al)) for c in range(2)]
        flux = whole_fluxes(cfg, ys, al, gh_ref, gl_ref, tj_ref)
        radial, polar = flux[:slots], flux[slots:]
        if cfg.split == 1:
            up = jnp.where(lower, jnp.concatenate([polar[4:], polar[:4]], axis=0), 0.0)
            after = pltpu.roll(jnp.where(lane < BS, up, polar), wide - BS, 1)
            polar_ref[...] = jnp.zeros_like(polar_ref)
        else:
            after = jnp.where(lane < wide - BS, pltpu.roll(polar, wide - BS, 1), 0.0)
            by_owner(cfg, me, polar_ref, polar)
        azimuthal = dot(
            taken[3 * slots : 4 * slots], source(cfg, first_half(cfg, pieces, 2), al)
        )
        total.append((azimuthal + (after - polar) - radial, radial))
        ys.append(dot(taken[: 3 * slots], source(cfg, first_half(cfg, pieces, 3), al)))
        remap = remapped(slots, ys, al, mh_ref, ml_ref, side_ref)
        for c, at in enumerate((1, 2, 0)):
            put(at, al, remap[c * slots : (c + 1) * slots])
    for al in range(cfg.radii):
        bp = total[al][0]
        put(3, al, bp + total[al + 1][1] if al + 1 < cfg.radii else bp)


def finish_kernel(cfg, orders, me_ref, *refs):
    me, group = place(cfg, me_ref)
    n, slots, per = cfg.n, cfg.slots, cfg.per
    pieces = refs[:n]
    mh_ref, ml_ref, side_ref, taken_ref, rows_ref, halo_ref, polar_ref = refs[n : n + 7]
    outs, mark_ref = refs[-len(orders) - 1 : -1], refs[-1]
    mark_ref[...] = jnp.zeros_like(mark_ref)
    rest = cfg.tiles - per
    low, count = min(orders) * SUB, len(orders) * SUB
    for al in range(cfg.radii):
        taken = jnp.concatenate(
            [taken_ref[al, d * slots + low : d * slots + low + count] for d in range(3)], axis=0
        )
        ys = [dot(taken, source(cfg, second_half(cfg, pieces, c), al)) for c in range(4)]
        remap = remapped(count, ys, al, mh_ref, ml_ref, side_ref)
        for out, k in zip(outs, orders):
            for c in range(4):
                for t in range(per):
                    at = c * count + k * SUB - low
                    out[1 + c, al * per + t] = remap[
                        at : at + SUB, t * LANES : (t + 1) * LANES
                    ]
    for out, k in zip(outs, orders):
        owner = jnp.bitwise_xor(me, k)
        out[0] = rows_ref[k, 0]
        out[5:8] = rows_ref[k, 1:4]
        out[7, rest:] = rows_ref[k, 3, rest:] + halo_ref[owner]
        if cfg.split > 1:
            after = polar_ref[owner, 0]
            row = lax.broadcasted_iota(jnp.int32, after.shape, 0)
            lane = lax.broadcasted_iota(jnp.int32, after.shape, 1)
            up = jnp.where(row < 4, jnp.concatenate([after[4:], after[:4]], axis=0), 0.0)
            after = jnp.where(lax.rem(group, cfg.split) == cfg.split - 1, up, after)
            after = pltpu.roll(jnp.where(lane < BS, after, 0.0), LANES - BS, 1)
            out[7, cfg.tiles - 1] = out[7, cfg.tiles - 1] + after


class Sizes:
    def __init__(self, n):
        self.n = n
        self.order = list(range(n // 2, n)) + list(range(n // 2 - 1, -1, -1))
        self.rows = BS * BS // n
        self.tiles = self.rows * BS // LANES
        self.lanes = min(self.rows, BS) * BS
        self.radii = max(1, self.rows // BS)
        self.last = self.order[n // 4 : n // 2]
        self.per = self.lanes // LANES
        self.split = max(1, BS // self.rows)
        self.slots = n * SUB


def shape(*dims, dtype=F32):
    return jax.ShapeDtypeStruct(dims, dtype)


def shards(conserved, face_field, block_ids, int_shift, frac_shift):
    n = lax.axis_size("phi")
    cfg = Sizes(n)
    count = lax.axis_size("tile") * n
    tiles, per = cfg.tiles, cfg.per
    smem = pl.BlockSpec(memory_space=pltpu.SMEM)
    vmem = pl.BlockSpec(memory_space=pltpu.VMEM)
    hbm = pl.BlockSpec(memory_space=pltpu.MemorySpace.HBM)

    def grant(mib):
        return pltpu.CompilerParams(vmem_limit_bytes=min(mib, 48) * 2**20)

    me = lax.axis_index(("tile", "phi")).astype(jnp.int32).reshape(1)

    def holder(group):
        tile, place = divmod(group, n)
        return tile * n + (place ^ (tile % 2 * (n - 1)))

    def tiled(x):
        return x.reshape(SUB, x.shape[1], n * tiles, LANES).transpose(1, 2, 0, 3)

    def untiled(x):
        return x.transpose(2, 0, 1, 3).reshape(SUB, x.shape[0], n * tiles * LANES)

    half = n // 2

    def exchange(pieces, order):
        return [
            lax.ppermute(piece, "phi", [(s, s ^ k) for s in range(n)]) if k else piece
            for piece, k in zip(pieces, order)
        ]

    def in_hbm(x):
        return pltpu.with_memory_space_constraint(x, pltpu.MemorySpace.HBM)

    sources = (in_hbm(block_ids), in_hbm(tiled(face_field)), in_hbm(tiled(conserved)))
    packed, token = [], []
    for late, shapes in (
        (False, [shape(4 * tiles + 1, SUB, LANES)] * half + [shape(SUB, LANES)]),
        (
            True,
            [shape(8 * tiles + 1, SUB, LANES)] * half + [shape(4 * tiles, SUB, LANES)] * half,
        ),
    ):
        pieces = pl.pallas_call(
            functools.partial(pack_kernel, cfg, late),
            out_shape=shapes,
            in_specs=[smem] + [hbm] * 3 + [vmem] * len(token),
            out_specs=[vmem] * len(shapes),
            scratch_shapes=[
                pltpu.VMEM((8, n * tiles, SUB, LANES), F32),
                pltpu.SMEM((SUB,), jnp.int32),
                pltpu.SemaphoreType.DMA((9,)),
            ],
            compiler_params=grant(3),
            name="pack_late" if late else "pack_early",
        )(me, *sources, *token)
        packed, token = packed + list(pieces[: None if late else half]), list(pieces[half:])[:1]
    first = exchange(packed[:n], cfg.order)
    far_second = exchange(packed[n:], cfg.order)

    def square(count):
        return shape(cfg.radii, count, cfg.lanes, cfg.lanes, dtype=BF16)

    mh, ml, gh, gl, tj, whole, side = pl.pallas_call(
        functools.partial(operators_kernel, cfg),
        out_shape=[square(2)] * 2
        + [square(3)] * 2
        + [
            shape(2, cfg.lanes, cfg.lanes, dtype=BF16),
            shape(cfg.radii, SUB, 3 * cfg.slots, dtype=jnp.int32),
            shape(cfg.radii, SUB, cfg.lanes, dtype=jnp.int32),
        ],
        in_specs=[smem] * 3,
        out_specs=[vmem] * 7,
        compiler_params=grant(8),
        name="operators",
    )(me, int_shift, frac_shift)

    owners = shape(n, per, SUB, LANES)
    halo = pl.pallas_call(
        functools.partial(edge_kernel, cfg),
        out_shape=owners,
        in_specs=[smem] + [vmem] * (n + 4),
        out_specs=vmem,
        compiler_params=grant(2 * n),
        name="edge",
    )(me, *first, gh, gl, tj, whole)
    halo = lax.ppermute(
        halo,
        ("tile", "phi"),
        [(holder(s), holder(s - cfg.split)) for s in range(cfg.split, count)],
    )
    rows, taken, polar = pl.pallas_call(
        functools.partial(fields_kernel, cfg),
        out_shape=[
            shape(n, 4, tiles, SUB, LANES),
            shape(cfg.radii, 3 * cfg.slots, 3 * cfg.slots, dtype=BF16),
            owners if cfg.split > 1 else shape(1, 1, SUB, LANES),
        ],
        in_specs=[smem] + [vmem] * (n + 7),
        out_specs=[vmem] * 3,
        compiler_params=grant(2 * n),
        name="fields",
    )(me, *first, mh, ml, gh, gl, tj, whole, side)
    if cfg.split > 1:
        polar = lax.ppermute(
            polar,
            ("tile", "phi"),
            [
                (holder(s), holder(s - 1 if s % cfg.split else s + cfg.split - 1))
                for s in range(count)
            ],
        )
    done, token = {}, []
    first_far, last_far = cfg.order[: n // 4], cfg.order[n // 4 : half]
    for name, orders in (
        ("finish_first", first_far),
        ("finish_near", cfg.order[half:]),
        ("finish_last", last_far),
    ):
        *pieces, mark = pl.pallas_call(
            functools.partial(finish_kernel, cfg, orders),
            out_shape=[shape(8, tiles, SUB, LANES)] * len(orders) + [shape(SUB, LANES)],
            in_specs=[smem] + [vmem] * (n + 7 + len(token)),
            out_specs=[vmem] * (len(orders) + 1),
            compiler_params=grant(2 * n),
            name=name,
        )(me, *far_second, *first[half:], mh, ml, side, taken, rows, halo, polar, *token)
        done.update(zip(orders, pieces))
        token = [mark]
    back = exchange([done[k] for k in cfg.order], cfg.order)
    outs = ()
    for name, late in (("unpack_early", False), ("unpack_late", True)):
        orders = [k for k in cfg.order if (k in cfg.last) == late]
        outs = pl.pallas_call(
            functools.partial(unpack_kernel, cfg, orders),
            out_shape=[shape(5, n * tiles, SUB, LANES), shape(3, n * tiles, SUB, LANES)],
            in_specs=[smem] + [vmem] * len(orders) + [hbm] * len(outs),
            out_specs=[hbm] * 2,
            input_output_aliases={1 + len(orders) + i: i for i in range(len(outs))},
            scratch_shapes=[pltpu.SemaphoreType.DMA((n, 2))],
            compiler_params=grant(2),
            name=name,
        )(me, *[back[cfg.order.index(k)] for k in orders], *outs)
    conserved_out, field_out = outs
    return untiled(conserved_out), untiled(field_out)


def solution(mesh):
    return jax.shard_map(
        shards,
        mesh=mesh,
        in_specs=(
            P(("tile", "phi"), None, None),
            P(("tile", "phi"), None, None),
            P(("tile", "phi")),
            P("tile"),
            P("tile"),
        ),
        out_specs=(P(("tile", "phi"), None, None), P(("tile", "phi"), None, None)),
        check_vma=False,
    )
```
